128 devices in a mesh: gx: 8 (over x_lo, y), gy: 16 (over z, x_hi, core).
Axes of the slice: x: 4 (x_hi: 2, x_lo: 2; x = x_hi * 2 + x_lo), y: 4, z: 4, core: 2. Of those that a mesh axis runs over, the one named last changes fastest.
Arguments:
- voxel_feats: bfloat16 [512, 64, 128], P(('gx', 'gy')), may hold values from -6 to 6
- w_first: bfloat16 [27, 128, 128], replicated, may hold values from -0.109375 to 0.109375
- w_second: bfloat16 [27, 128, 128], replicated, may hold values from -0.109375 to 0.109375
- norm_gain: float32 [2, 128], replicated, may hold values from 0.5 to 1.5
- norm_shift: float32 [2, 128], replicated, may hold values from -3 to 3
- grad_out: bfloat16 [512, 64, 128], P(('gx', 'gy')), may hold values from -6 to 6
- brick_count: int32 [128], P(('gx', 'gy')), may hold values from 1 to 4, as said below
- kernel_map: int32 [512, 27], P(('gx', 'gy')), may hold values from 0 to 12, as said below
- face_send: int32 [128, 4, 1], P(('gx', 'gy')), may hold values from 0 to 3, as said below
- corner_send: int32 [128, 4, 1], P(('gx', 'gy')), may hold values from 0 to 3, as said below
Outputs:
- out_feats: bfloat16 [512, 64, 128], P(('gx', 'gy'))
- grad_in: bfloat16 [512, 64, 128], P(('gx', 'gy'))
- weight_grads: float32 [2, 27, 128, 128], replicated
- norm_grads: float32 [4, 128], replicated
The draws below stay inside these ranges and needn't reach their ends.
Inputs may be any that keep to these rules, and one draw needn't show every extreme that they name: `brick_count`: some tile is full in every draw. `kernel_map`: direction 13 names the brick itself; index 12 is the zero brick. `face_send`: list k names bricks of the tile below its brick_count, sent to its +x, -x, +y, -y neighbour for k = 0, 1, 2, 3. `corner_send`: list k names bricks of the tile below its brick_count, sent to its (+x, +y), (+x, -y), (-x, +y), (-x, -y) neighbour for k = 0, 1, 2, 3.
All inputs are finite; a program needn't handle non-finite values.
Results may differ from the reference program's by a relative error of at most 0.006.
Values may be sent and summed in bfloat16 or wider, within the bound.
No kernel may reach another device: no remote copies, remote signals or barrier semaphores. Data moves between devices by JAX's collectives and lax.ppermute only.
A program may use at most 128 MiB of HBM per device.

```python
import jax
import jax.numpy as jnp
from jax import lax

C = 128
NB = 4
SF = 1
SC = 1
EXT = 13
TILES = 128
BRICKS = 512
N_GX = 8
N_GY = 16


def full_tile(key):
    return jax.random.randint(jax.random.fold_in(key, 12), (), 0, TILES)


def tile_counts(key):
    drawn = jax.random.randint(jax.random.fold_in(key, 11), (TILES,), NB // 4, NB + 1)
    chosen = full_tile(key)
    return jnp.where(jnp.arange(TILES) == chosen, NB, drawn).astype(jnp.int32)


def pin_ends(lists, key):
    chosen = full_tile(key)
    tile_ids = jnp.arange(TILES)[:, None, None]
    list_ids = jnp.arange(4)[None, :, None]
    slot_ids = jnp.arange(lists.shape[2])[None, None, :]
    at_top = (tile_ids == chosen) & (list_ids == 0) & (slot_ids == 0)
    at_bottom = (tile_ids == chosen) & (list_ids == 1) & (slot_ids == 0)
    lists = jnp.where(at_top, NB - 1, lists)
    return jnp.where(at_bottom, 0, lists)


def draw_brick_count(key, part):
    return tile_counts(key)


def draw_face_send(key, part):
    counts = tile_counts(key)
    random_ints = jax.random.randint(jax.random.fold_in(key, 21), (TILES, 4, SF), 0, 1 << 20)
    return pin_ends(random_ints % counts[:, None, None], key).astype(jnp.int32)


def draw_corner_send(key, part):
    counts = tile_counts(key)
    random_ints = jax.random.randint(jax.random.fold_in(key, 22), (TILES, 4, SC), 0, 1 << 20)
    return pin_ends(random_ints % counts[:, None, None], key).astype(jnp.int32)


def draw_kernel_map(key, part):
    picked = jax.random.randint(jax.random.fold_in(key, 31), (BRICKS, 27), 0, EXT - 1)
    dropped = jax.random.randint(jax.random.fold_in(key, 32), (BRICKS, 27), 0, 10) < 3
    picked = jnp.where(dropped, EXT - 1, picked)
    itself = (jnp.arange(BRICKS) % NB)[:, None]
    center = jnp.arange(27)[None, :] == 13
    return jnp.where(center, itself, picked).astype(jnp.int32)


def block_levels(rng, shape, split, smallest, high):
    def one(axis_at, blocks):
        draws = jax.random.uniform(jax.random.fold_in(jax.random.fold_in(rng, 6), axis_at), (blocks,), jnp.float32, smallest / len(split), high / len(split))
        return jnp.repeat(jnp.exp(draws), shape[axis_at] // blocks).reshape((-1,) + (1,) * (len(shape) - axis_at - 1))

    loudness = one(*split[0])
    for cut in split[1:]:
        loudness = loudness * one(*cut)
    return loudness


def noise(stream_key, dims, scale, bound, cuts=(), held_as=jnp.bfloat16):
    level = block_levels(stream_key, dims, cuts, -0.22, 0.18) if cuts else 1.0
    entries = jax.random.normal(stream_key, dims, jnp.float32) * scale * level
    return jnp.minimum(jnp.maximum(entries, -bound), bound).astype(held_as)


def setup_inputs(seed: int = 0) -> dict:
    splits = jax.random.split(jax.random.key(seed), 11)
    return {
        "voxel_feats": noise(splits[0], (BRICKS, 64, C), 1.0, 6.0, ((0, 128),)),
        "w_first": noise(splits[1], (27, C, C), (27 * C) ** -0.5, 0.109375),
        "w_second": noise(splits[2], (27, C, C), (27 * C) ** -0.5, 0.109375),
        "norm_gain": jnp.clip(1.0 + 0.1 * jax.random.normal(splits[3], (2, C), jnp.float32), 0.5, 1.5),
        "norm_shift": noise(splits[4], (2, C), 0.5, 3.0, (), jnp.float32),
        "grad_out": noise(splits[5], (BRICKS, 64, C), 1.0, 6.0, ((0, 128),)),
        "brick_count": draw_brick_count(jax.random.fold_in(splits[10], 71), 0),
        "kernel_map": draw_kernel_map(jax.random.fold_in(splits[10], 71), 0),
        "face_send": draw_face_send(jax.random.fold_in(splits[10], 71), 0),
        "corner_send": draw_corner_send(jax.random.fold_in(splits[10], 71), 0),
    }


TAP_LIST = [(a, b, c) for a in range(3) for b in range(3) for c in range(3)]
FACE_SIGNS = ((1, 0), (-1, 0), (0, 1), (0, -1))
CORNER_SIGNS = ((1, 1), (1, -1), (-1, 1), (-1, -1))
epsilon = 1e-05

def silu_slope(values):
    sigma = jax.nn.sigmoid(values)
    return sigma * (1.0 + values * (1.0 - sigma))

def source_range(e):
    if e < 0:
        return (slice(3, 4), slice(0, 1))
    if e == 0:
        return (slice(0, 4), slice(1, 5))
    return (slice(0, 1), slice(5, 6))

def assemble(extended, tile_table):
    planes = []
    for a in (-1, 0, 1):
        layers = []
        for b in (-1, 0, 1):
            pieces = []
            for c in (-1, 0, 1):
                d = 9 * (a + 1) + 3 * (b + 1) + (c + 1)
                region = extended[:, source_range(a)[0], source_range(b)[0], source_range(c)[0]]
                pieces.append(jnp.take(region, tile_table[:, d], axis=0))
            layers.append(jnp.concatenate(pieces, axis=3))
        planes.append(jnp.concatenate(layers, axis=2))
    return jnp.concatenate(planes, axis=1)

def patches(padded):
    bricks = padded.shape[0]
    channels = padded.shape[-1]
    return jnp.concatenate([padded[:, a:a + 4, b:b + 4, c:c + 4].reshape(bricks * 64, channels) for a, b, c in TAP_LIST], axis=1)

def spread(columns, bricks, channels):
    padded = jnp.zeros((bricks, 6, 6, 6, channels), jnp.float32)
    for k, (a, b, c) in enumerate(TAP_LIST):
        piece = columns[:, k * channels:(k + 1) * channels].reshape(bricks, 4, 4, 4, channels)
        padded = padded.at[:, a:a + 4, b:b + 4, c:c + 4].add(piece)
    return padded

def scatter_bricks(padded, tile_table, total):
    result = jnp.zeros((total, 4, 4, 4, padded.shape[-1]), jnp.float32)
    for a in (-1, 0, 1):
        for b in (-1, 0, 1):
            for c in (-1, 0, 1):
                d = 9 * (a + 1) + 3 * (b + 1) + (c + 1)
                range_a = source_range(a)
                range_b = source_range(b)
                range_c = source_range(c)
                result = result.at[tile_table[:, d], range_a[0], range_b[0], range_c[0]].add(padded[:, range_a[1], range_b[1], range_c[1]])
    return result

def moved(grid, shift_x, shift_y):
    widths = [(1, 1), (1, 1)] + [(0, 0)] * (grid.ndim - 2)
    padded = jnp.pad(grid, widths)
    return padded[1 - shift_x:1 - shift_x + N_GX, 1 - shift_y:1 - shift_y + N_GY]

def take_lists(field, lists):
    return jax.vmap(lambda tile_field, picks: jnp.take(tile_field, picks, axis=0))(field, lists)

def extend_all(field, face_send, corner_send):
    pieces = [field]
    for k in range(4):
        sent = take_lists(field, face_send[:, k])
        grid = sent.reshape((N_GX, N_GY) + sent.shape[1:])
        pieces.append(moved(grid, FACE_SIGNS[k][0], FACE_SIGNS[k][1]).reshape(sent.shape))
    for k in range(4):
        sent = take_lists(field, corner_send[:, k])
        grid = sent.reshape((N_GX, N_GY) + sent.shape[1:])
        pieces.append(moved(grid, CORNER_SIGNS[k][0], CORNER_SIGNS[k][1]).reshape(sent.shape))
    pieces.append(jnp.zeros((TILES, 1) + field.shape[2:], field.dtype))
    return jnp.concatenate(pieces, axis=1)

def add_lists(accum, lists, values):
    return jax.vmap(lambda tile_acc, picks, vals: tile_acc.at[picks].add(vals))(accum, lists, values)

def return_all(ext_grads, face_send, corner_send):
    result = ext_grads[:, :NB]
    for k in range(4):
        piece = ext_grads[:, NB + k * SF:NB + (k + 1) * SF]
        grid = piece.reshape((N_GX, N_GY) + piece.shape[1:])
        homed = moved(grid, -FACE_SIGNS[k][0], -FACE_SIGNS[k][1]).reshape(piece.shape)
        result = add_lists(result, face_send[:, k], homed)
    start = NB + 4 * SF
    for k in range(4):
        piece = ext_grads[:, start + k * SC:start + (k + 1) * SC]
        grid = piece.reshape((N_GX, N_GY) + piece.shape[1:])
        homed = moved(grid, -CORNER_SIGNS[k][0], -CORNER_SIGNS[k][1]).reshape(piece.shape)
        result = add_lists(result, corner_send[:, k], homed)
    return result

def forward_conv(extended, tables, weight):
    channels = weight.shape[2]
    flat = weight.reshape(27 * channels, channels)

    def single(pair):
        return jnp.dot(patches(assemble(pair[0], pair[1])), flat, preferred_element_type=jnp.float32)
    return lax.map(single, (extended, tables))

def backward_conv(extended, tables, grads, weight):
    channels = weight.shape[2]
    flat = weight.reshape(27 * channels, channels)

    def single(carry, items):
        columns = patches(assemble(items[0], items[1]))
        carry = carry + lax.dot_general(columns, items[2], (((0,), (0,)), ((), ())), preferred_element_type=jnp.float32)
        spread_cols = lax.dot_general(items[2], flat, (((1,), (1,)), ((), ())), preferred_element_type=jnp.float32)
        return (carry, scatter_bricks(spread(spread_cols, NB, channels), items[1], EXT))
    return lax.scan(single, jnp.zeros((27 * channels, channels), jnp.float32), (extended, tables, grads))

def normalize(values, occupied, voxels):
    center = lax.optimization_barrier(jnp.sum(values * occupied, axis=(0, 1))) / voxels
    spread_sq = lax.optimization_barrier(jnp.sum(values * values * occupied, axis=(0, 1))) / voxels - center * center
    recip = lax.rsqrt(spread_sq + epsilon)
    return ((values - center) * recip, recip)

def reference(voxel_feats, w_first, w_second, norm_gain, norm_shift, grad_out, brick_count, kernel_map, face_send, corner_send):
    channels = voxel_feats.shape[2]
    shape_five = (TILES, NB, 4, 4, 4, channels)
    tables = kernel_map.reshape(TILES, NB, 27)
    occupied = (jnp.arange(NB, dtype=jnp.int32)[None, :] < brick_count[:, None]).astype(jnp.float32)
    occupied = jnp.repeat(occupied, 64, axis=1)[:, :, None]
    feats = voxel_feats.reshape(TILES, NB * 64, channels) * occupied.astype(jnp.bfloat16)
    voxels = 64.0 * jnp.sum(brick_count.astype(jnp.float32))
    ext_one = extend_all(feats.reshape(shape_five), face_send, corner_send)
    z_one = forward_conv(ext_one, tables, w_first)
    xh_one, recip_one = normalize(z_one, occupied, voxels)
    u_one = norm_gain[0] * xh_one + norm_shift[0]
    a_one = (jax.nn.silu(u_one) * occupied).astype(jnp.bfloat16)
    ext_two = extend_all(a_one.reshape(shape_five), face_send, corner_send)
    z_two = forward_conv(ext_two, tables, w_second)
    xh_two, recip_two = normalize(z_two, occupied, voxels)
    pre = norm_gain[1] * xh_two + norm_shift[1] + feats.astype(jnp.float32)
    out_feats = (jax.nn.silu(pre) * occupied).astype(jnp.bfloat16)
    d_val = grad_out.reshape(TILES, NB * 64, channels).astype(jnp.float32) * occupied * silu_slope(pre)
    sum_two = lax.optimization_barrier(jnp.sum(d_val, axis=(0, 1)))
    cross_two = lax.optimization_barrier(jnp.sum(d_val * xh_two, axis=(0, 1)))
    dz_two = (occupied * norm_gain[1] * recip_two * (d_val - sum_two / voxels - xh_two * cross_two / voxels)).astype(jnp.bfloat16)
    dw_two, ge_two = backward_conv(ext_two, tables, dz_two, w_second)
    da_one = return_all(ge_two, face_send, corner_send).reshape(TILES, NB * 64, channels)
    du_one = da_one * occupied * silu_slope(u_one)
    sum_one = lax.optimization_barrier(jnp.sum(du_one, axis=(0, 1)))
    cross_one = lax.optimization_barrier(jnp.sum(du_one * xh_one, axis=(0, 1)))
    dz_one = (occupied * norm_gain[0] * recip_one * (du_one - sum_one / voxels - xh_one * cross_one / voxels)).astype(jnp.bfloat16)
    dw_one, ge_one = backward_conv(ext_one, tables, dz_one, w_first)
    back_in = return_all(ge_one, face_send, corner_send).reshape(TILES, NB * 64, channels)
    grad_in = ((d_val + back_in) * occupied).astype(jnp.bfloat16)
    root = jnp.sqrt(voxels)
    weight_grads = jnp.stack([dw_one, dw_two]).reshape(2, 27, channels, channels) / root
    norm_grads = jnp.stack([cross_one, sum_one, cross_two, sum_two]) / root
    return (out_feats.reshape(BRICKS, 64, channels), grad_in.reshape(BRICKS, 64, channels), weight_grads, norm_grads)
```

```python
import functools

import jax
import jax.numpy as jnp
import numpy as np
from jax import lax
from jax.experimental import pallas as pl
from jax.experimental.pallas import tpu as pltpu
from jax.sharding import Mesh
from jax.sharding import PartitionSpec as P

GX = ("gx_0", "gx_1")
GY = ("gy_0", "gy_1", "gy_2")
GX_GY = ("gx_0", "gx_1", "gy_0", "gy_1", "gy_2")
CORE = ("gy_2",)
CHIPS = ("gx_0", "gx_1", "gy_0", "gy_1")
C = 128
NB = 4
ROWS = NB * 64
TAPS = 27
EXT = 13
EPSILON = 1e-05
F32 = jnp.float32
BF16 = jnp.bfloat16
COUNT, FACE, CORNER, VALID = 108, 109, 113, 117
NEIGHBOURS = ((-1, 0), (1, 0), (0, -1), (0, 1), (-1, -1), (-1, 1), (1, -1), (1, 1))
CHUNK = 56
PADDED = 64 * CHUNK


def shift_matrix():
    shift = np.zeros((9, 4, 4, 9, 4, 4), np.float32)
    for b in range(3):
        for c in range(3):
            for q in range(4):
                for r in range(4):
                    y, x = q + b - 1, r + c - 1
                    ob = 0 if y < 0 else 1 if y < 4 else 2
                    oc = 0 if x < 0 else 1 if x < 4 else 2
                    shift[3 * b + c, q, r, 3 * ob + oc, y % 4, x % 4] = 1.0
    return shift.reshape(144, 144)


def sources():
    return [(0, 0, 3), (1, 1, 0), (2, 1, 1), (3, 1, 2), (4, 1, 3), (5, 2, 0)]


def sigmoid(v):
    return 1.0 / (1.0 + jnp.exp(-v))


def slope(v):
    s = sigmoid(v)
    return s * (1.0 + v * (1.0 - s))


def occupied_rows(meta):
    brick = lax.broadcasted_iota(jnp.int32, (ROWS, C), 0) // 64
    return (brick < meta[COUNT]).astype(F32)


def gather_columns(meta, ext, gathered, shift, columns):
    for b in range(NB):
        for plane, oa, source in sources():
            for d in range(9):
                entry = meta[27 * b + 9 * oa + d]
                gathered[16 * d : 16 * d + 16, (6 * b + plane) * C : (6 * b + plane + 1) * C] = ext[
                    entry, 16 * source : 16 * source + 16, :
                ]
    for b in range(NB):
        moved = jnp.dot(
            shift[...], gathered[:, 6 * b * C : 6 * (b + 1) * C], preferred_element_type=F32
        ).astype(BF16)
        for a in range(3):
            for p in range(4):
                for d in range(9):
                    k = 9 * a + d
                    columns[64 * b + 16 * p : 64 * b + 16 * p + 16, k * C : (k + 1) * C] = moved[
                        16 * d : 16 * d + 16, (p + a) * C : (p + a + 1) * C
                    ]


def convolve(columns, weight):
    return jnp.dot(columns[...], weight[...], preferred_element_type=F32)


def convolve_back(meta, dz, weight, shift_back, spread, moved, acc):
    for a in range(3):
        spread[a] = lax.dot_general(
            dz,
            weight[9 * a * C : 9 * (a + 1) * C, :],
            (((1,), (1,)), ((), ())),
            preferred_element_type=F32,
        )
    acc[...] = jnp.zeros_like(acc)
    for b in range(NB):
        for plane in range(6):
            taps = [a for a in range(3) if 0 <= plane - a < 4]
            for d in range(9):
                total = None
                for a in taps:
                    row = 64 * b + 16 * (plane - a)
                    piece = spread[a, row : row + 16, d * C : (d + 1) * C]
                    total = piece if total is None else total + piece
                moved[16 * d : 16 * d + 16, (6 * b + plane) * C : (6 * b + plane + 1) * C] = (
                    total.astype(BF16)
                )
    for b in range(NB):
        home = jnp.dot(
            shift_back[...], moved[:, 6 * b * C : 6 * (b + 1) * C], preferred_element_type=F32
        )
        for plane, oa, source in sources():
            for d in range(9):
                entry = meta[27 * b + 9 * oa + d]
                acc[entry, 16 * source : 16 * source + 16, :] += home[
                    16 * d : 16 * d + 16, plane * C : (plane + 1) * C
                ]


def write_sums(out, first, second):
    odd = lax.broadcasted_iota(jnp.int32, (8, C), 0) % 2
    both = jnp.where(odd == 0, jnp.broadcast_to(first, (8, C)), jnp.broadcast_to(second, (8, C)))
    out[...] = jnp.broadcast_to(both[None], (out.shape[0] // 8, 8, C)).reshape(out.shape)


def read_sums(got):
    total = jnp.sum(got[...].reshape(got.shape[0] // 8, 8, C), axis=0)
    odd = lax.broadcasted_iota(jnp.int32, (8, C), 0) % 2
    first = jnp.sum(jnp.where(odd == 0, total, 0.0), axis=0, keepdims=True)
    second = jnp.sum(jnp.where(odd == 1, total, 0.0), axis=0, keepdims=True)
    return first, second


def rows_sum(v):
    return jnp.sum(v, axis=0, keepdims=True)


def statistics(total, squares, voxels):
    center = total / voxels
    spread_sq = squares / voxels - center * center
    return center, lax.rsqrt(spread_sq + EPSILON)


def place_received(ext, ux, lx, uy, ly):
    for e, (ref, k) in enumerate(
        ((ux, 0), (lx, 0), (uy, 0), (ly, 0), (uy, 1), (ly, 1), (uy, 2), (ly, 2))
    ):
        ext[NB + e] = ref[k]


def send_kernel(meta, field, x_up, x_low, y_faces):
    x_up[0] = field[meta[FACE]]
    x_up[1] = field[meta[CORNER]]
    x_up[2] = field[meta[CORNER + 1]]
    x_low[0] = field[meta[FACE + 1]]
    x_low[1] = field[meta[CORNER + 2]]
    x_low[2] = field[meta[CORNER + 3]]
    y_faces[0] = field[meta[FACE + 2]]
    y_faces[1] = field[meta[FACE + 3]]


def first_kernel(
    meta, voxel_feats, ux, lx, uy, ly, weight, shift,
    z_out, columns, sums, x_up, x_low, y_faces, ext, gathered,
):
    ext[NB + 8] = jnp.zeros((64, C), BF16)
    for b in range(NB):
        keep = (meta[COUNT] > b).astype(F32)
        ext[b] = (voxel_feats[b].astype(F32) * keep).astype(BF16)
    place_received(ext, ux, lx, uy, ly)
    gather_columns(meta, ext, gathered, shift, columns)
    z = convolve(columns, weight)
    z_out[...] = z.reshape(NB, 64, C)
    masked = z * occupied_rows(meta)
    write_sums(sums, rows_sum(masked), rows_sum(z * masked))
    send_kernel(meta, z_out, x_up, x_low, y_faces)


def second_kernel(
    meta, got, voxels, z_one, ux, lx, uy, ly, norm, weight, shift,
    z_out, columns, sums, xh_out, recip_out, field, ext, gathered,
):
    total, squares = read_sums(got)
    center, recip = statistics(total, squares, voxels[0])
    recip_out[...] = jnp.broadcast_to(recip, (8, C))
    field[0:NB] = z_one[...]
    place_received(field, ux, lx, uy, ly)
    for e in range(EXT - 1):
        keep = meta[COUNT] > e if e < NB else meta[VALID + e - NB] > 0
        xh = (field[e] - center) * recip
        xh_out[e] = xh
        u = norm[0:1] * xh + norm[2:3]
        ext[e] = (u * sigmoid(u) * keep.astype(F32)).astype(BF16)
    ext[EXT - 1] = jnp.zeros((64, C), BF16)
    gather_columns(meta, ext, gathered, shift, columns)
    z = convolve(columns, weight)
    z_out[...] = z
    masked = z * occupied_rows(meta)
    write_sums(sums, rows_sum(masked), rows_sum(z * masked))


def third_kernel(
    meta, got, voxels, z_two, voxel_feats, grad_out, norm, out_feats, dv_out, xh_out, recip_out, sums
):
    total, squares = read_sums(got)
    center, recip = statistics(total, squares, voxels[0])
    recip_out[...] = jnp.broadcast_to(recip, (8, C))
    occupied = occupied_rows(meta)
    xh = (z_two[...] - center) * recip
    xh_out[...] = xh
    feats = voxel_feats[...].astype(F32) * occupied
    pre = norm[1:2] * xh + norm[3:4] + feats
    s = sigmoid(pre)
    out_feats[...] = (pre * s * occupied).astype(BF16)
    dv = grad_out[...].astype(F32) * occupied * (s * (1.0 + pre * (1.0 - s)))
    dv_out[...] = dv
    write_sums(sums, rows_sum(dv), rows_sum(dv * xh))


def norm_back(dv, xh, gain, recip, total, cross, voxels, occupied):
    return (occupied * gain * recip * (dv - total / voxels - xh * cross / voxels)).astype(BF16)


def send_gradients(acc, own, y_low, y_up, x_faces):
    own[...] = acc[0:NB].reshape(ROWS, C)
    y_low[0] = acc[NB + 2].astype(BF16)
    y_low[1] = acc[NB + 4].astype(BF16)
    y_low[2] = acc[NB + 6].astype(BF16)
    y_up[0] = acc[NB + 3].astype(BF16)
    y_up[1] = acc[NB + 5].astype(BF16)
    y_up[2] = acc[NB + 7].astype(BF16)
    x_faces[0] = acc[NB].astype(BF16)
    x_faces[1] = acc[NB + 1].astype(BF16)


def fourth_kernel(
    meta, got, voxels, dv, xh_two, recip, xh_one, norm, weight, shift_back,
    dz_out, own, y_low, y_up, x_faces, sums, grads, spread, moved, acc,
):
    total, cross = read_sums(got)
    grads[0:1] = cross
    grads[1:2] = total
    dz = norm_back(
        dv[...], xh_two[...], norm[1:2], recip[0:1], total, cross, voxels[0], occupied_rows(meta)
    )
    dz_out[...] = dz
    convolve_back(meta, dz, weight, shift_back, spread, moved, acc)
    send_gradients(acc, own, y_low, y_up, x_faces)
    first = jnp.zeros((64, C), F32)
    second = jnp.zeros((64, C), F32)
    for e in range(EXT - 1):
        keep = meta[COUNT] > e if e < NB else meta[VALID + e - NB] > 0
        xh = xh_one[e]
        du = acc[e] * slope(norm[0:1] * xh + norm[2:3]) * keep.astype(F32)
        first += du
        second += du * xh
    write_sums(sums, rows_sum(first), rows_sum(second))


def add_returned(meta, field, lx, ux, ly, uy):
    for e, (ref, k, at) in enumerate(
        (
            (lx, 0, FACE), (ux, 0, FACE + 1), (ly, 0, FACE + 2), (uy, 0, FACE + 3),
            (lx, 1, CORNER), (lx, 2, CORNER + 1), (ux, 1, CORNER + 2), (ux, 2, CORNER + 3),
        )
    ):
        field[meta[at]] += ref[k].astype(F32)


def fifth_kernel(
    meta, got, voxels, own_in, lx, ux, ly, uy, xh_one, recip, norm, weight, shift_back,
    dz_out, own, y_low, y_up, x_faces, grads, field, spread, moved, acc,
):
    total, cross = read_sums(got)
    grads[0:1] = cross
    grads[1:2] = total
    field[...] = own_in[...].reshape(NB, 64, C)
    add_returned(meta, field, lx, ux, ly, uy)
    occupied = occupied_rows(meta)
    xh = xh_one[0:NB].reshape(ROWS, C)
    du = field[...].reshape(ROWS, C) * occupied * slope(norm[0:1] * xh + norm[2:3])
    dz = norm_back(du, xh, norm[0:1], recip[0:1], total, cross, voxels[0], occupied)
    dz_out[...] = dz
    convolve_back(meta, dz, weight, shift_back, spread, moved, acc)
    send_gradients(acc, own, y_low, y_up, x_faces)


def taps_kernel(columns, dz, out):
    for k in range(TAPS):
        out[k * C : (k + 1) * C, :] = lax.dot_general(
            columns[:, k * C : (k + 1) * C],
            dz[...],
            (((0,), (0,)), ((), ())),
            preferred_element_type=F32,
        )


def last_kernel(meta, own, lx, ux, ly, uy, dv, grad_in, field):
    field[...] = own[...].reshape(NB, 64, C)
    add_returned(meta, field, lx, ux, ly, uy)
    total = (dv[...] + field[...].reshape(ROWS, C)) * occupied_rows(meta)
    grad_in[...] = total.astype(BF16)


def local(kernel, outs, ins, scratch=()):
    vmem = pl.BlockSpec(memory_space=pltpu.VMEM)
    smem = pl.BlockSpec(memory_space=pltpu.SMEM)
    specs = [smem if a.ndim == 1 else vmem for a in ins]
    return pl.pallas_call(
        kernel,
        out_shape=[jax.ShapeDtypeStruct(s, d) for s, d in outs],
        in_specs=specs,
        out_specs=[vmem] * len(outs),
        scratch_shapes=[pltpu.VMEM(s, d) for s, d in scratch],
        compiler_params=pltpu.CompilerParams(vmem_limit_bytes=48 << 20),
        name=kernel.__name__,
    )(*ins)


def shifted(value, axis, by):
    length = lax.axis_size(axis)
    pairs = [(i, i + by) for i in range(length) if 0 <= i + by < length]
    return lax.ppermute(value, axis, pairs)


def exchange(value, axes):
    return lax.all_to_all(value, axes, 0, 0, tiled=True)


def swap(value):
    return lax.ppermute(value, CORE, [(0, 1), (1, 0)])


def outward(x_up, x_low, y_faces):
    ux = shifted(x_up, GX, 1)
    lx = shifted(x_low, GX, -1)
    uy = shifted(jnp.concatenate([y_faces[0:1], ux[1:2], lx[1:2]], axis=0), GY, 1)
    ly = shifted(jnp.concatenate([y_faces[1:2], ux[2:3], lx[2:3]], axis=0), GY, -1)
    return ux, lx, uy, ly


def homeward(y_low, y_up, x_faces):
    ly = shifted(y_low, GY, -1)
    uy = shifted(y_up, GY, 1)
    lx = shifted(jnp.concatenate([x_faces[0:1], ly[1:2], uy[1:2]], axis=0), GX, -1)
    ux = shifted(jnp.concatenate([x_faces[1:2], ly[2:3], uy[2:3]], axis=0), GX, 1)
    return lx, ux, ly, uy


def body(
    voxel_feats,
    w_first,
    w_second,
    norm_gain,
    norm_shift,
    grad_out,
    brick_count,
    kernel_map,
    face_send,
    corner_send,
):
    i = lax.axis_index(GX)
    j = lax.axis_index(GY)
    dx = np.array([d[0] for d in NEIGHBOURS], np.int32)
    dy = np.array([d[1] for d in NEIGHBOURS], np.int32)
    inside = (i + dx >= 0) & (i + dx < 8) & (j + dy >= 0) & (j + dy < 16)
    meta = jnp.concatenate(
        [
            kernel_map.reshape(-1),
            brick_count,
            face_send.reshape(-1),
            corner_send.reshape(-1),
            inside.astype(jnp.int32),
        ]
    )
    norm = jnp.concatenate([norm_gain, norm_shift], axis=0)
    shift = jnp.asarray(shift_matrix(), BF16)
    shift_back = jnp.asarray(shift_matrix().T, BF16)
    flat_one = w_first.reshape(TAPS * C, C)
    flat_two = w_second.reshape(TAPS * C, C)
    brick = (64, C)
    three, two = (3,) + brick, (2,) + brick
    wide = (ROWS, TAPS * C)
    rows = (ROWS, C)
    sums = ((2 * 128, C), F32)
    ext = ((EXT,) + brick, BF16)
    gathered = ((144, 6 * NB * C), BF16)

    sends = local(send_kernel, [(three, BF16), (three, BF16), (two, BF16)], [meta, voxel_feats])
    received = outward(*sends)
    counts = exchange(jnp.broadcast_to(brick_count.astype(F32).reshape(1, 1), (128, C)), GX_GY)
    voxels = (64.0 * jnp.sum(counts[:, 0])).reshape(1)
    z_one, columns_one, part, *sends = local(
        first_kernel,
        [((NB,) + brick, F32), (wide, BF16), sums, (three, F32), (three, F32), (two, F32)],
        [meta, voxel_feats, *received, flat_one, shift],
        [ext, gathered],
    )
    received = outward(*sends)
    part = exchange(part, GX_GY)
    z_two, columns_two, part, xh_one, recip_one = local(
        second_kernel,
        [(rows, F32), (wide, BF16), sums, ((EXT - 1,) + brick, F32), ((8, C), F32)],
        [meta, part, voxels, z_one, *received, norm, flat_two, shift],
        [((EXT - 1,) + brick, F32), ext, gathered],
    )
    part = exchange(part, GX_GY)
    out_feats, dv, xh_two, recip_two, part = local(
        third_kernel,
        [(rows, BF16), (rows, F32), (rows, F32), ((8, C), F32), sums],
        [meta, part, voxels, z_two, voxel_feats.reshape(rows), grad_out.reshape(rows), norm],
    )
    part = exchange(part, GX_GY)
    back = [
        ((3, ROWS, 9 * C), F32),
        gathered,
        ((EXT,) + brick, F32),
    ]
    dz_two, own, y_low, y_up, x_faces, part, grads_two = local(
        fourth_kernel,
        [(rows, BF16), (rows, F32), (three, BF16), (three, BF16), (two, BF16), sums, ((2, C), F32)],
        [meta, part, voxels, dv, xh_two, recip_two, xh_one, norm, flat_two, shift_back],
        back,
    )
    returned = homeward(y_low, y_up, x_faces)
    (dw_two,) = local(taps_kernel, [((TAPS * C, C), F32)], [columns_two, dz_two])
    part = exchange(part, GX_GY)
    dz_one, own, y_low, y_up, x_faces, grads_one = local(
        fifth_kernel,
        [(rows, BF16), (rows, F32), (three, BF16), (three, BF16), (two, BF16), ((2, C), F32)],
        [meta, part, voxels, own, *returned, xh_one, recip_one, norm, flat_one, shift_back],
        [((NB,) + brick, F32)] + back,
    )
    returned = homeward(y_low, y_up, x_faces)
    (dw_one,) = local(taps_kernel, [((TAPS * C, C), F32)], [columns_one, dz_one])
    (grad_in,) = local(
        last_kernel, [(rows, BF16)], [meta, own, *returned, dv], [((NB,) + brick, F32)]
    )
    root = jnp.sqrt(voxels[0])
    core = lax.axis_index(CORE)
    mine = jnp.where(core == 0, dw_one, dw_two)
    other = jnp.where(core == 0, dw_two, dw_one).astype(BF16)
    mine = (mine + swap(other).astype(F32)).astype(BF16)
    mine = jnp.pad(mine, ((0, PADDED - TAPS * C), (0, 0)))
    pieces = exchange(mine, CHIPS).reshape(64, CHUNK, C)
    piece = (jnp.sum(pieces.astype(F32), axis=0) / root).astype(BF16)
    whole = exchange(jnp.broadcast_to(piece[None], (64, CHUNK, C)).reshape(PADDED, C), CHIPS)
    partner = swap(whole)
    first = jnp.where(core == 0, whole, partner)[: TAPS * C]
    second = jnp.where(core == 0, partner, whole)[: TAPS * C]
    weight_grads = jnp.stack([first, second]).reshape(2, TAPS, C, C).astype(F32)
    norm_grads = jnp.concatenate([grads_one, grads_two], axis=0) / root
    return (
        out_feats.reshape(NB, 64, C),
        grad_in.reshape(NB, 64, C),
        weight_grads,
        norm_grads,
    )


def solution(mesh):
    split = Mesh(mesh.devices.reshape(2, 4, 4, 2, 2), GX_GY)
    in_specs = (
        P(GX_GY, None, None),
        P(),
        P(),
        P(),
        P(),
        P(GX_GY, None, None),
        P(GX_GY),
        P(GX_GY, None),
        P(GX_GY, None, None),
        P(GX_GY, None, None),
    )
    out_specs = (P(GX_GY, None, None), P(GX_GY, None, None), P(), P())
    return jax.shard_map(body, mesh=split, in_specs=in_specs, out_specs=out_specs, check_vma=False)
```

```python
import functools

import jax
import jax.numpy as jnp
import numpy as np
from jax import lax
from jax.experimental import pallas as pl
from jax.experimental.pallas import tpu as pltpu
from jax.sharding import Mesh
from jax.sharding import PartitionSpec as P

GX = ("gx_0", "gx_1")
GY = ("gy_0", "gy_1", "gy_2")
GX_GY = ("gx_0", "gx_1", "gy_0", "gy_1", "gy_2")
CORE = ("gy_2",)
CHIPS = ("gx_0", "gx_1", "gy_0", "gy_1")
C = 128
NB = 4
ROWS = NB * 64
TAPS = 27
EXT = 13
EPSILON = 1e-05
F32 = jnp.float32
BF16 = jnp.bfloat16
COUNT, FACE, CORNER, VALID, CORE_AT = 108, 109, 113, 117, 125
NEIGHBOURS = ((-1, 0), (1, 0), (0, -1), (0, 1), (-1, -1), (-1, 1), (1, -1), (1, 1))
CHUNK = 56
HALF = TAPS * C // 2
VMEM_BYTES = 16 << 20


def shift_matrix():
    shift = np.zeros((9, 4, 4, 9, 4, 4), np.float32)
    for b in range(3):
        for c in range(3):
            for q in range(4):
                for r in range(4):
                    y, x = q + b - 1, r + c - 1
                    ob = 0 if y < 0 else 1 if y < 4 else 2
                    oc = 0 if x < 0 else 1 if x < 4 else 2
                    shift[3 * b + c, q, r, 3 * ob + oc, y % 4, x % 4] = 1.0
    return shift.reshape(144, 144)


def sources():
    return [(0, 0, 3), (1, 1, 0), (2, 1, 1), (3, 1, 2), (4, 1, 3), (5, 2, 0)]


def sigmoid(v):
    return 1.0 / (1.0 + jnp.exp(-v))


def slope(v):
    s = sigmoid(v)
    return s * (1.0 + v * (1.0 - s))


def occupied_rows(meta):
    brick = lax.broadcasted_iota(jnp.int32, (ROWS, C), 0) // 64
    return (brick < meta[COUNT]).astype(F32)


def gather_columns(meta, ext, gathered, shift, columns):
    for b in range(NB):
        for plane, oa, source in sources():
            for d in range(9):
                entry = meta[27 * b + 9 * oa + d]
                gathered[16 * d : 16 * d + 16, (6 * b + plane) * C : (6 * b + plane + 1) * C] = ext[
                    entry, 16 * source : 16 * source + 16, :
                ]
    for b in range(NB):
        moved = jnp.dot(
            shift[...], gathered[:, 6 * b * C : 6 * (b + 1) * C], preferred_element_type=F32
        ).astype(BF16)
        for a in range(3):
            for p in range(4):
                for d in range(9):
                    k = 9 * a + d
                    columns[64 * b + 16 * p : 64 * b + 16 * p + 16, k * C : (k + 1) * C] = moved[
                        16 * d : 16 * d + 16, (p + a) * C : (p + a + 1) * C
                    ]


def convolve(columns, weight):
    return jnp.dot(columns[...], weight[...], preferred_element_type=F32)


def convolve_back(meta, dz, weight, shift_back, spread, moved, acc):
    for a in range(3):
        spread[a] = lax.dot_general(
            dz,
            weight[9 * a * C : 9 * (a + 1) * C, :],
            (((1,), (1,)), ((), ())),
            preferred_element_type=F32,
        )
    acc[...] = jnp.zeros_like(acc)
    for b in range(NB):
        for plane in range(6):
            taps = [a for a in range(3) if 0 <= plane - a < 4]
            for d in range(9):
                total = None
                for a in taps:
                    row = 64 * b + 16 * (plane - a)
                    piece = spread[a, row : row + 16, d * C : (d + 1) * C]
                    total = piece if total is None else total + piece
                moved[16 * d : 16 * d + 16, (6 * b + plane) * C : (6 * b + plane + 1) * C] = (
                    total.astype(BF16)
                )
    for b in range(NB):
        home = jnp.dot(
            shift_back[...], moved[:, 6 * b * C : 6 * (b + 1) * C], preferred_element_type=F32
        )
        for plane, oa, source in sources():
            for d in range(9):
                entry = meta[27 * b + 9 * oa + d]
                acc[entry, 16 * source : 16 * source + 16, :] += home[
                    16 * d : 16 * d + 16, plane * C : (plane + 1) * C
                ]


def write_sums(out, first, second):
    odd = lax.broadcasted_iota(jnp.int32, (8, C), 0) % 2
    both = jnp.where(odd == 0, jnp.broadcast_to(first, (8, C)), jnp.broadcast_to(second, (8, C)))
    out[...] = jnp.broadcast_to(both[None], (out.shape[0] // 8, 8, C)).reshape(out.shape)


def read_sums(got):
    total = jnp.sum(got[...].reshape(got.shape[0] // 8, 8, C), axis=0)
    odd = lax.broadcasted_iota(jnp.int32, (8, C), 0) % 2
    first = jnp.sum(jnp.where(odd == 0, total, 0.0), axis=0, keepdims=True)
    second = jnp.sum(jnp.where(odd == 1, total, 0.0), axis=0, keepdims=True)
    return first, second


def rows_sum(v):
    return jnp.sum(v, axis=0, keepdims=True)


def statistics(total, squares, voxels):
    center = total / voxels
    spread_sq = squares / voxels - center * center
    return center, lax.rsqrt(spread_sq + EPSILON)


def received_bricks(ux, lx, uy, ly):
    return (
        ux.at[0], lx.at[0], uy.at[0], ly.at[0], uy.at[1], ly.at[1], uy.at[2], ly.at[2]
    )


def sends_of(face, corner, x_up, x_low, y_faces):
    return (
        (face(0), x_up.at[0]), (corner(0), x_up.at[1]), (corner(1), x_up.at[2]),
        (face(1), x_low.at[0]), (corner(2), x_low.at[1]), (corner(3), x_low.at[2]),
        (face(2), y_faces.at[0]), (face(3), y_faces.at[1]),
    )


def select_sends(meta, field, x_up, x_low, y_faces):
    for entry, out in sends_of(
        lambda k: meta[FACE + k], lambda k: meta[CORNER + k], x_up, x_low, y_faces
    ):
        out[...] = field[entry]


def send_kernel(face_far, corner_far, field, x_up, x_low, y_faces, face, corner, sems):
    lists = [
        pltpu.make_async_copy(face_far, face, sems.at[8]),
        pltpu.make_async_copy(corner_far, corner, sems.at[9]),
    ]
    for copy in lists:
        copy.start()
    for copy in lists:
        copy.wait()
    copies = []
    for n, (entry, out) in enumerate(
        sends_of(lambda k: face[0, k, 0], lambda k: corner[0, k, 0], x_up, x_low, y_faces)
    ):
        copies.append(pltpu.make_async_copy(field.at[entry], out, sems.at[n]))
        copies[-1].start()
    for copy in copies:
        copy.wait()


def join_kernel(faces, first, second, up, low):
    up[0] = faces[0]
    up[1] = first[1]
    up[2] = second[1]
    low[0] = faces[1]
    low[1] = first[2]
    low[2] = second[2]


def first_kernel(
    meta, voxel_feats, ux, lx, uy, ly, weight_far, shift,
    z_out, ext, sums, x_up, x_low, y_faces, weight, gathered, columns, sem,
):
    fetch = pltpu.make_async_copy(weight_far, weight, sem)
    fetch.start()
    ext[NB + 8] = jnp.zeros((64, C), BF16)
    for b in range(NB):
        keep = (meta[COUNT] > b).astype(F32)
        ext[b] = (voxel_feats[b].astype(F32) * keep).astype(BF16)
    for e, brick in enumerate(received_bricks(ux, lx, uy, ly)):
        keep = meta[VALID + e].astype(F32)
        ext[NB + e] = (brick[...].astype(F32) * keep).astype(BF16)
    gather_columns(meta, ext, gathered, shift, columns)
    fetch.wait()
    z = convolve(columns, weight)
    z_out[...] = z.reshape(NB, 64, C)
    select_sends(meta, z_out, x_up, x_low, y_faces)
    masked = z * occupied_rows(meta)
    row = lax.broadcasted_iota(jnp.int32, (8, C), 0) % 4
    count = (64 * meta[COUNT]).astype(F32)
    part = jnp.where(
        row == 0, rows_sum(masked), jnp.where(row == 1, rows_sum(z * masked), count)
    )
    sums[...] = jnp.broadcast_to(part[None], (64, 8, C)).reshape(512, C)


def second_kernel(
    meta, got, z_one, ux, lx, uy, ly, norm, weight_far, shift,
    z_out, ext, sums, xh_out, recip_out, voxels_out, weight, gathered, columns, sem,
):
    fetch = pltpu.make_async_copy(weight_far, weight, sem)
    fetch.start()
    row = lax.broadcasted_iota(jnp.int32, (8, C), 0) % 4
    both = jnp.sum(got[...].reshape(64, 8, C), axis=0)
    total = rows_sum(jnp.where(row == 0, both, 0.0))
    squares = rows_sum(jnp.where(row == 1, both, 0.0))
    voxels = rows_sum(jnp.where(row == 2, both, 0.0))
    center, recip = statistics(total, squares, voxels)
    recip_out[...] = jnp.broadcast_to(recip, (8, C))
    voxels_out[...] = jnp.broadcast_to(voxels, (8, C))
    for e in range(EXT - 1):
        keep = meta[COUNT] > e if e < NB else meta[VALID + e - NB] > 0
        field = z_one[e] if e < NB else received_bricks(ux, lx, uy, ly)[e - NB][...]
        xh = (field - center) * recip
        xh_out[e] = xh
        u = norm[0:1] * xh + norm[2:3]
        ext[e] = (u * sigmoid(u) * keep.astype(F32)).astype(BF16)
    ext[EXT - 1] = jnp.zeros((64, C), BF16)
    gather_columns(meta, ext, gathered, shift, columns)
    fetch.wait()
    z = convolve(columns, weight)
    z_out[...] = z
    masked = z * occupied_rows(meta)
    write_sums(sums, rows_sum(masked), rows_sum(z * masked))


def third_kernel(
    meta, got, voxels, z_two, voxel_feats, grad_out, norm, out_feats, dv_out, xh_out, recip_out, sums
):
    total, squares = read_sums(got)
    center, recip = statistics(total, squares, voxels[0:1])
    recip_out[...] = jnp.broadcast_to(recip, (8, C))
    occupied = occupied_rows(meta)
    xh = (z_two[...] - center) * recip
    xh_out[...] = xh
    feats = voxel_feats[...].astype(F32) * occupied
    pre = norm[1:2] * xh + norm[3:4] + feats
    s = sigmoid(pre)
    out_feats[...] = (pre * s * occupied).astype(BF16)
    dv = grad_out[...].astype(F32) * occupied * (s * (1.0 + pre * (1.0 - s)))
    dv_out[...] = dv
    write_sums(sums, rows_sum(dv), rows_sum(dv * xh))


def norm_back(dv, xh, gain, recip, total, cross, voxels, occupied):
    return (occupied * gain * recip * (dv - total / voxels - xh * cross / voxels)).astype(BF16)


def send_gradients(acc, own, y_low, y_up, x_faces):
    own[...] = acc[0:NB].reshape(ROWS, C)
    y_low[0] = acc[NB + 2].astype(BF16)
    y_low[1] = acc[NB + 4].astype(BF16)
    y_low[2] = acc[NB + 6].astype(BF16)
    y_up[0] = acc[NB + 3].astype(BF16)
    y_up[1] = acc[NB + 5].astype(BF16)
    y_up[2] = acc[NB + 7].astype(BF16)
    x_faces[0] = acc[NB].astype(BF16)
    x_faces[1] = acc[NB + 1].astype(BF16)


def fourth_kernel(
    meta, got, voxels, dv, xh_two, recip, xh_one, norm, weight_far, shift_back,
    dz_out, own, y_low, y_up, x_faces, sums, grads, weight, spread, moved, acc, sem,
):
    fetch = pltpu.make_async_copy(weight_far, weight, sem)
    fetch.start()
    total, cross = read_sums(got)
    grads[0:1] = cross
    grads[1:2] = total
    dz = norm_back(
        dv[...], xh_two[...], norm[1:2], recip[0:1], total, cross, voxels[0:1], occupied_rows(meta)
    )
    dz_out[...] = dz
    fetch.wait()
    convolve_back(meta, dz, weight, shift_back, spread, moved, acc)
    send_gradients(acc, own, y_low, y_up, x_faces)
    first = jnp.zeros((64, C), F32)
    second = jnp.zeros((64, C), F32)
    for e in range(EXT - 1):
        keep = meta[COUNT] > e if e < NB else meta[VALID + e - NB] > 0
        xh = xh_one[e]
        du = acc[e] * slope(norm[0:1] * xh + norm[2:3]) * keep.astype(F32)
        first += du
        second += du * xh
    write_sums(sums, rows_sum(first), rows_sum(second))


def add_returned(meta, field, lx, ux, ly, uy):
    for ref, k, at, neighbour in (
        (lx, 0, FACE, 1), (ux, 0, FACE + 1, 0), (ly, 0, FACE + 2, 3), (uy, 0, FACE + 3, 2),
        (lx, 1, CORNER, 7), (lx, 2, CORNER + 1, 6),
        (ux, 1, CORNER + 2, 5), (ux, 2, CORNER + 3, 4),
    ):
        field[meta[at]] += ref[k].astype(F32) * meta[VALID + neighbour].astype(F32)


def fifth_kernel(
    meta, got, voxels, own_in, lx, ux, ly, uy, xh_one, recip, norm, weight_far, shift_back,
    dz_out, own, y_low, y_up, x_faces, grads, weight, field, spread, moved, acc, sem,
):
    fetch = pltpu.make_async_copy(weight_far, weight, sem)
    fetch.start()
    total, cross = read_sums(got)
    grads[0:1] = cross
    grads[1:2] = total
    field[...] = own_in[...].reshape(NB, 64, C)
    add_returned(meta, field, lx, ux, ly, uy)
    occupied = occupied_rows(meta)
    xh = xh_one[0:NB].reshape(ROWS, C)
    du = field[...].reshape(ROWS, C) * occupied * slope(norm[0:1] * xh + norm[2:3])
    dz = norm_back(du, xh, norm[0:1], recip[0:1], total, cross, voxels[0:1], occupied)
    dz_out[...] = dz
    fetch.wait()
    convolve_back(meta, dz, weight, shift_back, spread, moved, acc)
    send_gradients(acc, own, y_low, y_up, x_faces)


def taps_kernel(meta, ext, dz, shift, mine, other, gathered, columns, taps):
    gather_columns(meta, ext, gathered, shift, columns)
    for k in range(TAPS):
        taps[k * C : (k + 1) * C, :] = lax.dot_general(
            columns[:, k * C : (k + 1) * C],
            dz[...],
            (((0,), (0,)), ((), ())),
            preferred_element_type=F32,
        )
    here = meta[CORE_AT] == 0
    mine[30:32] = jnp.zeros((2, CHUNK, C), F32)
    other[30:32] = jnp.zeros((2, CHUNK, C), BF16)
    for c in range(31):
        full = min(CHUNK, HALF - CHUNK * c)
        at = CHUNK * c
        low = taps[at : at + full, :]
        high = taps[HALF + at : HALF + at + full, :]
        mine[c, 0:full, :] = jnp.where(here, low, high)
        other[c, 0:full, :] = jnp.where(here, high, low).astype(BF16)


def second_sum_kernel(mine, received, out):
    out[...] = (mine[...] + received[...].astype(F32)).astype(BF16)


def first_sum_kernel(mine, received, second, out):
    out[0:32] = (mine[...] + received[...].astype(F32)).astype(BF16)
    out[32:64] = second[...]


def total_kernel(voxels, pieces, out):
    total = jnp.sum(pieces[...].astype(F32), axis=0) / jnp.sqrt(voxels[0:1])
    out[...] = jnp.broadcast_to(total.astype(BF16)[None], (64, CHUNK, C))


def widen_kernel(meta, whole, partner, out):
    same = meta[CORE_AT] == pl.program_id(1)
    for c in range(31):
        full = min(CHUNK, HALF - CHUNK * c)
        half = jnp.where(same, whole[c].astype(F32), partner[c].astype(F32))
        out[0, 0, CHUNK * c : CHUNK * c + full, :] = half[0:full]


def last_kernel(meta, own, lx, ux, ly, uy, dv, grad_in, field):
    field[...] = own[...].reshape(NB, 64, C)
    add_returned(meta, field, lx, ux, ly, uy)
    total = (dv[...] + field[...].reshape(ROWS, C)) * occupied_rows(meta)
    grad_in[...] = total.astype(BF16)


def local(kernel, outs, ins, scratch=(), far=()):
    vmem = pl.BlockSpec(memory_space=pltpu.VMEM)
    smem = pl.BlockSpec(memory_space=pltpu.SMEM)
    hbm = pl.BlockSpec(memory_space=pltpu.HBM)
    specs = [hbm if n in far else smem if a.ndim == 1 else vmem for n, a in enumerate(ins)]
    return pl.pallas_call(
        kernel,
        out_shape=[jax.ShapeDtypeStruct(s, d) for s, d in outs],
        in_specs=specs,
        out_specs=[vmem] * len(outs),
        scratch_shapes=[pltpu.VMEM(*s) if isinstance(s, tuple) else s for s in scratch],
        compiler_params=pltpu.CompilerParams(vmem_limit_bytes=VMEM_BYTES),
        name=kernel.__name__,
    )(*ins)


def widen(meta, whole, partner):
    block = pl.BlockSpec((32, CHUNK, C), lambda conv, half: (conv, 0, 0))
    return pl.pallas_call(
        widen_kernel,
        grid=(2, 2),
        out_shape=jax.ShapeDtypeStruct((2, 2, HALF, C), F32),
        in_specs=[pl.BlockSpec(memory_space=pltpu.SMEM), block, block],
        out_specs=pl.BlockSpec((1, 1, HALF, C), lambda conv, half: (conv, half, 0, 0)),
        compiler_params=pltpu.CompilerParams(vmem_limit_bytes=VMEM_BYTES),
        name="widen_kernel",
    )(meta, whole, partner)


def shifted(value, axis, by):
    length = lax.axis_size(axis)
    return lax.ppermute(value, axis, [(i, (i + by) % length) for i in range(length)])


def exchange(value, axes):
    return lax.all_to_all(value, axes, 0, 0, tiled=True)


def swap(value):
    return lax.ppermute(value, CORE, [(0, 1), (1, 0)])


def join(faces, first, second):
    outs = [(first.shape, first.dtype)] * 2
    return local(join_kernel, outs, [faces, first, second])


def outward(x_up, x_low, y_faces):
    ux = shifted(x_up, GX, 1)
    lx = shifted(x_low, GX, -1)
    up, low = join(y_faces, ux, lx)
    uy = shifted(up, GY, 1)
    ly = shifted(low, GY, -1)
    return ux, lx, uy, ly


def homeward(y_low, y_up, x_faces):
    ly = shifted(y_low, GY, -1)
    uy = shifted(y_up, GY, 1)
    low, up = join(x_faces, ly, uy)
    lx = shifted(low, GX, -1)
    ux = shifted(up, GX, 1)
    return lx, ux, ly, uy


def body(
    voxel_feats,
    w_first,
    w_second,
    norm_gain,
    norm_shift,
    grad_out,
    brick_count,
    kernel_map,
    face_send,
    corner_send,
):
    i = lax.axis_index(GX)
    j = lax.axis_index(GY)
    dx = np.array([d[0] for d in NEIGHBOURS], np.int32)
    dy = np.array([d[1] for d in NEIGHBOURS], np.int32)
    inside = (i + dx >= 0) & (i + dx < 8) & (j + dy >= 0) & (j + dy < 16)
    meta = jnp.concatenate(
        [
            kernel_map.reshape(-1),
            brick_count,
            face_send.reshape(-1),
            corner_send.reshape(-1),
            inside.astype(jnp.int32),
            lax.axis_index(CORE).reshape(1),
        ]
    )
    norm = jnp.concatenate([norm_gain, norm_shift], axis=0)
    shift = jnp.asarray(shift_matrix(), BF16)
    shift_back = jnp.asarray(shift_matrix().T, BF16)
    flat_one = w_first.reshape(TAPS * C, C)
    flat_two = w_second.reshape(TAPS * C, C)
    brick = (64, C)
    three, two = (3,) + brick, (2,) + brick
    rows = (ROWS, C)
    sums = ((2 * 128, C), F32)
    ext = ((EXT,) + brick, BF16)
    list_xh = ((EXT - 1,) + brick, F32)
    row8 = ((8, C), F32)
    sem = pltpu.SemaphoreType.DMA
    weight = ((TAPS * C, C), BF16)
    gathered = ((144, 6 * NB * C), BF16)
    columns = ((ROWS, TAPS * C), BF16)
    forward = [weight, gathered, columns, sem(())]
    lists = [pltpu.SMEM((1, 4, 1), jnp.int32)] * 2

    sends = local(
        send_kernel,
        [(three, BF16), (three, BF16), (two, BF16)],
        [face_send, corner_send, voxel_feats],
        lists + [sem((10,))],
        far=(0, 1, 2),
    )
    received = outward(*sends)
    z_one, ext_one, part, *sends = local(
        first_kernel,
        [((NB,) + brick, F32), ext, ((512, C), F32), (three, F32), (three, F32), (two, F32)],
        [meta, voxel_feats, *received, flat_one, shift],
        forward,
        far=(6,),
    )
    received = outward(*sends)
    part = exchange(part, GX_GY)
    z_two, ext_two, part, xh_one, recip_one, voxels = local(
        second_kernel,
        [(rows, F32), ext, sums, list_xh, row8, row8],
        [meta, part, z_one, *received, norm, flat_two, shift],
        forward,
        far=(8,),
    )
    part = exchange(part, GX_GY)
    out_feats, dv, xh_two, recip_two, part = local(
        third_kernel,
        [(rows, BF16), (rows, F32), (rows, F32), row8, sums],
        [meta, part, voxels, z_two, voxel_feats.reshape(rows), grad_out.reshape(rows), norm],
    )
    part = exchange(part, GX_GY)
    back = [((3, ROWS, 9 * C), F32), gathered, ((EXT,) + brick, F32), sem(())]
    dz_two, own, y_low, y_up, x_faces, part, grads_two = local(
        fourth_kernel,
        [(rows, BF16), (rows, F32), (three, BF16), (three, BF16), (two, BF16), sums, ((2, C), F32)],
        [meta, part, voxels, dv, xh_two, recip_two, xh_one, norm, flat_two, shift_back],
        [weight] + back,
        far=(8,),
    )
    returned = homeward(y_low, y_up, x_faces)
    chunks = (32, CHUNK, C)
    halves = [(chunks, F32), (chunks, BF16)]
    products = [gathered, columns, ((TAPS * C, C), F32)]
    mine, other = local(taps_kernel, halves, [meta, ext_two, dz_two, shift], products)
    (second,) = local(second_sum_kernel, [(chunks, BF16)], [mine, swap(other)])
    part = exchange(part, GX_GY)
    dz_one, own, y_low, y_up, x_faces, grads_one = local(
        fifth_kernel,
        [(rows, BF16), (rows, F32), (three, BF16), (three, BF16), (two, BF16), ((2, C), F32)],
        [meta, part, voxels, own, *returned, xh_one, recip_one, norm, flat_one, shift_back],
        [weight, ((NB,) + brick, F32)] + back,
        far=(11,),
    )
    returned = homeward(y_low, y_up, x_faces)
    mine, other = local(taps_kernel, halves, [meta, ext_one, dz_one, shift], products)
    (grad_in,) = local(
        last_kernel, [(rows, BF16)], [meta, own, *returned, dv], [((NB,) + brick, F32)]
    )
    both = ((64, CHUNK, C), BF16)
    (part,) = local(first_sum_kernel, [both], [mine, swap(other), second])
    (whole,) = local(total_kernel, [both], [voxels, exchange(part, CHIPS)])
    whole = exchange(whole, CHIPS)
    weight_grads = widen(meta, whole, swap(whole)).reshape(2, TAPS, C, C)
    root = jnp.sqrt(voxels[0, 0])
    norm_grads = jnp.concatenate([grads_one, grads_two], axis=0) / root
    return (
        out_feats.reshape(NB, 64, C),
        grad_in.reshape(NB, 64, C),
        weight_grads,
        norm_grads,
    )


def solution(mesh):
    split = Mesh(mesh.devices.reshape(2, 4, 4, 2, 2), GX_GY)
    in_specs = (
        P(GX_GY, None, None),
        P(),
        P(),
        P(),
        P(),
        P(GX_GY, None, None),
        P(GX_GY),
        P(GX_GY, None),
        P(GX_GY, None, None),
        P(GX_GY, None, None),
    )
    out_specs = (P(GX_GY, None, None), P(GX_GY, None, None), P(), P())
    return jax.shard_map(body, mesh=split, in_specs=in_specs, out_specs=out_specs, check_vma=False)
```

```python
import jax
import jax.numpy as jnp
import numpy as np
from jax import lax
from jax.experimental import pallas as pl
from jax.experimental.pallas import tpu as pltpu
from jax.sharding import Mesh
from jax.sharding import PartitionSpec as P

GX = ("gx_0", "gx_1")
GY = ("gy_0", "gy_1", "gy_2")
GX_GY = ("gx_0", "gx_1", "gy_0", "gy_1", "gy_2")
CORE = ("gy_2",)
CHIPS = ("gx_0", "gx_1", "gy_0", "gy_1")
C = 128
NB = 4
ROWS = NB * 64
TAPS = 27
EXT = 13
EPSILON = 1e-05
F32 = jnp.float32
BF16 = jnp.bfloat16
COUNT, FACE, CORNER, VALID, CORE_AT = 108, 109, 113, 117, 125
NEIGHBOURS = ((-1, 0), (1, 0), (0, -1), (0, 1), (-1, -1), (-1, 1), (1, -1), (1, 1))
CHUNK = 56
HALF = TAPS * C // 2
VMEM_BYTES = 64 << 20
SPARE = 48 << 20


def shift_matrix(flipped):
    def places(axis):
        at = lax.broadcasted_iota(jnp.int32, (144, 144), axis)
        major = (at >= 48).astype(jnp.int32) + (at >= 96).astype(jnp.int32)
        minor = (at >> 4) - 3 * major
        return major, minor, (at >> 2) & 3, at & 3

    b, c, q, r = places(1 if flipped else 0)
    ob, oc, qs, rs = places(0 if flipped else 1)
    hit = (4 * ob + qs == q + b + 3) & (4 * oc + rs == r + c + 3)
    return hit.astype(F32).astype(BF16)


def sources():
    return [(0, 0, 3), (1, 1, 0), (2, 1, 1), (3, 1, 2), (4, 1, 3), (5, 2, 0)]


def sigmoid(v):
    return 1.0 / (1.0 + jnp.exp(-v))


def slope(v):
    s = sigmoid(v)
    return s * (1.0 + v * (1.0 - s))


def occupied_rows(meta):
    brick = lax.broadcasted_iota(jnp.int32, (ROWS, C), 0) // 64
    return (brick < meta[COUNT]).astype(F32)


def gather_columns(meta, ext, gathered, columns):
    shift = shift_matrix(False)
    for b in range(NB):
        for plane, oa, source in sources():
            for d in range(9):
                entry = meta[27 * b + 9 * oa + d]
                gathered[16 * d : 16 * d + 16, (6 * b + plane) * C : (6 * b + plane + 1) * C] = ext[
                    entry, 16 * source : 16 * source + 16, :
                ]
    for b in range(NB):
        moved = jnp.dot(
            shift, gathered[:, 6 * b * C : 6 * (b + 1) * C], preferred_element_type=F32
        ).astype(BF16)
        for a in range(3):
            for p in range(4):
                for d in range(9):
                    k = 9 * a + d
                    columns[64 * b + 16 * p : 64 * b + 16 * p + 16, k * C : (k + 1) * C] = moved[
                        16 * d : 16 * d + 16, (p + a) * C : (p + a + 1) * C
                    ]


def convolve(columns, weight):
    return jnp.dot(columns[...], weight[...], preferred_element_type=F32)


def convolve_back(meta, dz, weight, spread, moved, acc):
    shift_back = shift_matrix(True)
    for a in range(3):
        spread[a] = lax.dot_general(
            dz,
            weight[9 * a * C : 9 * (a + 1) * C, :],
            (((1,), (1,)), ((), ())),
            preferred_element_type=F32,
        )
    acc[...] = jnp.zeros_like(acc)
    for b in range(NB):
        for plane in range(6):
            taps = [a for a in range(3) if 0 <= plane - a < 4]
            for d in range(9):
                total = None
                for a in taps:
                    row = 64 * b + 16 * (plane - a)
                    piece = spread[a, row : row + 16, d * C : (d + 1) * C]
                    total = piece if total is None else total + piece
                moved[16 * d : 16 * d + 16, (6 * b + plane) * C : (6 * b + plane + 1) * C] = (
                    total.astype(BF16)
                )
    for b in range(NB):
        home = jnp.dot(
            shift_back, moved[:, 6 * b * C : 6 * (b + 1) * C], preferred_element_type=F32
        )
        for plane, oa, source in sources():
            for d in range(9):
                entry = meta[27 * b + 9 * oa + d]
                acc[entry, 16 * source : 16 * source + 16, :] += home[
                    16 * d : 16 * d + 16, plane * C : (plane + 1) * C
                ]


def write_sums(out, first, second):
    odd = lax.broadcasted_iota(jnp.int32, (8, C), 0) % 2
    both = jnp.where(odd == 0, jnp.broadcast_to(first, (8, C)), jnp.broadcast_to(second, (8, C)))
    out[...] = jnp.broadcast_to(both[None], (out.shape[0] // 8, 8, C)).reshape(out.shape)


def read_sums(got):
    total = jnp.sum(got[...].reshape(got.shape[0] // 8, 8, C), axis=0)
    odd = lax.broadcasted_iota(jnp.int32, (8, C), 0) % 2
    first = jnp.sum(jnp.where(odd == 0, total, 0.0), axis=0, keepdims=True)
    second = jnp.sum(jnp.where(odd == 1, total, 0.0), axis=0, keepdims=True)
    return first, second


def rows_sum(v):
    return jnp.sum(v, axis=0, keepdims=True)


def statistics(total, squares, voxels):
    center = total / voxels
    spread_sq = squares / voxels - center * center
    return center, lax.rsqrt(spread_sq + EPSILON)


def received_bricks(ux, lx, uy, ly):
    return (
        ux.at[0], lx.at[0], uy.at[0], ly.at[0], uy.at[1], ly.at[1], uy.at[2], ly.at[2]
    )


def sends_of(face, corner, x_up, x_low, y_faces):
    return (
        (face(0), x_up.at[0]), (corner(0), x_up.at[1]), (corner(1), x_up.at[2]),
        (face(1), x_low.at[0]), (corner(2), x_low.at[1]), (corner(3), x_low.at[2]),
        (face(2), y_faces.at[0]), (face(3), y_faces.at[1]),
    )


def select_sends(meta, field, x_up, x_low, y_faces):
    for entry, out in sends_of(
        lambda k: meta[FACE + k], lambda k: meta[CORNER + k], x_up, x_low, y_faces
    ):
        out[...] = field[entry]


def send_kernel(lists, field, x_up, x_low, y_faces):
    for entry, out in sends_of(lambda k: lists[k], lambda k: lists[4 + k], x_up, x_low, y_faces):
        out[...] = field[entry]


def join_kernel(faces, first, second, up, low):
    up[0] = faces[0]
    up[1] = first[1]
    up[2] = second[1]
    low[0] = faces[1]
    low[1] = first[2]
    low[2] = second[2]


def first_kernel(
    meta, voxel_feats, ux, lx, uy, ly, weight_far,
    z_out, ext, sums, x_up, x_low, y_faces, weight, gathered, columns, sem,
):
    fetch = pltpu.make_async_copy(weight_far, weight, sem)
    fetch.start()
    ext[NB + 8] = jnp.zeros((64, C), BF16)
    for b in range(NB):
        keep = (meta[COUNT] > b).astype(F32)
        ext[b] = (voxel_feats[b].astype(F32) * keep).astype(BF16)
    for e, brick in enumerate(received_bricks(ux, lx, uy, ly)):
        keep = meta[VALID + e].astype(F32)
        ext[NB + e] = (brick[...].astype(F32) * keep).astype(BF16)
    gather_columns(meta, ext, gathered, columns)
    fetch.wait()
    z = convolve(columns, weight)
    z_out[...] = z.reshape(NB, 64, C)
    select_sends(meta, z_out, x_up, x_low, y_faces)
    masked = z * occupied_rows(meta)
    row = lax.broadcasted_iota(jnp.int32, (8, C), 0) % 4
    count = (64 * meta[COUNT]).astype(F32)
    part = jnp.where(
        row == 0, rows_sum(masked), jnp.where(row == 1, rows_sum(z * masked), count)
    )
    sums[...] = jnp.broadcast_to(part[None], (64, 8, C)).reshape(512, C)


def second_kernel(
    meta, got, z_one, ux, lx, uy, ly, norm, weight_far,
    z_out, ext, sums, xh_out, recip_out, voxels_out, weight, gathered, columns, sem,
):
    fetch = pltpu.make_async_copy(weight_far, weight, sem)
    fetch.start()
    row = lax.broadcasted_iota(jnp.int32, (8, C), 0) % 4
    both = jnp.sum(got[...].reshape(64, 8, C), axis=0)
    total = rows_sum(jnp.where(row == 0, both, 0.0))
    squares = rows_sum(jnp.where(row == 1, both, 0.0))
    voxels = rows_sum(jnp.where(row == 2, both, 0.0))
    center, recip = statistics(total, squares, voxels)
    recip_out[...] = jnp.broadcast_to(recip, (8, C))
    voxels_out[...] = jnp.broadcast_to(voxels, (8, C))
    for e in range(EXT - 1):
        keep = meta[COUNT] > e if e < NB else meta[VALID + e - NB] > 0
        field = z_one[e] if e < NB else received_bricks(ux, lx, uy, ly)[e - NB][...]
        xh = (field - center) * recip
        xh_out[e] = xh
        u = norm[0:1] * xh + norm[2:3]
        ext[e] = (u * sigmoid(u) * keep.astype(F32)).astype(BF16)
    ext[EXT - 1] = jnp.zeros((64, C), BF16)
    gather_columns(meta, ext, gathered, columns)
    fetch.wait()
    z = convolve(columns, weight)
    z_out[...] = z
    masked = z * occupied_rows(meta)
    write_sums(sums, rows_sum(masked), rows_sum(z * masked))


def third_kernel(
    meta, got, voxels, z_two, voxel_feats, grad_out, norm, out_feats, dv_out, xh_out, recip_out, sums
):
    total, squares = read_sums(got)
    center, recip = statistics(total, squares, voxels[0:1])
    recip_out[...] = jnp.broadcast_to(recip, (8, C))
    occupied = occupied_rows(meta)
    xh = (z_two[...] - center) * recip
    xh_out[...] = xh
    feats = voxel_feats[...].astype(F32) * occupied
    pre = norm[1:2] * xh + norm[3:4] + feats
    s = sigmoid(pre)
    out_feats[...] = (pre * s * occupied).astype(BF16)
    dv = grad_out[...].astype(F32) * occupied * (s * (1.0 + pre * (1.0 - s)))
    dv_out[...] = dv
    write_sums(sums, rows_sum(dv), rows_sum(dv * xh))


def norm_back(dv, xh, gain, recip, total, cross, voxels, occupied):
    return (occupied * gain * recip * (dv - total / voxels - xh * cross / voxels)).astype(BF16)


def send_gradients(acc, own, y_low, y_up, x_faces):
    own[...] = acc[0:NB].reshape(ROWS, C)
    y_low[0] = acc[NB + 2].astype(BF16)
    y_low[1] = acc[NB + 4].astype(BF16)
    y_low[2] = acc[NB + 6].astype(BF16)
    y_up[0] = acc[NB + 3].astype(BF16)
    y_up[1] = acc[NB + 5].astype(BF16)
    y_up[2] = acc[NB + 7].astype(BF16)
    x_faces[0] = acc[NB].astype(BF16)
    x_faces[1] = acc[NB + 1].astype(BF16)


def fourth_kernel(
    meta, got, voxels, dv, xh_two, recip, xh_one, norm, weight_far,
    dz_out, own, y_low, y_up, x_faces, sums, grads, weight, spread, moved, acc, sem,
):
    fetch = pltpu.make_async_copy(weight_far, weight, sem)
    fetch.start()
    total, cross = read_sums(got)
    grads[0:1] = cross
    grads[1:2] = total
    dz = norm_back(
        dv[...], xh_two[...], norm[1:2], recip[0:1], total, cross, voxels[0:1], occupied_rows(meta)
    )
    dz_out[...] = dz
    fetch.wait()
    convolve_back(meta, dz, weight, spread, moved, acc)
    send_gradients(acc, own, y_low, y_up, x_faces)
    first = jnp.zeros((64, C), F32)
    second = jnp.zeros((64, C), F32)
    for e in range(EXT - 1):
        keep = meta[COUNT] > e if e < NB else meta[VALID + e - NB] > 0
        xh = xh_one[e]
        du = acc[e] * slope(norm[0:1] * xh + norm[2:3]) * keep.astype(F32)
        first += du
        second += du * xh
    write_sums(sums, rows_sum(first), rows_sum(second))


def add_returned(meta, field, lx, ux, ly, uy):
    for ref, k, at, neighbour in (
        (lx, 0, FACE, 1), (ux, 0, FACE + 1, 0), (ly, 0, FACE + 2, 3), (uy, 0, FACE + 3, 2),
        (lx, 1, CORNER, 7), (lx, 2, CORNER + 1, 6),
        (ux, 1, CORNER + 2, 5), (ux, 2, CORNER + 3, 4),
    ):
        field[meta[at]] += ref[k].astype(F32) * meta[VALID + neighbour].astype(F32)


def fifth_kernel(
    meta, got, voxels, own_in, lx, ux, ly, uy, xh_one, recip, norm, weight_far,
    dz_out, own, y_low, y_up, x_faces, grads, weight, field, spread, moved, acc, sem,
):
    fetch = pltpu.make_async_copy(weight_far, weight, sem)
    fetch.start()
    total, cross = read_sums(got)
    grads[0:1] = cross
    grads[1:2] = total
    field[...] = own_in[...].reshape(NB, 64, C)
    add_returned(meta, field, lx, ux, ly, uy)
    occupied = occupied_rows(meta)
    xh = xh_one[0:NB].reshape(ROWS, C)
    du = field[...].reshape(ROWS, C) * occupied * slope(norm[0:1] * xh + norm[2:3])
    dz = norm_back(du, xh, norm[0:1], recip[0:1], total, cross, voxels[0:1], occupied)
    dz_out[...] = dz
    fetch.wait()
    convolve_back(meta, dz, weight, spread, moved, acc)
    send_gradients(acc, own, y_low, y_up, x_faces)


def taps_kernel(meta, ext, dz, mine, other, gathered, columns, taps):
    gather_columns(meta, ext, gathered, columns)
    for k in range(TAPS):
        taps[k * C : (k + 1) * C, :] = lax.dot_general(
            columns[:, k * C : (k + 1) * C],
            dz[...],
            (((0,), (0,)), ((), ())),
            preferred_element_type=F32,
        )
    here = meta[CORE_AT] == 0
    mine[30:32] = jnp.zeros((2, CHUNK, C), F32)
    other[30:32] = jnp.zeros((2, CHUNK, C), BF16)
    for c in range(31):
        full = min(CHUNK, HALF - CHUNK * c)
        at = CHUNK * c
        low = taps[at : at + full, :]
        high = taps[HALF + at : HALF + at + full, :]
        mine[c, 0:full, :] = jnp.where(here, low, high)
        other[c, 0:full, :] = jnp.where(here, high, low).astype(BF16)


def second_sum_kernel(mine, received, out):
    out[...] = (mine[...] + received[...].astype(F32)).astype(BF16)


def first_sum_kernel(mine, received, second, out):
    out[0:32] = (mine[...] + received[...].astype(F32)).astype(BF16)
    out[32:64] = second[...]


def total_kernel(voxels, pieces, out):
    total = jnp.sum(pieces[...].astype(F32), axis=0) / jnp.sqrt(voxels[0:1])
    out[...] = jnp.broadcast_to(total.astype(BF16)[None], (64, CHUNK, C))


def widen_kernel(meta, whole, partner, out):
    same = meta[CORE_AT] == pl.program_id(1)
    for c in range(31):
        full = min(CHUNK, HALF - CHUNK * c)
        half = jnp.where(same, whole[c].astype(F32), partner[c].astype(F32))
        out[0, 0, CHUNK * c : CHUNK * c + full, :] = half[0:full]


def last_kernel(meta, own, lx, ux, ly, uy, dv, grad_in, field):
    field[...] = own[...].reshape(NB, 64, C)
    add_returned(meta, field, lx, ux, ly, uy)
    total = (dv[...] + field[...].reshape(ROWS, C)) * occupied_rows(meta)
    grad_in[...] = total.astype(BF16)


def local(kernel, outs, ins, scratch=(), far=(), spare=SPARE):
    vmem = pl.BlockSpec(memory_space=pltpu.VMEM)
    smem = pl.BlockSpec(memory_space=pltpu.SMEM)
    hbm = pl.BlockSpec(memory_space=pltpu.HBM)
    specs = [hbm if n in far else smem if a.ndim == 1 else vmem for n, a in enumerate(ins)]
    return pl.pallas_call(
        kernel,
        out_shape=[jax.ShapeDtypeStruct(s, d) for s, d in outs],
        in_specs=specs,
        out_specs=[vmem] * len(outs),
        scratch_shapes=[pltpu.VMEM(*s) if isinstance(s, tuple) else s for s in scratch],
        compiler_params=pltpu.CompilerParams(vmem_limit_bytes=VMEM_BYTES - spare),
    )(*ins)


def widen(meta, whole, partner):
    block = pl.BlockSpec((32, CHUNK, C), lambda conv, half: (conv, 0, 0))
    return pl.pallas_call(
        widen_kernel,
        grid=(2, 2),
        out_shape=jax.ShapeDtypeStruct((2, 2, HALF, C), F32),
        in_specs=[pl.BlockSpec(memory_space=pltpu.SMEM), block, block],
        out_specs=pl.BlockSpec((1, 1, HALF, C), lambda conv, half: (conv, half, 0, 0)),
        compiler_params=pltpu.CompilerParams(vmem_limit_bytes=16 << 20),
        name="widen_kernel",
    )(meta, whole, partner)


def shifted(value, axis, by):
    length = lax.axis_size(axis)
    return lax.ppermute(value, axis, [(i, (i + by) % length) for i in range(length)])


def exchange(value, axes):
    return lax.all_to_all(value, axes, 0, 0, tiled=True)


def swap(value):
    return lax.ppermute(value, CORE, [(0, 1), (1, 0)])


def join(faces, first, second):
    outs = [(first.shape, first.dtype)] * 2
    return local(join_kernel, outs, [faces, first, second])


def pair(first, second, axis, by):
    return shifted(first, axis, by), shifted(second, axis, -by)


def outward(x_up, x_low, y_faces):
    ux, lx = pair(x_up, x_low, GX, 1)
    up, low = join(y_faces, ux, lx)
    uy, ly = pair(up, low, GY, 1)
    return ux, lx, uy, ly


def homeward(y_low, y_up, x_faces):
    ly, uy = pair(y_low, y_up, GY, -1)
    low, up = join(x_faces, ly, uy)
    lx, ux = pair(low, up, GX, -1)
    return lx, ux, ly, uy


def program(
    voxel_feats,
    w_first,
    w_second,
    norm_gain,
    norm_shift,
    grad_out,
    brick_count,
    kernel_map,
    face_send,
    corner_send,
):
    lists = jnp.concatenate([face_send.reshape(4), corner_send.reshape(4)])
    i = lax.axis_index(GX)
    j = lax.axis_index(GY)
    dx = np.array([d[0] for d in NEIGHBOURS], np.int32)
    dy = np.array([d[1] for d in NEIGHBOURS], np.int32)
    inside = (i + dx >= 0) & (i + dx < 8) & (j + dy >= 0) & (j + dy < 16)
    meta = jnp.concatenate(
        [
            kernel_map.reshape(-1),
            brick_count,
            lists,
            inside.astype(jnp.int32),
            lax.axis_index(CORE).reshape(1),
        ]
    )
    norm = jnp.concatenate([norm_gain, norm_shift], axis=0)
    flat_one = w_first.reshape(TAPS * C, C)
    flat_two = w_second.reshape(TAPS * C, C)
    brick = (64, C)
    three, two = (3,) + brick, (2,) + brick
    rows = (ROWS, C)
    sums = ((2 * 128, C), F32)
    ext = ((EXT,) + brick, BF16)
    list_xh = ((EXT - 1,) + brick, F32)
    row8 = ((8, C), F32)
    sem = pltpu.SemaphoreType.DMA
    weight = ((TAPS * C, C), BF16)
    gathered = ((144, 6 * NB * C), BF16)
    columns = ((ROWS, TAPS * C), BF16)
    forward = [weight, gathered, columns, sem(())]

    sends = local(
        send_kernel, [(three, BF16), (three, BF16), (two, BF16)], [lists, voxel_feats]
    )
    received = outward(*sends)
    z_one, ext_one, part, *sends = local(
        first_kernel,
        [((NB,) + brick, F32), ext, ((512, C), F32), (three, F32), (three, F32), (two, F32)],
        [meta, voxel_feats, *received, flat_one],
        forward,
        far=(6,),
    )
    received = outward(*sends)
    part = exchange(part, GX_GY)
    z_two, ext_two, part, xh_one, recip_one, voxels = local(
        second_kernel,
        [(rows, F32), ext, sums, list_xh, row8, row8],
        [meta, part, z_one, *received, norm, flat_two],
        forward,
        far=(8,),
    )
    part = exchange(part, GX_GY)
    out_feats, dv, xh_two, recip_two, part = local(
        third_kernel,
        [(rows, BF16), (rows, F32), (rows, F32), row8, sums],
        [meta, part, voxels, z_two, voxel_feats.reshape(rows), grad_out.reshape(rows), norm],
    )
    part = exchange(part, GX_GY)
    back = [((3, ROWS, 9 * C), F32), gathered, ((EXT,) + brick, F32), sem(())]
    dz_two, own, y_low, y_up, x_faces, part, grads_two = local(
        fourth_kernel,
        [(rows, BF16), (rows, F32), (three, BF16), (three, BF16), (two, BF16), sums, ((2, C), F32)],
        [meta, part, voxels, dv, xh_two, recip_two, xh_one, norm, flat_two],
        [weight] + back,
        far=(8,),
    )
    returned = homeward(y_low, y_up, x_faces)
    chunks = (32, CHUNK, C)
    halves = [(chunks, F32), (chunks, BF16)]
    products = [gathered, columns, ((TAPS * C, C), F32)]
    mine, other = local(taps_kernel, halves, [meta, ext_two, dz_two], products)
    (second,) = local(second_sum_kernel, [(chunks, BF16)], [mine, swap(other)])
    part = exchange(part, GX_GY)
    dz_one, own, y_low, y_up, x_faces, grads_one = local(
        fifth_kernel,
        [(rows, BF16), (rows, F32), (three, BF16), (three, BF16), (two, BF16), ((2, C), F32)],
        [meta, part, voxels, own, *returned, xh_one, recip_one, norm, flat_one],
        [weight, ((NB,) + brick, F32)] + back,
        far=(11,),
    )
    returned = homeward(y_low, y_up, x_faces)
    mine, other = local(taps_kernel, halves, [meta, ext_one, dz_one], products)
    (grad_in,) = local(
        last_kernel, [(rows, BF16)], [meta, own, *returned, dv], [((NB,) + brick, F32)]
    )
    both = ((64, CHUNK, C), BF16)
    (part,) = local(first_sum_kernel, [both], [mine, swap(other), second])
    (whole,) = local(total_kernel, [both], [voxels, exchange(part, CHIPS)])
    whole = exchange(whole, CHIPS)
    weight_grads = widen(meta, whole, swap(whole)).reshape(2, TAPS, C, C)
    root = jnp.sqrt(voxels[0, 0])
    norm_grads = jnp.concatenate([grads_one, grads_two], axis=0) / root
    return (
        out_feats.reshape(NB, 64, C),
        grad_in.reshape(NB, 64, C),
        weight_grads,
        norm_grads,
    )


def solution(mesh):
    split = Mesh(mesh.devices.reshape(2, 4, 4, 2, 2), GX_GY)
    in_specs = (
        P(GX_GY, None, None),
        P(),
        P(),
        P(),
        P(),
        P(GX_GY, None, None),
        P(GX_GY),
        P(GX_GY, None),
        P(GX_GY, None, None),
        P(GX_GY, None, None),
    )
    out_specs = (P(GX_GY, None, None), P(GX_GY, None, None), P(), P())
    return jax.shard_map(program, mesh=split, in_specs=in_specs, out_specs=out_specs, check_vma=False)
```

```python
import jax
import jax.numpy as jnp
import numpy as np
from jax import lax
from jax.experimental import pallas as pl
from jax.experimental.pallas import tpu as pltpu
from jax.sharding import Mesh
from jax.sharding import PartitionSpec as P

GX = ("gx_0", "gx_1")
GY = ("gy_0", "gy_1", "gy_2")
GX_GY = ("gx_0", "gx_1", "gy_0", "gy_1", "gy_2")
CORE = ("gy_2",)
CHIPS = ("gx_0", "gx_1", "gy_0", "gy_1")
C = 128
NB = 4
ROWS = NB * 64
TAPS = 27
EXT = 13
EPSILON = 1e-05
F32 = jnp.float32
BF16 = jnp.bfloat16
COUNT, FACE, CORNER, VALID, CORE_AT = 108, 109, 113, 117, 125
NEIGHBOURS = ((-1, 0), (1, 0), (0, -1), (0, 1), (-1, -1), (-1, 1), (1, -1), (1, 1))
CHUNK = 56
HALF = TAPS * C // 2
VMEM_BYTES = 16 << 20


def row_of(k):
    return slice(k, k + 1)


VOXELS = row_of(0)
RECIP = (row_of(1), row_of(2))
NORM_ROWS = slice(4, 8)
GAIN = (row_of(4), row_of(5))
SHIFT = (row_of(6), row_of(7))
CROSS = (row_of(8), row_of(9))
TOTAL = (row_of(10), row_of(11))


def shift_matrix(flipped):
    def places(axis):
        at = lax.broadcasted_iota(jnp.int32, (144, 144), axis)
        major = (at >= 48).astype(jnp.int32) + (at >= 96).astype(jnp.int32)
        minor = (at >> 4) - 3 * major
        return major, minor, (at >> 2) & 3, at & 3

    b, c, q, r = places(1 if flipped else 0)
    ob, oc, qs, rs = places(0 if flipped else 1)
    hit = (4 * ob + qs == q + b + 3) & (4 * oc + rs == r + c + 3)
    return hit.astype(F32).astype(BF16)


def sources():
    return [(0, 0, 3), (1, 1, 0), (2, 1, 1), (3, 1, 2), (4, 1, 3), (5, 2, 0)]


def sigmoid(v):
    return 1.0 / (1.0 + jnp.exp(-v))


def slope(v):
    s = sigmoid(v)
    return s * (1.0 + v * (1.0 - s))


def occupied_rows(meta):
    brick = lax.broadcasted_iota(jnp.int32, (ROWS, C), 0) // 64
    return (brick < meta[COUNT]).astype(F32)


def gather_columns(meta, ext, gathered, columns):
    shift = shift_matrix(False)
    for b in range(NB):
        for plane, oa, source in sources():
            for d in range(9):
                entry = meta[27 * b + 9 * oa + d]
                gathered[16 * d : 16 * d + 16, (6 * b + plane) * C : (6 * b + plane + 1) * C] = ext[
                    entry, 16 * source : 16 * source + 16, :
                ]
    for b in range(NB):
        moved = jnp.dot(
            shift, gathered[:, 6 * b * C : 6 * (b + 1) * C], preferred_element_type=F32
        ).astype(BF16)
        for a in range(3):
            for p in range(4):
                for d in range(9):
                    k = 9 * a + d
                    columns[64 * b + 16 * p : 64 * b + 16 * p + 16, k * C : (k + 1) * C] = moved[
                        16 * d : 16 * d + 16, (p + a) * C : (p + a + 1) * C
                    ]


def convolve(columns, weight):
    return jnp.dot(columns[...], weight[...], preferred_element_type=F32)


def convolve_back(meta, dz, weight, spread, moved, acc):
    shift_back = shift_matrix(True)
    for a in range(3):
        spread[a] = lax.dot_general(
            dz,
            weight[9 * a * C : 9 * (a + 1) * C, :],
            (((1,), (1,)), ((), ())),
            preferred_element_type=F32,
        )
    acc[...] = jnp.zeros_like(acc)
    for b in range(NB):
        for plane in range(6):
            taps = [a for a in range(3) if 0 <= plane - a < 4]
            for d in range(9):
                total = None
                for a in taps:
                    row = 64 * b + 16 * (plane - a)
                    piece = spread[a, row : row + 16, d * C : (d + 1) * C]
                    total = piece if total is None else total + piece
                moved[16 * d : 16 * d + 16, (6 * b + plane) * C : (6 * b + plane + 1) * C] = (
                    total.astype(BF16)
                )
    for b in range(NB):
        home = jnp.dot(
            shift_back, moved[:, 6 * b * C : 6 * (b + 1) * C], preferred_element_type=F32
        )
        for plane, oa, source in sources():
            for d in range(9):
                entry = meta[27 * b + 9 * oa + d]
                acc[entry, 16 * source : 16 * source + 16, :] += home[
                    16 * d : 16 * d + 16, plane * C : (plane + 1) * C
                ]


def write_sums(out, first, second):
    odd = lax.broadcasted_iota(jnp.int32, (8, C), 0) % 2
    both = jnp.where(odd == 0, jnp.broadcast_to(first, (8, C)), jnp.broadcast_to(second, (8, C)))
    out[...] = jnp.broadcast_to(both[None], (out.shape[0] // 8, 8, C)).reshape(out.shape)


def read_sums(got):
    total = jnp.sum(got[...].reshape(got.shape[0] // 8, 8, C), axis=0)
    odd = lax.broadcasted_iota(jnp.int32, (8, C), 0) % 2
    first = jnp.sum(jnp.where(odd == 0, total, 0.0), axis=0, keepdims=True)
    second = jnp.sum(jnp.where(odd == 1, total, 0.0), axis=0, keepdims=True)
    return first, second


def rows_sum(v):
    return jnp.sum(v, axis=0, keepdims=True)


def statistics(total, squares, voxels):
    center = total / voxels
    spread_sq = squares / voxels - center * center
    return center, lax.rsqrt(spread_sq + EPSILON)


def received_bricks(ux, lx, uy, ly):
    return (
        ux.at[0], lx.at[0], uy.at[0], ly.at[0], uy.at[1], ly.at[1], uy.at[2], ly.at[2]
    )


def sends_of(face, corner, x_up, x_low, y_faces):
    return (
        (face(0), x_up.at[0]), (corner(0), x_up.at[1]), (corner(1), x_up.at[2]),
        (face(1), x_low.at[0]), (corner(2), x_low.at[1]), (corner(3), x_low.at[2]),
        (face(2), y_faces.at[0]), (face(3), y_faces.at[1]),
    )


def select_sends(meta, field, x_up, x_low, y_faces):
    for entry, out in sends_of(
        lambda k: meta[FACE + k], lambda k: meta[CORNER + k], x_up, x_low, y_faces
    ):
        out[...] = field[entry]


def send_kernel(lists, field, x_up, x_low, y_faces, kept):
    kept[...] = field[...]
    for entry, out in sends_of(lambda k: lists[k], lambda k: lists[4 + k], x_up, x_low, y_faces):
        out[...] = field[entry]


def join_kernel(faces, first, second, up, low):
    up[0] = faces[0]
    up[1] = first[1]
    up[2] = second[1]
    low[0] = faces[1]
    low[1] = first[2]
    low[2] = second[2]


def first_kernel(
    meta, voxel_feats, ux, lx, uy, ly, weight_far,
    z_out, ext, sums, x_up, x_low, y_faces, weight, gathered, columns, sem,
):
    fetch = pltpu.make_async_copy(weight_far, weight, sem)
    fetch.start()
    ext[NB + 8] = jnp.zeros((64, C), BF16)
    for b in range(NB):
        keep = (meta[COUNT] > b).astype(F32)
        ext[b] = (voxel_feats[b].astype(F32) * keep).astype(BF16)
    for e, brick in enumerate(received_bricks(ux, lx, uy, ly)):
        keep = meta[VALID + e].astype(F32)
        ext[NB + e] = (brick[...].astype(F32) * keep).astype(BF16)
    gather_columns(meta, ext, gathered, columns)
    fetch.wait()
    z = convolve(columns, weight)
    z_out[...] = z.reshape(NB, 64, C)
    select_sends(meta, z_out, x_up, x_low, y_faces)
    masked = z * occupied_rows(meta)
    row = lax.broadcasted_iota(jnp.int32, (8, C), 0) % 4
    count = (64 * meta[COUNT]).astype(F32)
    part = jnp.where(
        row == 0, rows_sum(masked), jnp.where(row == 1, rows_sum(z * masked), count)
    )
    sums[...] = jnp.broadcast_to(part[None], (64, 8, C)).reshape(512, C)


def second_kernel(
    meta, got, z_one, ux, lx, uy, ly, norm, weight_far,
    z_out, ext, sums, xh_out, consts, weight, gathered, columns, sem,
):
    fetch = pltpu.make_async_copy(weight_far, weight, sem)
    fetch.start()
    row = lax.broadcasted_iota(jnp.int32, (8, C), 0) % 4
    both = jnp.sum(got[...].reshape(64, 8, C), axis=0)
    total = rows_sum(jnp.where(row == 0, both, 0.0))
    squares = rows_sum(jnp.where(row == 1, both, 0.0))
    voxels = rows_sum(jnp.where(row == 2, both, 0.0))
    center, recip = statistics(total, squares, voxels)
    consts[...] = jnp.zeros_like(consts)
    consts[VOXELS] = voxels
    consts[RECIP[0]] = recip
    consts[NORM_ROWS] = norm[...]
    for e in range(EXT - 1):
        keep = meta[COUNT] > e if e < NB else meta[VALID + e - NB] > 0
        field = z_one[e] if e < NB else received_bricks(ux, lx, uy, ly)[e - NB][...]
        xh = (field - center) * recip
        xh_out[e] = xh
        u = norm[0:1] * xh + norm[2:3]
        ext[e] = (u * sigmoid(u) * keep.astype(F32)).astype(BF16)
    ext[EXT - 1] = jnp.zeros((64, C), BF16)
    gather_columns(meta, ext, gathered, columns)
    fetch.wait()
    z = convolve(columns, weight)
    z_out[...] = z
    masked = z * occupied_rows(meta)
    write_sums(sums, rows_sum(masked), rows_sum(z * masked))


def third_kernel(
    meta, got, constants, z_two, voxel_feats, grad_out, out_feats, dv_out, xh_out, consts, sums
):
    total, squares = read_sums(got)
    center, recip = statistics(total, squares, constants[VOXELS])
    consts[...] = constants[...]
    consts[RECIP[1]] = recip
    occupied = occupied_rows(meta)
    xh = (z_two[...] - center) * recip
    xh_out[...] = xh
    feats = voxel_feats[...].astype(F32) * occupied
    pre = constants[GAIN[1]] * xh + constants[SHIFT[1]] + feats
    s = sigmoid(pre)
    out_feats[...] = (pre * s * occupied).astype(BF16)
    dv = grad_out[...].astype(F32) * occupied * (s * (1.0 + pre * (1.0 - s)))
    dv_out[...] = dv
    write_sums(sums, rows_sum(dv), rows_sum(dv * xh))


def norm_back(dv, xh, consts, number, total, cross, occupied):
    voxels = consts[VOXELS]
    scale = occupied * consts[GAIN[number]] * consts[RECIP[number]]
    return (scale * (dv - total / voxels - xh * cross / voxels)).astype(BF16)


def send_gradients(acc, own, y_low, y_up, x_faces):
    own[...] = acc[0:NB].reshape(ROWS, C)
    y_low[0] = acc[NB + 2].astype(BF16)
    y_low[1] = acc[NB + 4].astype(BF16)
    y_low[2] = acc[NB + 6].astype(BF16)
    y_up[0] = acc[NB + 3].astype(BF16)
    y_up[1] = acc[NB + 5].astype(BF16)
    y_up[2] = acc[NB + 7].astype(BF16)
    x_faces[0] = acc[NB].astype(BF16)
    x_faces[1] = acc[NB + 1].astype(BF16)


def fourth_kernel(
    meta, got, dv, xh_two, constants, xh_one, weight_far,
    dz_out, own, y_low, y_up, x_faces, sums, consts, weight, spread, moved, acc, sem,
):
    fetch = pltpu.make_async_copy(weight_far, weight, sem)
    fetch.start()
    total, cross = read_sums(got)
    consts[...] = constants[...]
    consts[CROSS[1]] = cross
    consts[TOTAL[1]] = total
    dz = norm_back(dv[...], xh_two[...], constants, 1, total, cross, occupied_rows(meta))
    dz_out[...] = dz
    fetch.wait()
    convolve_back(meta, dz, weight, spread, moved, acc)
    send_gradients(acc, own, y_low, y_up, x_faces)
    first = jnp.zeros((64, C), F32)
    second = jnp.zeros((64, C), F32)
    for e in range(EXT - 1):
        keep = meta[COUNT] > e if e < NB else meta[VALID + e - NB] > 0
        xh = xh_one[e]
        du = acc[e] * slope(constants[GAIN[0]] * xh + constants[SHIFT[0]]) * keep.astype(F32)
        first += du
        second += du * xh
    write_sums(sums, rows_sum(first), rows_sum(second))


def add_returned(meta, field, lx, ux, ly, uy):
    for ref, k, at, neighbour in (
        (lx, 0, FACE, 1), (ux, 0, FACE + 1, 0), (ly, 0, FACE + 2, 3), (uy, 0, FACE + 3, 2),
        (lx, 1, CORNER, 7), (lx, 2, CORNER + 1, 6),
        (ux, 1, CORNER + 2, 5), (ux, 2, CORNER + 3, 4),
    ):
        field[meta[at]] += ref[k].astype(F32) * meta[VALID + neighbour].astype(F32)


def fifth_kernel(
    meta, got, own_in, lx, ux, ly, uy, xh_one, constants, weight_far,
    dz_out, own, y_low, y_up, x_faces, consts, weight, field, spread, moved, acc, sem,
):
    fetch = pltpu.make_async_copy(weight_far, weight, sem)
    fetch.start()
    total, cross = read_sums(got)
    consts[...] = constants[...]
    consts[CROSS[0]] = cross
    consts[TOTAL[0]] = total
    field[...] = own_in[...].reshape(NB, 64, C)
    add_returned(meta, field, lx, ux, ly, uy)
    occupied = occupied_rows(meta)
    xh = xh_one[0:NB].reshape(ROWS, C)
    du = field[...].reshape(ROWS, C) * occupied * slope(
        constants[GAIN[0]] * xh + constants[SHIFT[0]]
    )
    dz = norm_back(du, xh, constants, 0, total, cross, occupied)
    dz_out[...] = dz
    fetch.wait()
    convolve_back(meta, dz, weight, spread, moved, acc)
    send_gradients(acc, own, y_low, y_up, x_faces)


def taps_kernel(meta, ext, dz, mine, other, gathered, columns, taps):
    gather_columns(meta, ext, gathered, columns)
    for k in range(TAPS):
        taps[k * C : (k + 1) * C, :] = lax.dot_general(
            columns[:, k * C : (k + 1) * C],
            dz[...],
            (((0,), (0,)), ((), ())),
            preferred_element_type=F32,
        )
    here = meta[CORE_AT] == 0
    mine[30:32] = jnp.zeros((2, CHUNK, C), F32)
    other[30:32] = jnp.zeros((2, CHUNK, C), BF16)
    for c in range(31):
        full = min(CHUNK, HALF - CHUNK * c)
        at = CHUNK * c
        low = taps[at : at + full, :]
        high = taps[HALF + at : HALF + at + full, :]
        mine[c, 0:full, :] = jnp.where(here, low, high)
        other[c, 0:full, :] = jnp.where(here, high, low).astype(BF16)


def second_sum_kernel(mine, received, out):
    out[...] = (mine[...] + received[...].astype(F32)).astype(BF16)


def first_sum_kernel(mine, received, second, out):
    out[0:32] = (mine[...] + received[...].astype(F32)).astype(BF16)
    out[32:64] = second[...]


def total_kernel(consts, pieces, out):
    total = jnp.sum(pieces[...].astype(F32), axis=0) / jnp.sqrt(consts[VOXELS])
    out[...] = jnp.broadcast_to(total.astype(BF16)[None], (64, CHUNK, C))


def last_kernel(meta, own, lx, ux, ly, uy, dv, consts, grad_in, norm_grads, field):
    field[...] = own[...].reshape(NB, 64, C)
    add_returned(meta, field, lx, ux, ly, uy)
    total = (dv[...] + field[...].reshape(ROWS, C)) * occupied_rows(meta)
    grad_in[...] = total.astype(BF16)
    root = jnp.sqrt(consts[VOXELS])
    for row, at in enumerate((CROSS[0], TOTAL[0], CROSS[1], TOTAL[1])):
        norm_grads[row : row + 1] = consts[at] / root


def widen_kernel(core, half, *refs):
    out = refs[-1]
    for c in range(31):
        full = min(CHUNK, HALF - CHUNK * c)
        out[0, 0, CHUNK * c : CHUNK * c + full, :] = half[c].astype(F32)[0:full]


def local(kernel, outs, ins, scratch=(), far=()):
    vmem = pl.BlockSpec(memory_space=pltpu.VMEM)
    smem = pl.BlockSpec(memory_space=pltpu.SMEM)
    hbm = pl.BlockSpec(memory_space=pltpu.HBM)
    specs = [hbm if n in far else smem if a.ndim == 1 else vmem for n, a in enumerate(ins)]
    ins = [
        pltpu.with_memory_space_constraint(a, pltpu.HBM) if n in far else a
        for n, a in enumerate(ins)
    ]
    return pl.pallas_call(
        kernel,
        out_shape=[jax.ShapeDtypeStruct(s, d) for s, d in outs],
        in_specs=specs,
        out_specs=[vmem] * len(outs),
        scratch_shapes=[pltpu.VMEM(*s) if isinstance(s, tuple) else s for s in scratch],
        compiler_params=pltpu.CompilerParams(vmem_limit_bytes=VMEM_BYTES),
    )(*ins)


def widen(core, half, partner, before):
    def place(conv, core):
        return conv, 1 - core[0] if partner else core[0], 0, 0

    held = [] if before is None else [before]
    return pl.pallas_call(
        widen_kernel,
        out_shape=jax.ShapeDtypeStruct((2, 2, HALF, C), F32),
        grid_spec=pltpu.PrefetchScalarGridSpec(
            num_scalar_prefetch=1,
            grid=(2,),
            in_specs=[pl.BlockSpec((32, CHUNK, C), lambda conv, core: (conv, 0, 0))]
            + [pl.BlockSpec(memory_space=pl.ANY)] * len(held),
            out_specs=pl.BlockSpec((1, 1, HALF, C), place),
        ),
        input_output_aliases={2: 0} if held else {},
        compiler_params=pltpu.CompilerParams(vmem_limit_bytes=VMEM_BYTES),
        name="widen_kernel",
    )(core, half, *held)


def shifted(value, axis, by):
    length = lax.axis_size(axis)
    return lax.ppermute(value, axis, [(i, (i + by) % length) for i in range(length)])


def exchange(value, axes):
    return lax.all_to_all(value, axes, 0, 0, tiled=True)


def swap(value):
    return lax.ppermute(value, CORE, [(0, 1), (1, 0)])


def join(faces, first, second):
    outs = [(first.shape, first.dtype)] * 2
    return local(join_kernel, outs, [faces, first, second])


def pair(first, second, axis, by):
    return shifted(first, axis, by), shifted(second, axis, -by)


def outward(x_up, x_low, y_faces):
    ux, lx = pair(x_up, x_low, GX, 1)
    up, low = join(y_faces, ux, lx)
    uy, ly = pair(up, low, GY, 1)
    return ux, lx, uy, ly


def homeward(y_low, y_up, x_faces):
    ly, uy = pair(y_low, y_up, GY, -1)
    low, up = join(x_faces, ly, uy)
    lx, ux = pair(low, up, GX, -1)
    return lx, ux, ly, uy


def program(
    voxel_feats,
    w_first,
    w_second,
    norm_gain,
    norm_shift,
    grad_out,
    brick_count,
    kernel_map,
    face_send,
    corner_send,
):
    lists = jnp.concatenate([face_send.reshape(4), corner_send.reshape(4)])
    i = lax.axis_index(GX)
    j = lax.axis_index(GY)
    dx = np.array([d[0] for d in NEIGHBOURS], np.int32)
    dy = np.array([d[1] for d in NEIGHBOURS], np.int32)
    inside = (i + dx >= 0) & (i + dx < 8) & (j + dy >= 0) & (j + dy < 16)
    meta = jnp.concatenate(
        [
            kernel_map.reshape(-1),
            brick_count,
            lists,
            inside.astype(jnp.int32),
            lax.axis_index(CORE).reshape(1),
        ]
    )
    norm = jnp.concatenate([norm_gain, norm_shift], axis=0)
    flat_one = w_first.reshape(TAPS * C, C)
    flat_two = w_second.reshape(TAPS * C, C)
    brick = (64, C)
    three, two = (3,) + brick, (2,) + brick
    rows = (ROWS, C)
    sums = ((2 * 128, C), F32)
    ext = ((EXT,) + brick, BF16)
    list_xh = ((EXT - 1,) + brick, F32)
    table = ((16, C), F32)
    sem = pltpu.SemaphoreType.DMA
    weight = ((TAPS * C, C), BF16)
    gathered = ((144, 6 * NB * C), BF16)
    columns = ((ROWS, TAPS * C), BF16)
    forward = [weight, gathered, columns, sem(())]

    *sends, kept = local(
        send_kernel,
        [(three, BF16), (three, BF16), (two, BF16), ((NB,) + brick, BF16)],
        [lists, voxel_feats],
    )
    received = outward(*sends)
    z_one, ext_one, part, *sends = local(
        first_kernel,
        [((NB,) + brick, F32), ext, ((512, C), F32), (three, F32), (three, F32), (two, F32)],
        [meta, kept, *received, flat_one],
        forward,
        far=(6,),
    )
    received = outward(*sends)
    part = exchange(part, GX_GY)
    z_two, ext_two, part, xh_one, consts = local(
        second_kernel,
        [(rows, F32), ext, sums, list_xh, table],
        [meta, part, z_one, *received, norm, flat_two],
        forward,
        far=(8,),
    )
    part = exchange(part, GX_GY)
    out_feats, dv, xh_two, consts, part = local(
        third_kernel,
        [(rows, BF16), (rows, F32), (rows, F32), table, sums],
        [meta, part, consts, z_two, voxel_feats.reshape(rows), grad_out.reshape(rows)],
    )
    part = exchange(part, GX_GY)
    back = [((3, ROWS, 9 * C), F32), gathered, ((EXT,) + brick, F32), sem(())]
    dz_two, own, y_low, y_up, x_faces, part, consts = local(
        fourth_kernel,
        [(rows, BF16), (rows, F32), (three, BF16), (three, BF16), (two, BF16), sums, table],
        [meta, part, dv, xh_two, consts, xh_one, flat_two],
        [weight] + back,
        far=(6,),
    )
    returned = homeward(y_low, y_up, x_faces)
    chunks = (32, CHUNK, C)
    halves = [(chunks, F32), (chunks, BF16)]
    products = [gathered, columns, ((TAPS * C, C), F32)]
    mine, other = local(taps_kernel, halves, [meta, ext_two, dz_two], products)
    (second,) = local(second_sum_kernel, [(chunks, BF16)], [mine, swap(other)])
    part = exchange(part, GX_GY)
    dz_one, own, y_low, y_up, x_faces, consts = local(
        fifth_kernel,
        [(rows, BF16), (rows, F32), (three, BF16), (three, BF16), (two, BF16), table],
        [meta, part, own, *returned, xh_one, consts, flat_one],
        [weight, ((NB,) + brick, F32)] + back,
        far=(9,),
    )
    returned = homeward(y_low, y_up, x_faces)
    mine, other = local(taps_kernel, halves, [meta, ext_one, dz_one], products)
    grad_in, norm_grads = local(
        last_kernel,
        [(rows, BF16), ((4, C), F32)],
        [meta, own, *returned, dv, consts],
        [((NB,) + brick, F32)],
    )
    both = ((64, CHUNK, C), BF16)
    (part,) = local(first_sum_kernel, [both], [mine, swap(other), second])
    (whole,) = local(total_kernel, [both], [consts, exchange(part, CHIPS)])
    whole = exchange(whole, CHIPS)
    partner = swap(whole)
    core = lax.axis_index(CORE).reshape(1)
    weight_grads = widen(core, whole, False, None)
    weight_grads = widen(core, partner, True, weight_grads).reshape(2, TAPS, C, C)
    return (
        out_feats.reshape(NB, 64, C),
        grad_in.reshape(NB, 64, C),
        weight_grads,
        norm_grads,
    )


def solution(mesh):
    split = Mesh(mesh.devices.reshape(2, 4, 4, 2, 2), GX_GY)
    in_specs = (
        P(GX_GY, None, None),
        P(),
        P(),
        P(),
        P(),
        P(GX_GY, None, None),
        P(GX_GY),
        P(GX_GY, None),
        P(GX_GY, None, None),
        P(GX_GY, None, None),
    )
    out_specs = (P(GX_GY, None, None), P(GX_GY, None, None), P(), P())
    return jax.shard_map(program, mesh=split, in_specs=in_specs, out_specs=out_specs, check_vma=False)
```

```python
import functools

import jax
import jax.numpy as jnp
import numpy as np
from jax import lax
from jax.experimental import pallas as pl
from jax.experimental.pallas import tpu as pltpu
from jax.sharding import Mesh
from jax.sharding import PartitionSpec as P

GX = ("gx_0", "gx_1")
GY = ("gy_0", "gy_1", "gy_2")
GX_GY = ("gx_0", "gx_1", "gy_0", "gy_1", "gy_2")
CORE = ("gy_2",)
CHIPS = ("gx_0", "gx_1", "gy_0", "gy_1")
C = 128
NB = 4
ROWS = NB * 64
TAPS = 27
EXT = 13
EPSILON = 1e-05
F32 = jnp.float32
BF16 = jnp.bfloat16
COUNT, FACE, CORNER, VALID, CORE_AT = 108, 109, 113, 117, 125
NEIGHBOURS = ((-1, 0), (1, 0), (0, -1), (0, 1), (-1, -1), (-1, 1), (1, -1), (1, 1))
CHUNK = 56
HALF = TAPS * C // 2
VMEM_BYTES = 16 << 20


def row_of(k):
    return slice(k, k + 1)


VOXELS = row_of(0)
RECIP = (row_of(1), row_of(2))
NORM_ROWS = slice(4, 8)
GAIN = (row_of(4), row_of(5))
SHIFT = (row_of(6), row_of(7))
CROSS = (row_of(8), row_of(9))
TOTAL = (row_of(10), row_of(11))


def shift_matrix(flipped):
    def places(axis):
        at = lax.broadcasted_iota(jnp.int32, (144, 144), axis)
        major = (at >= 48).astype(jnp.int32) + (at >= 96).astype(jnp.int32)
        minor = (at >> 4) - 3 * major
        return major, minor, (at >> 2) & 3, at & 3

    b, c, q, r = places(1 if flipped else 0)
    ob, oc, qs, rs = places(0 if flipped else 1)
    hit = (4 * ob + qs == q + b + 3) & (4 * oc + rs == r + c + 3)
    return hit.astype(F32).astype(BF16)


def sources():
    return [(0, 0, 3), (1, 1, 0), (2, 1, 1), (3, 1, 2), (4, 1, 3), (5, 2, 0)]


def sigmoid(v):
    return 1.0 / (1.0 + jnp.exp(-v))


def slope(v):
    s = sigmoid(v)
    return s * (1.0 + v * (1.0 - s))


def occupied_rows(meta):
    brick = lax.broadcasted_iota(jnp.int32, (ROWS, C), 0) // 64
    return (brick < meta[COUNT]).astype(F32)


def gather_columns(meta, ext, gathered, columns):
    shift = shift_matrix(False)
    for b in range(NB):
        for plane, oa, source in sources():
            for d in range(9):
                entry = meta[27 * b + 9 * oa + d]
                gathered[16 * d : 16 * d + 16, (6 * b + plane) * C : (6 * b + plane + 1) * C] = ext[
                    entry, 16 * source : 16 * source + 16, :
                ]
    for b in range(NB):
        moved = jnp.dot(
            shift, gathered[:, 6 * b * C : 6 * (b + 1) * C], preferred_element_type=F32
        ).astype(BF16)
        for a in range(3):
            for p in range(4):
                for d in range(9):
                    k = 9 * a + d
                    columns[64 * b + 16 * p : 64 * b + 16 * p + 16, k * C : (k + 1) * C] = moved[
                        16 * d : 16 * d + 16, (p + a) * C : (p + a + 1) * C
                    ]


def convolve(columns, weight):
    return jnp.dot(columns[...], weight[...], preferred_element_type=F32)


def convolve_back(meta, dz, weight, spread, moved, acc):
    shift_back = shift_matrix(True)
    for a in range(3):
        spread[a] = lax.dot_general(
            dz,
            weight[9 * a * C : 9 * (a + 1) * C, :],
            (((1,), (1,)), ((), ())),
            preferred_element_type=F32,
        )
    acc[...] = jnp.zeros_like(acc)
    for b in range(NB):
        for plane in range(6):
            taps = [a for a in range(3) if 0 <= plane - a < 4]
            for d in range(9):
                total = None
                for a in taps:
                    row = 64 * b + 16 * (plane - a)
                    piece = spread[a, row : row + 16, d * C : (d + 1) * C]
                    total = piece if total is None else total + piece
                moved[16 * d : 16 * d + 16, (6 * b + plane) * C : (6 * b + plane + 1) * C] = (
                    total.astype(BF16)
                )
    for b in range(NB):
        home = jnp.dot(
            shift_back, moved[:, 6 * b * C : 6 * (b + 1) * C], preferred_element_type=F32
        )
        for plane, oa, source in sources():
            for d in range(9):
                entry = meta[27 * b + 9 * oa + d]
                acc[entry, 16 * source : 16 * source + 16, :] += home[
                    16 * d : 16 * d + 16, plane * C : (plane + 1) * C
                ]


def write_sums(out, first, second):
    odd = lax.broadcasted_iota(jnp.int32, (8, C), 0) % 2
    both = jnp.where(odd == 0, jnp.broadcast_to(first, (8, C)), jnp.broadcast_to(second, (8, C)))
    out[...] = jnp.broadcast_to(both[None], (out.shape[0] // 8, 8, C)).reshape(out.shape)


def read_sums(got):
    total = jnp.sum(got[...].reshape(got.shape[0] // 8, 8, C), axis=0)
    odd = lax.broadcasted_iota(jnp.int32, (8, C), 0) % 2
    first = jnp.sum(jnp.where(odd == 0, total, 0.0), axis=0, keepdims=True)
    second = jnp.sum(jnp.where(odd == 1, total, 0.0), axis=0, keepdims=True)
    return first, second


def rows_sum(v):
    return jnp.sum(v, axis=0, keepdims=True)


def statistics(total, squares, voxels):
    center = total / voxels
    spread_sq = squares / voxels - center * center
    return center, lax.rsqrt(spread_sq + EPSILON)


def received_bricks(ux, lx, uy, ly):
    return (
        ux.at[0], lx.at[0], uy.at[0], ly.at[0], ux.at[1], ux.at[2], lx.at[1], lx.at[2]
    )


def sends_of(face, corner, y_up, y_low, x_faces):
    return (
        (face(2), y_up.at[0]), (corner(0), y_up.at[1]), (corner(2), y_up.at[2]),
        (face(3), y_low.at[0]), (corner(1), y_low.at[1]), (corner(3), y_low.at[2]),
        (face(0), x_faces.at[0]), (face(1), x_faces.at[1]),
    )


def select_sends(meta, field, y_up, y_low, x_faces):
    for entry, out in sends_of(
        lambda k: meta[FACE + k], lambda k: meta[CORNER + k], y_up, y_low, x_faces
    ):
        out[...] = field[entry]


def send_kernel(lists, field, y_up, y_low, x_faces, kept):
    kept[...] = field[...]
    for entry, out in sends_of(lambda k: lists[k], lambda k: lists[4 + k], y_up, y_low, x_faces):
        out[...] = field[entry]


def fetch_one_kernel(far, out, sem):
    copy = pltpu.make_async_copy(far, out, sem)
    copy.start()
    copy.wait()


def fetch_two_kernel(far, out, sem):
    copy = pltpu.make_async_copy(far, out, sem)
    copy.start()
    copy.wait()


def join_kernel(faces, first, second, up, low):
    up[0] = faces[0]
    up[1] = first[1]
    up[2] = second[1]
    low[0] = faces[1]
    low[1] = first[2]
    low[2] = second[2]


def first_kernel(
    meta, voxel_feats, ux, lx, uy, ly, weight,
    z_out, ext, sums, y_up, y_low, x_faces, gathered, columns,
):
    ext[NB + 8] = jnp.zeros((64, C), BF16)
    for b in range(NB):
        keep = (meta[COUNT] > b).astype(F32)
        ext[b] = (voxel_feats[b].astype(F32) * keep).astype(BF16)
    for e, brick in enumerate(received_bricks(ux, lx, uy, ly)):
        keep = meta[VALID + e].astype(F32)
        ext[NB + e] = (brick[...].astype(F32) * keep).astype(BF16)
    gather_columns(meta, ext, gathered, columns)
    z = convolve(columns, weight)
    z_out[...] = z.reshape(NB, 64, C)
    select_sends(meta, z_out, y_up, y_low, x_faces)
    masked = z * occupied_rows(meta)
    row = lax.broadcasted_iota(jnp.int32, (8, C), 0) % 4
    count = (64 * meta[COUNT]).astype(F32)
    part = jnp.where(
        row == 0, rows_sum(masked), jnp.where(row == 1, rows_sum(z * masked), count)
    )
    sums[...] = jnp.broadcast_to(part[None], (64, 8, C)).reshape(512, C)


def second_kernel(
    meta, got, z_one, ux, lx, uy, ly, norm, weight,
    z_out, ext, sums, xh_out, consts, gathered, columns,
):
    row = lax.broadcasted_iota(jnp.int32, (8, C), 0) % 4
    both = jnp.sum(got[...].reshape(64, 8, C), axis=0)
    total = rows_sum(jnp.where(row == 0, both, 0.0))
    squares = rows_sum(jnp.where(row == 1, both, 0.0))
    voxels = rows_sum(jnp.where(row == 2, both, 0.0))
    center, recip = statistics(total, squares, voxels)
    consts[...] = jnp.zeros_like(consts)
    consts[VOXELS] = voxels
    consts[RECIP[0]] = recip
    consts[NORM_ROWS] = norm[...]
    for e in range(EXT - 1):
        keep = meta[COUNT] > e if e < NB else meta[VALID + e - NB] > 0
        field = z_one[e] if e < NB else received_bricks(ux, lx, uy, ly)[e - NB][...]
        xh = (field - center) * recip
        xh_out[e] = xh
        u = norm[0:1] * xh + norm[2:3]
        ext[e] = (u * sigmoid(u) * keep.astype(F32)).astype(BF16)
    ext[EXT - 1] = jnp.zeros((64, C), BF16)
    gather_columns(meta, ext, gathered, columns)
    z = convolve(columns, weight)
    z_out[...] = z
    masked = z * occupied_rows(meta)
    write_sums(sums, rows_sum(masked), rows_sum(z * masked))


def third_kernel(
    meta, got, constants, z_two, voxel_feats, grad_out, out_feats, dv_out, xh_out, consts, sums
):
    total, squares = read_sums(got)
    center, recip = statistics(total, squares, constants[VOXELS])
    consts[...] = constants[...]
    consts[RECIP[1]] = recip
    occupied = occupied_rows(meta)
    xh = (z_two[...] - center) * recip
    xh_out[...] = xh
    feats = voxel_feats[...].astype(F32) * occupied
    pre = constants[GAIN[1]] * xh + constants[SHIFT[1]] + feats
    s = sigmoid(pre)
    out_feats[...] = (pre * s * occupied).astype(BF16)
    dv = grad_out[...].astype(F32) * occupied * (s * (1.0 + pre * (1.0 - s)))
    dv_out[...] = dv
    write_sums(sums, rows_sum(dv), rows_sum(dv * xh))


def norm_back(dv, xh, consts, number, total, cross, occupied):
    voxels = consts[VOXELS]
    scale = occupied * consts[GAIN[number]] * consts[RECIP[number]]
    return (scale * (dv - total / voxels - xh * cross / voxels)).astype(BF16)


def send_gradients(acc, own, y_low, y_up, x_faces):
    own[...] = acc[0:NB].reshape(ROWS, C)
    y_low[0] = acc[NB + 2].astype(BF16)
    y_low[1] = acc[NB + 4].astype(BF16)
    y_low[2] = acc[NB + 6].astype(BF16)
    y_up[0] = acc[NB + 3].astype(BF16)
    y_up[1] = acc[NB + 5].astype(BF16)
    y_up[2] = acc[NB + 7].astype(BF16)
    x_faces[0] = acc[NB].astype(BF16)
    x_faces[1] = acc[NB + 1].astype(BF16)


def fourth_kernel(
    meta, got, dv, xh_two, constants, xh_one, weight,
    dz_out, own, y_low, y_up, x_faces, sums, consts, spread, moved, acc,
):
    total, cross = read_sums(got)
    consts[...] = constants[...]
    consts[CROSS[1]] = cross
    consts[TOTAL[1]] = total
    dz = norm_back(dv[...], xh_two[...], constants, 1, total, cross, occupied_rows(meta))
    dz_out[...] = dz
    convolve_back(meta, dz, weight, spread, moved, acc)
    send_gradients(acc, own, y_low, y_up, x_faces)
    first = jnp.zeros((64, C), F32)
    second = jnp.zeros((64, C), F32)
    for e in range(EXT - 1):
        keep = meta[COUNT] > e if e < NB else meta[VALID + e - NB] > 0
        xh = xh_one[e]
        du = acc[e] * slope(constants[GAIN[0]] * xh + constants[SHIFT[0]]) * keep.astype(F32)
        first += du
        second += du * xh
    write_sums(sums, rows_sum(first), rows_sum(second))


def add_returned(meta, field, lx, ux, ly, uy):
    for ref, k, at, neighbour in (
        (lx, 0, FACE, 1), (ux, 0, FACE + 1, 0), (ly, 0, FACE + 2, 3), (uy, 0, FACE + 3, 2),
        (lx, 1, CORNER, 7), (lx, 2, CORNER + 1, 6),
        (ux, 1, CORNER + 2, 5), (ux, 2, CORNER + 3, 4),
    ):
        field[meta[at]] += ref[k].astype(F32) * meta[VALID + neighbour].astype(F32)


def fifth_kernel(
    meta, got, own_in, lx, ux, ly, uy, xh_one, constants, weight_far,
    dz_out, own, y_low, y_up, x_faces, consts, weight, sem, field, spread, moved, acc,
):
    fetch = pltpu.make_async_copy(weight_far, weight, sem)
    fetch.start()
    total, cross = read_sums(got)
    consts[...] = constants[...]
    consts[CROSS[0]] = cross
    consts[TOTAL[0]] = total
    field[...] = own_in[...].reshape(NB, 64, C)
    add_returned(meta, field, lx, ux, ly, uy)
    occupied = occupied_rows(meta)
    xh = xh_one[0:NB].reshape(ROWS, C)
    du = field[...].reshape(ROWS, C) * occupied * slope(
        constants[GAIN[0]] * xh + constants[SHIFT[0]]
    )
    dz = norm_back(du, xh, constants, 0, total, cross, occupied)
    dz_out[...] = dz
    fetch.wait()
    convolve_back(meta, dz, weight, spread, moved, acc)
    send_gradients(acc, own, y_low, y_up, x_faces)


def taps_kernel(meta, ext, dz, mine, other, gathered, columns, taps):
    gather_columns(meta, ext, gathered, columns)
    for k in range(TAPS):
        taps[k * C : (k + 1) * C, :] = lax.dot_general(
            columns[:, k * C : (k + 1) * C],
            dz[...],
            (((0,), (0,)), ((), ())),
            preferred_element_type=F32,
        )
    here = meta[CORE_AT] == 0
    mine[30:32] = jnp.zeros((2, CHUNK, C), F32)
    other[30:32] = jnp.zeros((2, CHUNK, C), BF16)
    for c in range(31):
        full = min(CHUNK, HALF - CHUNK * c)
        at = CHUNK * c
        low = taps[at : at + full, :]
        high = taps[HALF + at : HALF + at + full, :]
        mine[c, 0:full, :] = jnp.where(here, low, high)
        other[c, 0:full, :] = jnp.where(here, high, low).astype(BF16)


def second_sum_kernel(mine, received, out):
    out[...] = (mine[...] + received[...].astype(F32)).astype(BF16)


def first_sum_kernel(mine, received, second, out):
    out[0:32] = (mine[...] + received[...].astype(F32)).astype(BF16)
    out[32:64] = second[...]


def total_kernel(consts, pieces, out):
    total = jnp.sum(pieces[...].astype(F32), axis=0) / jnp.sqrt(consts[VOXELS])
    out[...] = jnp.broadcast_to(total.astype(BF16)[None], (64, CHUNK, C))


def last_kernel(meta, own, lx, ux, ly, uy, dv, consts, grad_in, norm_grads, field):
    field[...] = own[...].reshape(NB, 64, C)
    add_returned(meta, field, lx, ux, ly, uy)
    total = (dv[...] + field[...].reshape(ROWS, C)) * occupied_rows(meta)
    grad_in[...] = total.astype(BF16)
    root = jnp.sqrt(consts[VOXELS])
    for row, at in enumerate((CROSS[0], TOTAL[0], CROSS[1], TOTAL[1])):
        norm_grads[row : row + 1] = consts[at] / root


def widen_kernel(core, half, *refs, partner):
    out, wide, sems = refs[-3:]
    at = 1 - core[0] if partner else core[0]
    copies = []
    for conv in range(2):
        for piece in range(4):
            for c in range(8 * piece, min(8 * piece + 8, 31)):
                full = min(CHUNK, HALF - CHUNK * c)
                wide[conv, CHUNK * c : CHUNK * c + full, :] = half[32 * conv + c].astype(F32)[
                    0:full
                ]
            first = 8 * CHUNK * piece
            rows = pl.ds(first, min(8 * CHUNK, HALF - first))
            copies.append(
                pltpu.make_async_copy(
                    wide.at[conv, rows], out.at[conv, at, rows], sems.at[4 * conv + piece]
                )
            )
            copies[-1].start()
    for copy in copies:
        copy.wait()


def local(kernel, outs, ins, scratch=(), far=()):
    vmem = pl.BlockSpec(memory_space=pltpu.VMEM)
    smem = pl.BlockSpec(memory_space=pltpu.SMEM)
    hbm = pl.BlockSpec(memory_space=pltpu.HBM)
    specs = [hbm if n in far else smem if a.ndim == 1 else vmem for n, a in enumerate(ins)]
    ins = [
        pltpu.with_memory_space_constraint(a, pltpu.HBM) if n in far else a
        for n, a in enumerate(ins)
    ]
    return pl.pallas_call(
        kernel,
        out_shape=[jax.ShapeDtypeStruct(s, d) for s, d in outs],
        in_specs=specs,
        out_specs=[vmem] * len(outs),
        scratch_shapes=[pltpu.VMEM(*s) if isinstance(s, tuple) else s for s in scratch],
        compiler_params=pltpu.CompilerParams(vmem_limit_bytes=VMEM_BYTES),
    )(*ins)


def widen(core, half, partner, before):
    held = [] if before is None else [before]
    far = pl.BlockSpec(memory_space=pltpu.HBM)
    return pl.pallas_call(
        functools.partial(widen_kernel, partner=partner),
        out_shape=jax.ShapeDtypeStruct((2, 2, HALF, C), F32),
        in_specs=[pl.BlockSpec(memory_space=pltpu.SMEM), pl.BlockSpec(memory_space=pltpu.VMEM)]
        + [far] * len(held),
        out_specs=far,
        scratch_shapes=[pltpu.VMEM((2, HALF, C), F32), pltpu.SemaphoreType.DMA((8,))],
        input_output_aliases={2: 0} if held else {},
        compiler_params=pltpu.CompilerParams(vmem_limit_bytes=VMEM_BYTES),
        name="widen_kernel",
    )(core, half, *held)


def shifted(value, axis, by):
    length = lax.axis_size(axis)
    return lax.ppermute(value, axis, [(i, (i + by) % length) for i in range(length)])


def exchange(value, axes):
    return lax.all_to_all(value, axes, 0, 0, tiled=True)


def swap(value):
    return lax.ppermute(value, CORE, [(0, 1), (1, 0)])


def join(faces, first, second):
    outs = [(first.shape, first.dtype)] * 2
    return local(join_kernel, outs, [faces, first, second])


def pair(first, second, axis, by):
    return shifted(first, axis, by), shifted(second, axis, -by)


def outward(y_up, y_low, x_faces):
    uy, ly = pair(y_up, y_low, GY, 1)
    up, low = join(x_faces, uy, ly)
    ux, lx = pair(up, low, GX, 1)
    return ux, lx, uy, ly


def homeward(y_low, y_up, x_faces):
    ly, uy = pair(y_low, y_up, GY, -1)
    low, up = join(x_faces, ly, uy)
    lx, ux = pair(low, up, GX, -1)
    return lx, ux, ly, uy


def program(
    voxel_feats,
    w_first,
    w_second,
    norm_gain,
    norm_shift,
    grad_out,
    brick_count,
    kernel_map,
    face_send,
    corner_send,
):
    lists = jnp.concatenate([face_send.reshape(4), corner_send.reshape(4)])
    i = lax.axis_index(GX)
    j = lax.axis_index(GY)
    dx = np.array([d[0] for d in NEIGHBOURS], np.int32)
    dy = np.array([d[1] for d in NEIGHBOURS], np.int32)
    inside = (i + dx >= 0) & (i + dx < 8) & (j + dy >= 0) & (j + dy < 16)
    meta = jnp.concatenate(
        [
            kernel_map.reshape(-1),
            brick_count,
            lists,
            inside.astype(jnp.int32),
            lax.axis_index(CORE).reshape(1),
        ]
    )
    norm = jnp.concatenate([norm_gain, norm_shift], axis=0)
    flat_one = w_first.reshape(TAPS * C, C)
    flat_two = w_second.reshape(TAPS * C, C)
    brick = (64, C)
    three, two = (3,) + brick, (2,) + brick
    rows = (ROWS, C)
    sums = ((2 * 128, C), F32)
    ext = ((EXT,) + brick, BF16)
    list_xh = ((EXT - 1,) + brick, F32)
    table = ((16, C), F32)
    sem = pltpu.SemaphoreType.DMA
    weight = ((TAPS * C, C), BF16)
    gathered = ((144, 6 * NB * C), BF16)
    columns = ((ROWS, TAPS * C), BF16)
    forward = [gathered, columns]

    *sends, kept = local(
        send_kernel,
        [(three, BF16), (three, BF16), (two, BF16), ((NB,) + brick, BF16)],
        [lists, voxel_feats],
    )
    (near_one,) = local(fetch_one_kernel, [weight], [flat_one], [sem(())], far=(0,))
    (near_two,) = local(fetch_two_kernel, [weight], [flat_two], [sem(())], far=(0,))
    received = outward(*sends)
    z_one, ext_one, part, *sends = local(
        first_kernel,
        [((NB,) + brick, F32), ext, ((512, C), F32), (three, F32), (three, F32), (two, F32)],
        [meta, kept, *received, near_one],
        forward,
    )
    received = outward(*sends)
    part = exchange(part, GX_GY)
    z_two, ext_two, part, xh_one, consts = local(
        second_kernel,
        [(rows, F32), ext, sums, list_xh, table],
        [meta, part, z_one, *received, norm, near_two],
        forward,
    )
    part = exchange(part, GX_GY)
    out_feats, dv, xh_two, consts, part = local(
        third_kernel,
        [(rows, BF16), (rows, F32), (rows, F32), table, sums],
        [meta, part, consts, z_two, voxel_feats.reshape(rows), grad_out.reshape(rows)],
    )
    part = exchange(part, GX_GY)
    back = [((3, ROWS, 9 * C), F32), gathered, ((EXT,) + brick, F32)]
    dz_two, own, y_low, y_up, x_faces, part, consts = local(
        fourth_kernel,
        [(rows, BF16), (rows, F32), (three, BF16), (three, BF16), (two, BF16), sums, table],
        [meta, part, dv, xh_two, consts, xh_one, near_two],
        back,
    )
    returned = homeward(y_low, y_up, x_faces)
    chunks = (32, CHUNK, C)
    halves = [(chunks, F32), (chunks, BF16)]
    products = [gathered, columns, ((TAPS * C, C), F32)]
    mine, other = local(taps_kernel, halves, [meta, ext_two, dz_two], products)
    (second,) = local(second_sum_kernel, [(chunks, BF16)], [mine, swap(other)])
    part = exchange(part, GX_GY)
    dz_one, own, y_low, y_up, x_faces, consts = local(
        fifth_kernel,
        [(rows, BF16), (rows, F32), (three, BF16), (three, BF16), (two, BF16), table],
        [meta, part, own, *returned, xh_one, consts, flat_one],
        [weight, sem(()), ((NB,) + brick, F32)] + back,
        far=(9,),
    )
    returned = homeward(y_low, y_up, x_faces)
    mine, other = local(taps_kernel, halves, [meta, ext_one, dz_one], products)
    grad_in, norm_grads = local(
        last_kernel,
        [(rows, BF16), ((4, C), F32)],
        [meta, own, *returned, dv, consts],
        [((NB,) + brick, F32)],
    )
    both = ((64, CHUNK, C), BF16)
    (part,) = local(first_sum_kernel, [both], [mine, swap(other), second])
    (whole,) = local(total_kernel, [both], [consts, exchange(part, CHIPS)])
    whole = exchange(whole, CHIPS)
    partner = swap(whole)
    core = lax.axis_index(CORE).reshape(1)
    weight_grads = widen(core, whole, False, None)
    weight_grads = widen(core, partner, True, weight_grads).reshape(2, TAPS, C, C)
    return (
        out_feats.reshape(NB, 64, C),
        grad_in.reshape(NB, 64, C),
        weight_grads,
        norm_grads,
    )


def solution(mesh):
    split = Mesh(mesh.devices.reshape(2, 4, 4, 2, 2), GX_GY)
    in_specs = (
        P(GX_GY, None, None),
        P(),
        P(),
        P(),
        P(),
        P(GX_GY, None, None),
        P(GX_GY),
        P(GX_GY, None),
        P(GX_GY, None, None),
        P(GX_GY, None, None),
    )
    out_specs = (P(GX_GY, None, None), P(GX_GY, None, None), P(), P())
    return jax.shard_map(program, mesh=split, in_specs=in_specs, out_specs=out_specs, check_vma=False)
```

```python
import functools

import jax
import jax.numpy as jnp
import numpy as np
from jax import lax
from jax.experimental import pallas as pl
from jax.experimental.pallas import tpu as pltpu
from jax.sharding import Mesh
from jax.sharding import PartitionSpec as P

GX = ("gx_0", "gx_1")
GY = ("gy_0", "gy_1", "gy_2")
GX_GY = ("gx_0", "gx_1", "gy_0", "gy_1", "gy_2")
CORE = ("gy_2",)
CHIPS = ("gx_0", "gx_1", "gy_0", "gy_1")
C = 128
NB = 4
ROWS = NB * 64
TAPS = 27
EXT = 13
EPSILON = 1e-05
F32 = jnp.float32
BF16 = jnp.bfloat16
COUNT, FACE, CORNER, VALID, CORE_AT = 108, 109, 113, 117, 125
NEIGHBOURS = ((-1, 0), (1, 0), (0, -1), (0, 1), (-1, -1), (-1, 1), (1, -1), (1, 1))
CHUNK = 56
HALF = TAPS * C // 2
VMEM_BYTES = 16 << 20


def row_of(k):
    return slice(k, k + 1)


VOXELS = row_of(0)
RECIP = (row_of(1), row_of(2))
NORM_ROWS = slice(4, 8)
GAIN = (row_of(4), row_of(5))
SHIFT = (row_of(6), row_of(7))
CROSS = (row_of(8), row_of(9))
TOTAL = (row_of(10), row_of(11))


def shift_matrix(flipped):
    def places(axis):
        at = lax.broadcasted_iota(jnp.int32, (144, 144), axis)
        major = (at >= 48).astype(jnp.int32) + (at >= 96).astype(jnp.int32)
        minor = (at >> 4) - 3 * major
        return major, minor, (at >> 2) & 3, at & 3

    b, c, q, r = places(1 if flipped else 0)
    ob, oc, qs, rs = places(0 if flipped else 1)
    hit = (4 * ob + qs == q + b + 3) & (4 * oc + rs == r + c + 3)
    return hit.astype(F32).astype(BF16)


def sources():
    return [(0, 0, 3), (1, 1, 0), (2, 1, 1), (3, 1, 2), (4, 1, 3), (5, 2, 0)]


def sigmoid(v):
    return 1.0 / (1.0 + jnp.exp(-v))


def slope(v):
    s = sigmoid(v)
    return s * (1.0 + v * (1.0 - s))


def occupied_rows(meta):
    brick = lax.broadcasted_iota(jnp.int32, (ROWS, C), 0) // 64
    return (brick < meta[COUNT]).astype(F32)


def shifted_planes(meta, ext, gathered, planes):
    shift = shift_matrix(False)
    for b in range(NB):
        for plane, oa, source in sources():
            for d in range(9):
                entry = meta[27 * b + 9 * oa + d]
                gathered[16 * d : 16 * d + 16, (6 * b + plane) * C : (6 * b + plane + 1) * C] = ext[
                    entry, 16 * source : 16 * source + 16, :
                ]
    for b in range(NB):
        at = slice(6 * b * C, 6 * (b + 1) * C)
        planes[:, at] = jnp.dot(shift, gathered[:, at], preferred_element_type=F32).astype(BF16)


def patches(planes, k):
    a, d = divmod(k, 9)
    tiles = [
        planes[16 * d : 16 * d + 16, (6 * b + p + a) * C : (6 * b + p + a + 1) * C]
        for b in range(NB)
        for p in range(4)
    ]
    return jnp.concatenate(tiles, axis=0)


def convolve(planes, weight):
    total = jnp.zeros((ROWS, C), F32)
    for k in range(0, TAPS, 2):
        taps = range(k, min(k + 2, TAPS))
        columns = jnp.concatenate([patches(planes, tap) for tap in taps], axis=1)
        total += jnp.dot(
            columns, weight[k * C : (k + len(taps)) * C, :], preferred_element_type=F32
        )
    return total


def convolve_back(meta, dz, weight, spread, moved, acc):
    shift_back = shift_matrix(True)
    for a in range(3):
        spread[a] = lax.dot_general(
            dz,
            weight[9 * a * C : 9 * (a + 1) * C, :],
            (((1,), (1,)), ((), ())),
            preferred_element_type=F32,
        )
    acc[...] = jnp.zeros_like(acc)
    for b in range(NB):
        for plane in range(6):
            taps = [a for a in range(3) if 0 <= plane - a < 4]
            for d in range(9):
                total = None
                for a in taps:
                    row = 64 * b + 16 * (plane - a)
                    piece = spread[a, row : row + 16, d * C : (d + 1) * C]
                    total = piece if total is None else total + piece
                moved[16 * d : 16 * d + 16, (6 * b + plane) * C : (6 * b + plane + 1) * C] = (
                    total.astype(BF16)
                )
    for b in range(NB):
        home = jnp.dot(
            shift_back, moved[:, 6 * b * C : 6 * (b + 1) * C], preferred_element_type=F32
        )
        for plane, oa, source in sources():
            for d in range(9):
                entry = meta[27 * b + 9 * oa + d]
                acc[entry, 16 * source : 16 * source + 16, :] += home[
                    16 * d : 16 * d + 16, plane * C : (plane + 1) * C
                ]


def write_sums(out, first, second):
    odd = lax.broadcasted_iota(jnp.int32, (8, C), 0) % 2
    both = jnp.where(odd == 0, jnp.broadcast_to(first, (8, C)), jnp.broadcast_to(second, (8, C)))
    out[...] = jnp.broadcast_to(both[None], (out.shape[0] // 8, 8, C)).reshape(out.shape)


def read_sums(got):
    total = jnp.sum(got[...].reshape(got.shape[0] // 8, 8, C), axis=0)
    odd = lax.broadcasted_iota(jnp.int32, (8, C), 0) % 2
    first = jnp.sum(jnp.where(odd == 0, total, 0.0), axis=0, keepdims=True)
    second = jnp.sum(jnp.where(odd == 1, total, 0.0), axis=0, keepdims=True)
    return first, second


def rows_sum(v):
    return jnp.sum(v, axis=0, keepdims=True)


def statistics(total, squares, voxels):
    center = total / voxels
    spread_sq = squares / voxels - center * center
    return center, lax.rsqrt(spread_sq + EPSILON)


def received_bricks(ux, lx, uy, ly):
    return (
        ux.at[0], lx.at[0], uy.at[0], ly.at[0], ux.at[1], ux.at[2], lx.at[1], lx.at[2]
    )


def sends_of(face, corner, y_up, y_low, x_faces):
    return (
        (face(2), y_up.at[0]), (corner(0), y_up.at[1]), (corner(2), y_up.at[2]),
        (face(3), y_low.at[0]), (corner(1), y_low.at[1]), (corner(3), y_low.at[2]),
        (face(0), x_faces.at[0]), (face(1), x_faces.at[1]),
    )


def select_sends(meta, field, y_up, y_low, x_faces):
    for entry, out in sends_of(
        lambda k: meta[FACE + k], lambda k: meta[CORNER + k], y_up, y_low, x_faces
    ):
        out[...] = field[entry]


def send_kernel(face_far, corner_far, field, y_up, y_low, x_faces, kept, face, corner, sems):
    copies = [
        pltpu.make_async_copy(field, kept, sems.at[0]),
        pltpu.make_async_copy(face_far, face, sems.at[1]),
        pltpu.make_async_copy(corner_far, corner, sems.at[2]),
    ]
    for copy in copies:
        copy.start()
    for copy in copies:
        copy.wait()
    for entry, out in sends_of(lambda k: face[k], lambda k: corner[k], y_up, y_low, x_faces):
        out[...] = kept[entry]


def fetch_one_kernel(far, out, sem):
    copy = pltpu.make_async_copy(far, out, sem)
    copy.start()
    copy.wait()


def fetch_two_kernel(far, out, sem):
    copy = pltpu.make_async_copy(far, out, sem)
    copy.start()
    copy.wait()


def join_kernel(faces, first, second, up, low):
    up[0] = faces[0]
    up[1] = first[1]
    up[2] = second[1]
    low[0] = faces[1]
    low[1] = first[2]
    low[2] = second[2]


def first_kernel(
    meta, voxel_feats, ux, lx, uy, ly, weight,
    z_out, ext, sums, y_up, y_low, x_faces, gathered, planes,
):
    ext[NB + 8] = jnp.zeros((64, C), BF16)
    for b in range(NB):
        keep = (meta[COUNT] > b).astype(F32)
        ext[b] = (voxel_feats[b].astype(F32) * keep).astype(BF16)
    for e, brick in enumerate(received_bricks(ux, lx, uy, ly)):
        keep = meta[VALID + e].astype(F32)
        ext[NB + e] = (brick[...].astype(F32) * keep).astype(BF16)
    shifted_planes(meta, ext, gathered, planes)
    z = convolve(planes, weight)
    z_out[...] = z.reshape(NB, 64, C)
    select_sends(meta, z_out, y_up, y_low, x_faces)
    masked = z * occupied_rows(meta)
    row = lax.broadcasted_iota(jnp.int32, (8, C), 0) % 4
    count = (64 * meta[COUNT]).astype(F32)
    part = jnp.where(
        row == 0, rows_sum(masked), jnp.where(row == 1, rows_sum(z * masked), count)
    )
    sums[...] = jnp.broadcast_to(part[None], (64, 8, C)).reshape(512, C)


def second_kernel(
    meta, got, z_one, ux, lx, uy, ly, norm, weight,
    z_out, ext, sums, xh_out, consts, gathered, planes,
):
    row = lax.broadcasted_iota(jnp.int32, (8, C), 0) % 4
    both = jnp.sum(got[...].reshape(64, 8, C), axis=0)
    total = rows_sum(jnp.where(row == 0, both, 0.0))
    squares = rows_sum(jnp.where(row == 1, both, 0.0))
    voxels = rows_sum(jnp.where(row == 2, both, 0.0))
    center, recip = statistics(total, squares, voxels)
    consts[...] = jnp.zeros_like(consts)
    consts[VOXELS] = voxels
    consts[RECIP[0]] = recip
    consts[NORM_ROWS] = norm[...]
    for e in range(EXT - 1):
        keep = meta[COUNT] > e if e < NB else meta[VALID + e - NB] > 0
        field = z_one[e] if e < NB else received_bricks(ux, lx, uy, ly)[e - NB][...]
        xh = (field - center) * recip
        xh_out[e] = xh
        u = norm[0:1] * xh + norm[2:3]
        ext[e] = (u * sigmoid(u) * keep.astype(F32)).astype(BF16)
    ext[EXT - 1] = jnp.zeros((64, C), BF16)
    shifted_planes(meta, ext, gathered, planes)
    z = convolve(planes, weight)
    z_out[...] = z
    masked = z * occupied_rows(meta)
    write_sums(sums, rows_sum(masked), rows_sum(z * masked))


def third_kernel(
    meta, got, constants, z_two, voxel_feats, grad_out, out_feats, dv_out, xh_out, consts, sums
):
    total, squares = read_sums(got)
    center, recip = statistics(total, squares, constants[VOXELS])
    consts[...] = constants[...]
    consts[RECIP[1]] = recip
    occupied = occupied_rows(meta)
    xh = (z_two[...] - center) * recip
    xh_out[...] = xh
    feats = voxel_feats[...].astype(F32) * occupied
    pre = constants[GAIN[1]] * xh + constants[SHIFT[1]] + feats
    s = sigmoid(pre)
    out_feats[...] = (pre * s * occupied).astype(BF16)
    dv = grad_out[...].astype(F32) * occupied * (s * (1.0 + pre * (1.0 - s)))
    dv_out[...] = dv
    write_sums(sums, rows_sum(dv), rows_sum(dv * xh))


def norm_back(dv, xh, consts, number, total, cross, occupied):
    voxels = consts[VOXELS]
    scale = occupied * consts[GAIN[number]] * consts[RECIP[number]]
    return (scale * (dv - total / voxels - xh * cross / voxels)).astype(BF16)


def send_gradients(acc, own, y_low, y_up, x_faces):
    own[...] = acc[0:NB].reshape(ROWS, C)
    y_low[0] = acc[NB + 2].astype(BF16)
    y_low[1] = acc[NB + 4].astype(BF16)
    y_low[2] = acc[NB + 6].astype(BF16)
    y_up[0] = acc[NB + 3].astype(BF16)
    y_up[1] = acc[NB + 5].astype(BF16)
    y_up[2] = acc[NB + 7].astype(BF16)
    x_faces[0] = acc[NB].astype(BF16)
    x_faces[1] = acc[NB + 1].astype(BF16)


def fourth_kernel(
    meta, got, dv, xh_two, constants, xh_one, weight,
    dz_out, own, y_low, y_up, x_faces, sums, consts, spread, moved, acc,
):
    total, cross = read_sums(got)
    consts[...] = constants[...]
    consts[CROSS[1]] = cross
    consts[TOTAL[1]] = total
    dz = norm_back(dv[...], xh_two[...], constants, 1, total, cross, occupied_rows(meta))
    dz_out[...] = dz
    convolve_back(meta, dz, weight, spread, moved, acc)
    send_gradients(acc, own, y_low, y_up, x_faces)
    first = jnp.zeros((64, C), F32)
    second = jnp.zeros((64, C), F32)
    for e in range(EXT - 1):
        keep = meta[COUNT] > e if e < NB else meta[VALID + e - NB] > 0
        xh = xh_one[e]
        du = acc[e] * slope(constants[GAIN[0]] * xh + constants[SHIFT[0]]) * keep.astype(F32)
        first += du
        second += du * xh
    write_sums(sums, rows_sum(first), rows_sum(second))


def add_returned(meta, field, lx, ux, ly, uy):
    for ref, k, at, neighbour in (
        (lx, 0, FACE, 1), (ux, 0, FACE + 1, 0), (ly, 0, FACE + 2, 3), (uy, 0, FACE + 3, 2),
        (lx, 1, CORNER, 7), (lx, 2, CORNER + 1, 6),
        (ux, 1, CORNER + 2, 5), (ux, 2, CORNER + 3, 4),
    ):
        field[meta[at]] += ref[k].astype(F32) * meta[VALID + neighbour].astype(F32)


def fifth_kernel(
    meta, got, own_in, lx, ux, ly, uy, xh_one, constants, weight_far,
    dz_out, own, y_low, y_up, x_faces, consts, weight, sem, field, spread, moved, acc,
):
    fetch = pltpu.make_async_copy(weight_far, weight, sem)
    fetch.start()
    total, cross = read_sums(got)
    consts[...] = constants[...]
    consts[CROSS[0]] = cross
    consts[TOTAL[0]] = total
    field[...] = own_in[...].reshape(NB, 64, C)
    add_returned(meta, field, lx, ux, ly, uy)
    occupied = occupied_rows(meta)
    xh = xh_one[0:NB].reshape(ROWS, C)
    du = field[...].reshape(ROWS, C) * occupied * slope(
        constants[GAIN[0]] * xh + constants[SHIFT[0]]
    )
    dz = norm_back(du, xh, constants, 0, total, cross, occupied)
    dz_out[...] = dz
    fetch.wait()
    convolve_back(meta, dz, weight, spread, moved, acc)
    send_gradients(acc, own, y_low, y_up, x_faces)


def taps_kernel(meta, ext, dz, mine, other, gathered, planes, taps):
    shifted_planes(meta, ext, gathered, planes)
    for k in range(TAPS):
        taps[k * C : (k + 1) * C, :] = lax.dot_general(
            patches(planes, k),
            dz[...],
            (((0,), (0,)), ((), ())),
            preferred_element_type=F32,
        )
    here = meta[CORE_AT] == 0
    mine[30:32] = jnp.zeros((2, CHUNK, C), F32)
    other[30:32] = jnp.zeros((2, CHUNK, C), BF16)
    for c in range(31):
        full = min(CHUNK, HALF - CHUNK * c)
        at = CHUNK * c
        low = taps[at : at + full, :]
        high = taps[HALF + at : HALF + at + full, :]
        mine[c, 0:full, :] = jnp.where(here, low, high)
        other[c, 0:full, :] = jnp.where(here, high, low).astype(BF16)


def second_sum_kernel(mine, received, out):
    out[...] = (mine[...] + received[...].astype(F32)).astype(BF16)


def first_sum_kernel(mine, received, second, out):
    out[0:32] = (mine[...] + received[...].astype(F32)).astype(BF16)
    out[32:64] = second[...]


def total_kernel(consts, pieces, out):
    total = jnp.sum(pieces[...].astype(F32), axis=0) / jnp.sqrt(consts[VOXELS])
    out[...] = jnp.broadcast_to(total.astype(BF16)[None], (64, CHUNK, C))


def last_kernel(meta, own, lx, ux, ly, uy, dv, consts, grad_in, norm_grads, field):
    field[...] = own[...].reshape(NB, 64, C)
    add_returned(meta, field, lx, ux, ly, uy)
    total = (dv[...] + field[...].reshape(ROWS, C)) * occupied_rows(meta)
    grad_in[...] = total.astype(BF16)
    root = jnp.sqrt(consts[VOXELS])
    for row, at in enumerate((CROSS[0], TOTAL[0], CROSS[1], TOTAL[1])):
        norm_grads[row : row + 1] = consts[at] / root


def widen_kernel(core, half, *refs, partner):
    out, wide, sems = refs[-3:]
    at = 1 - core[0] if partner else core[0]
    copies = []
    for conv in range(2):
        for piece in range(4):
            for c in range(8 * piece, min(8 * piece + 8, 31)):
                full = min(CHUNK, HALF - CHUNK * c)
                wide[conv, CHUNK * c : CHUNK * c + full, :] = half[32 * conv + c].astype(F32)[
                    0:full
                ]
            first = 8 * CHUNK * piece
            rows = pl.ds(first, min(8 * CHUNK, HALF - first))
            copies.append(
                pltpu.make_async_copy(
                    wide.at[conv, rows], out.at[conv, at, rows], sems.at[4 * conv + piece]
                )
            )
            copies[-1].start()
    for copy in copies:
        copy.wait()


def local(kernel, outs, ins, scratch=(), far=()):
    vmem = pl.BlockSpec(memory_space=pltpu.VMEM)
    smem = pl.BlockSpec(memory_space=pltpu.SMEM)
    hbm = pl.BlockSpec(memory_space=pltpu.HBM)
    specs = [hbm if n in far else smem if a.ndim == 1 else vmem for n, a in enumerate(ins)]
    ins = [
        pltpu.with_memory_space_constraint(a, pltpu.HBM) if n in far else a
        for n, a in enumerate(ins)
    ]
    return pl.pallas_call(
        kernel,
        out_shape=[jax.ShapeDtypeStruct(s, d) for s, d in outs],
        in_specs=specs,
        out_specs=[vmem] * len(outs),
        scratch_shapes=[pltpu.VMEM(*s) if isinstance(s, tuple) else s for s in scratch],
        compiler_params=pltpu.CompilerParams(vmem_limit_bytes=VMEM_BYTES),
    )(*ins)


def widen(core, half, partner, before):
    held = [] if before is None else [before]
    far = pl.BlockSpec(memory_space=pltpu.HBM)
    return pl.pallas_call(
        functools.partial(widen_kernel, partner=partner),
        out_shape=jax.ShapeDtypeStruct((2, 2, HALF, C), F32),
        in_specs=[pl.BlockSpec(memory_space=pltpu.SMEM), pl.BlockSpec(memory_space=pltpu.VMEM)]
        + [far] * len(held),
        out_specs=far,
        scratch_shapes=[pltpu.VMEM((2, HALF, C), F32), pltpu.SemaphoreType.DMA((8,))],
        input_output_aliases={2: 0} if held else {},
        compiler_params=pltpu.CompilerParams(vmem_limit_bytes=VMEM_BYTES),
        name="widen_kernel",
    )(core, half, *held)


def shifted(value, axis, by):
    length = lax.axis_size(axis)
    return lax.ppermute(value, axis, [(i, (i + by) % length) for i in range(length)])


def exchange(value, axes):
    return lax.all_to_all(value, axes, 0, 0, tiled=True)


def swap(value):
    return lax.ppermute(value, CORE, [(0, 1), (1, 0)])


def join(faces, first, second):
    outs = [(first.shape, first.dtype)] * 2
    return local(join_kernel, outs, [faces, first, second])


def pair(first, second, axis, by):
    return shifted(first, axis, by), shifted(second, axis, -by)


def outward(y_up, y_low, x_faces):
    uy, ly = pair(y_up, y_low, GY, 1)
    up, low = join(x_faces, uy, ly)
    ux, lx = pair(up, low, GX, 1)
    return ux, lx, uy, ly


def homeward(y_low, y_up, x_faces):
    ly, uy = pair(y_low, y_up, GY, -1)
    low, up = join(x_faces, ly, uy)
    lx, ux = pair(low, up, GX, -1)
    return lx, ux, ly, uy


def program(
    voxel_feats,
    w_first,
    w_second,
    norm_gain,
    norm_shift,
    grad_out,
    brick_count,
    kernel_map,
    face_send,
    corner_send,
):
    face = face_send.reshape(4)
    corner = corner_send.reshape(4)
    i = lax.axis_index(GX)
    j = lax.axis_index(GY)
    dx = np.array([d[0] for d in NEIGHBOURS], np.int32)
    dy = np.array([d[1] for d in NEIGHBOURS], np.int32)
    inside = (i + dx >= 0) & (i + dx < 8) & (j + dy >= 0) & (j + dy < 16)
    meta = jnp.concatenate(
        [
            kernel_map.reshape(-1),
            brick_count,
            face,
            corner,
            inside.astype(jnp.int32),
            lax.axis_index(CORE).reshape(1),
        ]
    )
    norm = jnp.concatenate([norm_gain, norm_shift], axis=0)
    flat_one = w_first.reshape(TAPS * C, C)
    flat_two = w_second.reshape(TAPS * C, C)
    brick = (64, C)
    three, two = (3,) + brick, (2,) + brick
    rows = (ROWS, C)
    sums = ((2 * 128, C), F32)
    ext = ((EXT,) + brick, BF16)
    list_xh = ((EXT - 1,) + brick, F32)
    table = ((16, C), F32)
    sem = pltpu.SemaphoreType.DMA
    weight = ((TAPS * C, C), BF16)
    gathered = ((144, 6 * NB * C), BF16)
    forward = [gathered, gathered]

    *sends, kept = local(
        send_kernel,
        [(three, BF16), (three, BF16), (two, BF16), ((NB,) + brick, BF16)],
        [face, corner, voxel_feats],
        [pltpu.SMEM((4,), jnp.int32), pltpu.SMEM((4,), jnp.int32), sem((3,))],
        far=(0, 1, 2),
    )
    (near_one,) = local(fetch_one_kernel, [weight], [flat_one], [sem(())], far=(0,))
    (near_two,) = local(fetch_two_kernel, [weight], [flat_two], [sem(())], far=(0,))
    received = outward(*sends)
    z_one, ext_one, part, *sends = local(
        first_kernel,
        [((NB,) + brick, F32), ext, ((512, C), F32), (three, F32), (three, F32), (two, F32)],
        [meta, kept, *received, near_one],
        forward,
    )
    received = outward(*sends)
    part = exchange(part, GX_GY)
    z_two, ext_two, part, xh_one, consts = local(
        second_kernel,
        [(rows, F32), ext, sums, list_xh, table],
        [meta, part, z_one, *received, norm, near_two],
        forward,
    )
    part = exchange(part, GX_GY)
    out_feats, dv, xh_two, consts, part = local(
        third_kernel,
        [(rows, BF16), (rows, F32), (rows, F32), table, sums],
        [meta, part, consts, z_two, voxel_feats.reshape(rows), grad_out.reshape(rows)],
    )
    part = exchange(part, GX_GY)
    back = [((3, ROWS, 9 * C), F32), gathered, ((EXT,) + brick, F32)]
    dz_two, own, y_low, y_up, x_faces, part, consts = local(
        fourth_kernel,
        [(rows, BF16), (rows, F32), (three, BF16), (three, BF16), (two, BF16), sums, table],
        [meta, part, dv, xh_two, consts, xh_one, near_two],
        back,
    )
    returned = homeward(y_low, y_up, x_faces)
    chunks = (32, CHUNK, C)
    halves = [(chunks, F32), (chunks, BF16)]
    products = [gathered, gathered, ((TAPS * C, C), F32)]
    mine, other = local(taps_kernel, halves, [meta, ext_two, dz_two], products)
    (second,) = local(second_sum_kernel, [(chunks, BF16)], [mine, swap(other)])
    part = exchange(part, GX_GY)
    dz_one, own, y_low, y_up, x_faces, consts = local(
        fifth_kernel,
        [(rows, BF16), (rows, F32), (three, BF16), (three, BF16), (two, BF16), table],
        [meta, part, own, *returned, xh_one, consts, flat_one],
        [weight, sem(()), ((NB,) + brick, F32)] + back,
        far=(9,),
    )
    returned = homeward(y_low, y_up, x_faces)
    mine, other = local(taps_kernel, halves, [meta, ext_one, dz_one], products)
    grad_in, norm_grads = local(
        last_kernel,
        [(rows, BF16), ((4, C), F32)],
        [meta, own, *returned, dv, consts],
        [((NB,) + brick, F32)],
    )
    both = ((64, CHUNK, C), BF16)
    (part,) = local(first_sum_kernel, [both], [mine, swap(other), second])
    (whole,) = local(total_kernel, [both], [consts, exchange(part, CHIPS)])
    whole = exchange(whole, CHIPS)
    partner = swap(whole)
    core = lax.axis_index(CORE).reshape(1)
    weight_grads = widen(core, whole, False, None)
    weight_grads = widen(core, partner, True, weight_grads).reshape(2, TAPS, C, C)
    return (
        out_feats.reshape(NB, 64, C),
        grad_in.reshape(NB, 64, C),
        weight_grads,
        norm_grads,
    )


def solution(mesh):
    split = Mesh(mesh.devices.reshape(2, 4, 4, 2, 2), GX_GY)
    in_specs = (
        P(GX_GY, None, None),
        P(),
        P(),
        P(),
        P(),
        P(GX_GY, None, None),
        P(GX_GY),
        P(GX_GY, None),
        P(GX_GY, None, None),
        P(GX_GY, None, None),
    )
    out_specs = (P(GX_GY, None, None), P(GX_GY, None, None), P(), P())
    return jax.shard_map(program, mesh=split, in_specs=in_specs, out_specs=out_specs, check_vma=False)
```

```python
import functools

import jax
import jax.numpy as jnp
import numpy as np
from jax import lax
from jax.experimental import pallas as pl
from jax.experimental.pallas import tpu as pltpu
from jax.sharding import Mesh
from jax.sharding import PartitionSpec as P

GX = ("gx_0", "gx_1")
GY = ("gy_0", "gy_1", "gy_2")
GX_GY = ("gx_0", "gx_1", "gy_0", "gy_1", "gy_2")
CORE = ("gy_2",)
PLANE = ("gx_1", "gy_0")
LINE = ("gx_0", "gy_1")
C = 128
NB = 4
ROWS = NB * 64
TAPS = 27
EXT = 13
EPSILON = 1e-05
F32 = jnp.float32
BF16 = jnp.bfloat16
COUNT, FACE, CORNER, VALID, CORE_AT = 108, 109, 113, 117, 125
NEIGHBOURS = ((-1, 0), (1, 0), (0, -1), (0, 1), (-1, -1), (-1, 1), (1, -1), (1, 1))
CHUNK = 56
HALF = TAPS * C // 2
VMEM_BYTES = 16 << 20


def row_of(k):
    return slice(k, k + 1)


VOXELS = row_of(0)
RECIP = (row_of(1), row_of(2))
NORM_ROWS = slice(4, 8)
GAIN = (row_of(4), row_of(5))
SHIFT = (row_of(6), row_of(7))
CROSS = (row_of(8), row_of(9))
TOTAL = (row_of(10), row_of(11))


def shift_matrix(flipped):
    def places(axis):
        at = lax.broadcasted_iota(jnp.int32, (144, 144), axis)
        major = (at >= 48).astype(jnp.int32) + (at >= 96).astype(jnp.int32)
        minor = (at >> 4) - 3 * major
        return major, minor, (at >> 2) & 3, at & 3

    b, c, q, r = places(1 if flipped else 0)
    ob, oc, qs, rs = places(0 if flipped else 1)
    hit = (4 * ob + qs == q + b + 3) & (4 * oc + rs == r + c + 3)
    return hit.astype(F32).astype(BF16)


def sources():
    return [(0, 0, 3), (1, 1, 0), (2, 1, 1), (3, 1, 2), (4, 1, 3), (5, 2, 0)]


def sigmoid(v):
    return 1.0 / (1.0 + jnp.exp(-v))


def slope(v):
    s = sigmoid(v)
    return s * (1.0 + v * (1.0 - s))


def occupied_rows(meta):
    brick = lax.broadcasted_iota(jnp.int32, (ROWS, C), 0) // 64
    return (brick < meta[COUNT]).astype(F32)


def shifted_planes(meta, ext, gathered, planes):
    shift = shift_matrix(False)
    for b in range(NB):
        for plane, oa, source in sources():
            for d in range(9):
                entry = meta[27 * b + 9 * oa + d]
                gathered[16 * d : 16 * d + 16, (6 * b + plane) * C : (6 * b + plane + 1) * C] = ext[
                    entry, 16 * source : 16 * source + 16, :
                ]
    for b in range(NB):
        at = slice(6 * b * C, 6 * (b + 1) * C)
        planes[:, at] = jnp.dot(shift, gathered[:, at], preferred_element_type=F32).astype(BF16)


def patches(planes, k):
    a, d = divmod(k, 9)
    tiles = [
        planes[16 * d : 16 * d + 16, (6 * b + p + a) * C : (6 * b + p + a + 1) * C]
        for b in range(NB)
        for p in range(4)
    ]
    return jnp.concatenate(tiles, axis=0)


def convolve(planes, weight):
    total = jnp.zeros((ROWS, C), F32)
    for k in range(0, TAPS, 2):
        taps = range(k, min(k + 2, TAPS))
        columns = jnp.concatenate([patches(planes, tap) for tap in taps], axis=1)
        total += jnp.dot(
            columns, weight[k * C : (k + len(taps)) * C, :], preferred_element_type=F32
        )
    return total


def convolve_back(meta, dz, weight, spread, moved, acc):
    shift_back = shift_matrix(True)
    for a in range(3):
        spread[a] = lax.dot_general(
            dz,
            weight[9 * a * C : 9 * (a + 1) * C, :],
            (((1,), (1,)), ((), ())),
            preferred_element_type=F32,
        )
    acc[...] = jnp.zeros_like(acc)
    for b in range(NB):
        for plane in range(6):
            taps = [a for a in range(3) if 0 <= plane - a < 4]
            for d in range(9):
                total = None
                for a in taps:
                    row = 64 * b + 16 * (plane - a)
                    piece = spread[a, row : row + 16, d * C : (d + 1) * C]
                    total = piece if total is None else total + piece
                moved[16 * d : 16 * d + 16, (6 * b + plane) * C : (6 * b + plane + 1) * C] = (
                    total.astype(BF16)
                )
    for b in range(NB):
        home = jnp.dot(
            shift_back, moved[:, 6 * b * C : 6 * (b + 1) * C], preferred_element_type=F32
        )
        for plane, oa, source in sources():
            for d in range(9):
                entry = meta[27 * b + 9 * oa + d]
                acc[entry, 16 * source : 16 * source + 16, :] += home[
                    16 * d : 16 * d + 16, plane * C : (plane + 1) * C
                ]


def write_sums(out, first, second):
    odd = lax.broadcasted_iota(jnp.int32, (8, C), 0) % 2
    both = jnp.where(odd == 0, jnp.broadcast_to(first, (8, C)), jnp.broadcast_to(second, (8, C)))
    out[...] = jnp.broadcast_to(both[None], (out.shape[0] // 8, 8, C)).reshape(out.shape)


def read_sums(got):
    total = jnp.sum(got[...].reshape(got.shape[0] // 8, 8, C), axis=0)
    odd = lax.broadcasted_iota(jnp.int32, (8, C), 0) % 2
    first = jnp.sum(jnp.where(odd == 0, total, 0.0), axis=0, keepdims=True)
    second = jnp.sum(jnp.where(odd == 1, total, 0.0), axis=0, keepdims=True)
    return first, second


def rows_sum(v):
    return jnp.sum(v, axis=0, keepdims=True)


def statistics(total, squares, voxels):
    center = total / voxels
    spread_sq = squares / voxels - center * center
    return center, lax.rsqrt(spread_sq + EPSILON)


def received_bricks(ux, lx, uy, ly):
    return (
        ux.at[0], lx.at[0], uy.at[0], ly.at[0], ux.at[1], ux.at[2], lx.at[1], lx.at[2]
    )


def sends_of(face, corner, y_up, y_low, x_faces):
    return (
        (face(2), y_up.at[0]), (corner(0), y_up.at[1]), (corner(2), y_up.at[2]),
        (face(3), y_low.at[0]), (corner(1), y_low.at[1]), (corner(3), y_low.at[2]),
        (face(0), x_faces.at[0]), (face(1), x_faces.at[1]),
    )


def select_sends(meta, field, y_up, y_low, x_faces):
    for entry, out in sends_of(
        lambda k: meta[FACE + k], lambda k: meta[CORNER + k], y_up, y_low, x_faces
    ):
        out[...] = field[entry]


def send_kernel(face_far, corner_far, field, y_up, y_low, x_faces, kept, face, corner, sems):
    copies = [
        pltpu.make_async_copy(field, kept, sems.at[0]),
        pltpu.make_async_copy(face_far, face, sems.at[1]),
        pltpu.make_async_copy(corner_far, corner, sems.at[2]),
    ]
    for copy in copies:
        copy.start()
    for copy in copies:
        copy.wait()
    for entry, out in sends_of(lambda k: face[k], lambda k: corner[k], y_up, y_low, x_faces):
        out[...] = kept[entry]


def fetch_one_kernel(far, out, sem):
    copy = pltpu.make_async_copy(far, out, sem)
    copy.start()
    copy.wait()


def fetch_two_kernel(far, out, sem):
    copy = pltpu.make_async_copy(far, out, sem)
    copy.start()
    copy.wait()


def join_kernel(faces, first, second, up, low):
    up[0] = faces[0]
    up[1] = first[1]
    up[2] = second[1]
    low[0] = faces[1]
    low[1] = first[2]
    low[2] = second[2]


def first_kernel(
    meta, voxel_feats, ux, lx, uy, ly, weight,
    z_out, ext, sums, y_up, y_low, x_faces, gathered, planes,
):
    ext[NB + 8] = jnp.zeros((64, C), BF16)
    for b in range(NB):
        keep = (meta[COUNT] > b).astype(F32)
        ext[b] = (voxel_feats[b].astype(F32) * keep).astype(BF16)
    for e, brick in enumerate(received_bricks(ux, lx, uy, ly)):
        keep = meta[VALID + e].astype(F32)
        ext[NB + e] = (brick[...].astype(F32) * keep).astype(BF16)
    shifted_planes(meta, ext, gathered, planes)
    z = convolve(planes, weight)
    z_out[...] = z.reshape(NB, 64, C)
    select_sends(meta, z_out, y_up, y_low, x_faces)
    masked = z * occupied_rows(meta)
    row = lax.broadcasted_iota(jnp.int32, (8, C), 0) % 4
    count = (64 * meta[COUNT]).astype(F32)
    part = jnp.where(
        row == 0, rows_sum(masked), jnp.where(row == 1, rows_sum(z * masked), count)
    )
    sums[...] = jnp.broadcast_to(part[None], (64, 8, C)).reshape(512, C)


def second_kernel(
    meta, got, z_one, ux, lx, uy, ly, norm, weight,
    z_out, ext, sums, xh_out, consts, gathered, planes,
):
    row = lax.broadcasted_iota(jnp.int32, (8, C), 0) % 4
    both = jnp.sum(got[...].reshape(64, 8, C), axis=0)
    total = rows_sum(jnp.where(row == 0, both, 0.0))
    squares = rows_sum(jnp.where(row == 1, both, 0.0))
    voxels = rows_sum(jnp.where(row == 2, both, 0.0))
    center, recip = statistics(total, squares, voxels)
    consts[...] = jnp.zeros_like(consts)
    consts[VOXELS] = voxels
    consts[RECIP[0]] = recip
    consts[NORM_ROWS] = norm[...]
    for e in range(EXT - 1):
        keep = meta[COUNT] > e if e < NB else meta[VALID + e - NB] > 0
        field = z_one[e] if e < NB else received_bricks(ux, lx, uy, ly)[e - NB][...]
        xh = (field - center) * recip
        xh_out[e] = xh
        u = norm[0:1] * xh + norm[2:3]
        ext[e] = (u * sigmoid(u) * keep.astype(F32)).astype(BF16)
    ext[EXT - 1] = jnp.zeros((64, C), BF16)
    shifted_planes(meta, ext, gathered, planes)
    z = convolve(planes, weight)
    z_out[...] = z
    masked = z * occupied_rows(meta)
    write_sums(sums, rows_sum(masked), rows_sum(z * masked))


def third_kernel(
    meta, got, constants, z_two, voxel_feats, grad_out, out_feats, dv_out, xh_out, consts, sums
):
    total, squares = read_sums(got)
    center, recip = statistics(total, squares, constants[VOXELS])
    consts[...] = constants[...]
    consts[RECIP[1]] = recip
    occupied = occupied_rows(meta)
    xh = (z_two[...] - center) * recip
    xh_out[...] = xh
    feats = voxel_feats[...].astype(F32) * occupied
    pre = constants[GAIN[1]] * xh + constants[SHIFT[1]] + feats
    s = sigmoid(pre)
    out_feats[...] = (pre * s * occupied).astype(BF16)
    dv = grad_out[...].astype(F32) * occupied * (s * (1.0 + pre * (1.0 - s)))
    dv_out[...] = dv
    write_sums(sums, rows_sum(dv), rows_sum(dv * xh))


def norm_back(dv, xh, consts, number, total, cross, occupied):
    voxels = consts[VOXELS]
    scale = occupied * consts[GAIN[number]] * consts[RECIP[number]]
    return (scale * (dv - total / voxels - xh * cross / voxels)).astype(BF16)


def send_gradients(acc, own, y_low, y_up, x_faces):
    own[...] = acc[0:NB].reshape(ROWS, C)
    y_low[0] = acc[NB + 2].astype(BF16)
    y_low[1] = acc[NB + 4].astype(BF16)
    y_low[2] = acc[NB + 6].astype(BF16)
    y_up[0] = acc[NB + 3].astype(BF16)
    y_up[1] = acc[NB + 5].astype(BF16)
    y_up[2] = acc[NB + 7].astype(BF16)
    x_faces[0] = acc[NB].astype(BF16)
    x_faces[1] = acc[NB + 1].astype(BF16)


def fourth_kernel(
    meta, got, dv, xh_two, constants, xh_one, weight,
    dz_out, own, y_low, y_up, x_faces, sums, consts, spread, moved, acc,
):
    total, cross = read_sums(got)
    consts[...] = constants[...]
    consts[CROSS[1]] = cross
    consts[TOTAL[1]] = total
    dz = norm_back(dv[...], xh_two[...], constants, 1, total, cross, occupied_rows(meta))
    dz_out[...] = dz
    convolve_back(meta, dz, weight, spread, moved, acc)
    send_gradients(acc, own, y_low, y_up, x_faces)
    first = jnp.zeros((64, C), F32)
    second = jnp.zeros((64, C), F32)
    for e in range(EXT - 1):
        keep = meta[COUNT] > e if e < NB else meta[VALID + e - NB] > 0
        xh = xh_one[e]
        du = acc[e] * slope(constants[GAIN[0]] * xh + constants[SHIFT[0]]) * keep.astype(F32)
        first += du
        second += du * xh
    write_sums(sums, rows_sum(first), rows_sum(second))


def add_returned(meta, field, lx, ux, ly, uy):
    for ref, k, at, neighbour in (
        (lx, 0, FACE, 1), (ux, 0, FACE + 1, 0), (ly, 0, FACE + 2, 3), (uy, 0, FACE + 3, 2),
        (lx, 1, CORNER, 7), (lx, 2, CORNER + 1, 6),
        (ux, 1, CORNER + 2, 5), (ux, 2, CORNER + 3, 4),
    ):
        field[meta[at]] += ref[k].astype(F32) * meta[VALID + neighbour].astype(F32)


def fifth_kernel(
    meta, got, own_in, lx, ux, ly, uy, xh_one, constants, weight_far,
    dz_out, own, y_low, y_up, x_faces, consts, weight, sem, field, spread, moved, acc,
):
    fetch = pltpu.make_async_copy(weight_far, weight, sem)
    fetch.start()
    total, cross = read_sums(got)
    consts[...] = constants[...]
    consts[CROSS[0]] = cross
    consts[TOTAL[0]] = total
    field[...] = own_in[...].reshape(NB, 64, C)
    add_returned(meta, field, lx, ux, ly, uy)
    occupied = occupied_rows(meta)
    xh = xh_one[0:NB].reshape(ROWS, C)
    du = field[...].reshape(ROWS, C) * occupied * slope(
        constants[GAIN[0]] * xh + constants[SHIFT[0]]
    )
    dz = norm_back(du, xh, constants, 0, total, cross, occupied)
    dz_out[...] = dz
    fetch.wait()
    convolve_back(meta, dz, weight, spread, moved, acc)
    send_gradients(acc, own, y_low, y_up, x_faces)


def taps_kernel(meta, ext, dz, mine, other, gathered, planes, taps):
    shifted_planes(meta, ext, gathered, planes)
    for k in range(TAPS):
        taps[k * C : (k + 1) * C, :] = lax.dot_general(
            patches(planes, k),
            dz[...],
            (((0,), (0,)), ((), ())),
            preferred_element_type=F32,
        )
    here = meta[CORE_AT] == 0
    mine[30:32] = jnp.zeros((2, CHUNK, C), F32)
    other[30:32] = jnp.zeros((2, CHUNK, C), BF16)
    for c in range(31):
        full = min(CHUNK, HALF - CHUNK * c)
        at = CHUNK * c
        low = taps[at : at + full, :]
        high = taps[HALF + at : HALF + at + full, :]
        mine[c, 0:full, :] = jnp.where(here, low, high)
        other[c, 0:full, :] = jnp.where(here, high, low).astype(BF16)


def second_sum_kernel(mine, received, out):
    out[...] = (mine[...] + received[...].astype(F32)).astype(BF16)


def first_sum_kernel(mine, received, second, out):
    out[0:32] = (mine[...] + received[...].astype(F32)).astype(BF16)
    out[32:64] = second[...]


def plane_sum_kernel(pieces, out):
    out[...] = jnp.sum(pieces[...].astype(F32), axis=0).astype(BF16)


def total_kernel(consts, own, next_one, opposite, last_one, out):
    even = own[...].astype(F32) + opposite[...].astype(F32)
    odd = next_one[...].astype(F32) + last_one[...].astype(F32)
    total = (even + odd) / jnp.sqrt(consts[VOXELS])
    out[...] = jnp.broadcast_to(total.astype(BF16)[None], out.shape)


def last_kernel(meta, own, lx, ux, ly, uy, dv, consts, grad_in, norm_grads, field):
    field[...] = own[...].reshape(NB, 64, C)
    add_returned(meta, field, lx, ux, ly, uy)
    total = (dv[...] + field[...].reshape(ROWS, C)) * occupied_rows(meta)
    grad_in[...] = total.astype(BF16)
    root = jnp.sqrt(consts[VOXELS])
    for row, at in enumerate((CROSS[0], TOTAL[0], CROSS[1], TOTAL[1])):
        norm_grads[row : row + 1] = consts[at] / root


def widen_kernel(core, half, *refs, partner):
    out, wide, sems = refs[-3:]
    at = 1 - core[0] if partner else core[0]
    copies = []
    for conv in range(2):
        for piece in range(4):
            for c in range(8 * piece, min(8 * piece + 8, 31)):
                full = min(CHUNK, HALF - CHUNK * c)
                wide[conv, CHUNK * c : CHUNK * c + full, :] = half[32 * conv + c].astype(F32)[
                    0:full
                ]
            first = 8 * CHUNK * piece
            rows = pl.ds(first, min(8 * CHUNK, HALF - first))
            copies.append(
                pltpu.make_async_copy(
                    wide.at[conv, rows], out.at[conv, at, rows], sems.at[4 * conv + piece]
                )
            )
            copies[-1].start()
    for copy in copies:
        copy.wait()


def local(kernel, outs, ins, scratch=(), far=()):
    vmem = pl.BlockSpec(memory_space=pltpu.VMEM)
    smem = pl.BlockSpec(memory_space=pltpu.SMEM)
    hbm = pl.BlockSpec(memory_space=pltpu.HBM)
    specs = [hbm if n in far else smem if a.ndim == 1 else vmem for n, a in enumerate(ins)]
    ins = [
        pltpu.with_memory_space_constraint(a, pltpu.HBM) if n in far else a
        for n, a in enumerate(ins)
    ]
    return pl.pallas_call(
        kernel,
        out_shape=[jax.ShapeDtypeStruct(s, d) for s, d in outs],
        in_specs=specs,
        out_specs=[vmem] * len(outs),
        scratch_shapes=[pltpu.VMEM(*s) if isinstance(s, tuple) else s for s in scratch],
        compiler_params=pltpu.CompilerParams(vmem_limit_bytes=VMEM_BYTES),
    )(*ins)


def widen(core, half, partner, before):
    held = [] if before is None else [before]
    far = pl.BlockSpec(memory_space=pltpu.HBM)
    return pl.pallas_call(
        functools.partial(widen_kernel, partner=partner),
        out_shape=jax.ShapeDtypeStruct((2, 2, HALF, C), F32),
        in_specs=[pl.BlockSpec(memory_space=pltpu.SMEM), pl.BlockSpec(memory_space=pltpu.VMEM)]
        + [far] * len(held),
        out_specs=far,
        scratch_shapes=[pltpu.VMEM((2, HALF, C), F32), pltpu.SemaphoreType.DMA((8,))],
        input_output_aliases={2: 0} if held else {},
        compiler_params=pltpu.CompilerParams(vmem_limit_bytes=VMEM_BYTES),
        name="widen_kernel",
    )(core, half, *held)


def shifted(value, axis, by):
    length = lax.axis_size(axis)
    return lax.ppermute(value, axis, [(i, (i + by) % length) for i in range(length)])


def exchange(value, axes):
    return lax.all_to_all(value, axes, 0, 0, tiled=True)


def swap(value):
    return lax.ppermute(value, CORE, [(0, 1), (1, 0)])


def join(faces, first, second):
    outs = [(first.shape, first.dtype)] * 2
    return local(join_kernel, outs, [faces, first, second])


def pair(first, second, axis, by):
    return shifted(first, axis, by), shifted(second, axis, -by)


def outward(y_up, y_low, x_faces):
    uy, ly = pair(y_up, y_low, GY, 1)
    up, low = join(x_faces, uy, ly)
    ux, lx = pair(up, low, GX, 1)
    return ux, lx, uy, ly


def homeward(y_low, y_up, x_faces):
    ly, uy = pair(y_low, y_up, GY, -1)
    low, up = join(x_faces, ly, uy)
    lx, ux = pair(low, up, GX, -1)
    return lx, ux, ly, uy


def program(
    voxel_feats,
    w_first,
    w_second,
    norm_gain,
    norm_shift,
    grad_out,
    brick_count,
    kernel_map,
    face_send,
    corner_send,
):
    face = face_send.reshape(4)
    corner = corner_send.reshape(4)
    i = lax.axis_index(GX)
    j = lax.axis_index(GY)
    dx = np.array([d[0] for d in NEIGHBOURS], np.int32)
    dy = np.array([d[1] for d in NEIGHBOURS], np.int32)
    inside = (i + dx >= 0) & (i + dx < 8) & (j + dy >= 0) & (j + dy < 16)
    meta = jnp.concatenate(
        [
            kernel_map.reshape(-1),
            brick_count,
            face,
            corner,
            inside.astype(jnp.int32),
            lax.axis_index(CORE).reshape(1),
        ]
    )
    norm = jnp.concatenate([norm_gain, norm_shift], axis=0)
    flat_one = w_first.reshape(TAPS * C, C)
    flat_two = w_second.reshape(TAPS * C, C)
    brick = (64, C)
    three, two = (3,) + brick, (2,) + brick
    rows = (ROWS, C)
    sums = ((2 * 128, C), F32)
    ext = ((EXT,) + brick, BF16)
    list_xh = ((EXT - 1,) + brick, F32)
    table = ((16, C), F32)
    sem = pltpu.SemaphoreType.DMA
    weight = ((TAPS * C, C), BF16)
    gathered = ((144, 6 * NB * C), BF16)
    forward = [gathered, gathered]

    *sends, kept = local(
        send_kernel,
        [(three, BF16), (three, BF16), (two, BF16), ((NB,) + brick, BF16)],
        [face, corner, voxel_feats],
        [pltpu.SMEM((4,), jnp.int32), pltpu.SMEM((4,), jnp.int32), sem((3,))],
        far=(0, 1, 2),
    )
    (near_one,) = local(fetch_one_kernel, [weight], [flat_one], [sem(())], far=(0,))
    (near_two,) = local(fetch_two_kernel, [weight], [flat_two], [sem(())], far=(0,))
    received = outward(*sends)
    z_one, ext_one, part, *sends = local(
        first_kernel,
        [((NB,) + brick, F32), ext, ((512, C), F32), (three, F32), (three, F32), (two, F32)],
        [meta, kept, *received, near_one],
        forward,
    )
    received = outward(*sends)
    part = exchange(part, GX_GY)
    z_two, ext_two, part, xh_one, consts = local(
        second_kernel,
        [(rows, F32), ext, sums, list_xh, table],
        [meta, part, z_one, *received, norm, near_two],
        forward,
    )
    part = exchange(part, GX_GY)
    out_feats, dv, xh_two, consts, part = local(
        third_kernel,
        [(rows, BF16), (rows, F32), (rows, F32), table, sums],
        [meta, part, consts, z_two, voxel_feats.reshape(rows), grad_out.reshape(rows)],
    )
    part = exchange(part, GX_GY)
    back = [((3, ROWS, 9 * C), F32), gathered, ((EXT,) + brick, F32)]
    dz_two, own, y_low, y_up, x_faces, part, consts = local(
        fourth_kernel,
        [(rows, BF16), (rows, F32), (three, BF16), (three, BF16), (two, BF16), sums, table],
        [meta, part, dv, xh_two, consts, xh_one, near_two],
        back,
    )
    returned = homeward(y_low, y_up, x_faces)
    chunks = (32, CHUNK, C)
    halves = [(chunks, F32), (chunks, BF16)]
    products = [gathered, gathered, ((TAPS * C, C), F32)]
    mine, other = local(taps_kernel, halves, [meta, ext_two, dz_two], products)
    (second,) = local(second_sum_kernel, [(chunks, BF16)], [mine, swap(other)])
    part = exchange(part, GX_GY)
    dz_one, own, y_low, y_up, x_faces, consts = local(
        fifth_kernel,
        [(rows, BF16), (rows, F32), (three, BF16), (three, BF16), (two, BF16), table],
        [meta, part, own, *returned, xh_one, consts, flat_one],
        [weight, sem(()), ((NB,) + brick, F32)] + back,
        far=(9,),
    )
    returned = homeward(y_low, y_up, x_faces)
    mine, other = local(taps_kernel, halves, [meta, ext_one, dz_one], products)
    grad_in, norm_grads = local(
        last_kernel,
        [(rows, BF16), ((4, C), F32)],
        [meta, own, *returned, dv, consts],
        [((NB,) + brick, F32)],
    )
    both = ((64, CHUNK, C), BF16)
    (part,) = local(first_sum_kernel, [both], [mine, swap(other), second])
    chunk = (4 * CHUNK, C)
    part = exchange(part.reshape((16,) + chunk), PLANE)
    (part,) = local(plane_sum_kernel, [(chunk, BF16)], [part])
    others = [shifted(part, LINE, by) for by in (1, 2, 3)]
    (whole,) = local(total_kernel, [((16,) + chunk, BF16)], [consts, part, *others])
    whole = exchange(whole, PLANE).reshape(64, CHUNK, C)
    partner = swap(whole)
    core = lax.axis_index(CORE).reshape(1)
    weight_grads = widen(core, whole, False, None)
    weight_grads = widen(core, partner, True, weight_grads).reshape(2, TAPS, C, C)
    return (
        out_feats.reshape(NB, 64, C),
        grad_in.reshape(NB, 64, C),
        weight_grads,
        norm_grads,
    )


def solution(mesh):
    split = Mesh(mesh.devices.reshape(2, 4, 4, 2, 2), GX_GY)
    in_specs = (
        P(GX_GY, None, None),
        P(),
        P(),
        P(),
        P(),
        P(GX_GY, None, None),
        P(GX_GY),
        P(GX_GY, None),
        P(GX_GY, None, None),
        P(GX_GY, None, None),
    )
    out_specs = (P(GX_GY, None, None), P(GX_GY, None, None), P(), P())
    return jax.shard_map(program, mesh=split, in_specs=in_specs, out_specs=out_specs, check_vma=False)
```

```python
import functools

import jax
import jax.numpy as jnp
import numpy as np
from jax import lax
from jax.experimental import pallas as pl
from jax.experimental.pallas import tpu as pltpu
from jax.sharding import Mesh
from jax.sharding import PartitionSpec as P

GX = ("gx_0", "gx_1")
GY = ("gy_0", "gy_1", "gy_2")
GX_GY = ("gx_0", "gx_1", "gy_0", "gy_1", "gy_2")
CORE = ("gy_2",)
X_LINE = "gx_1"
Y_LINE = "gy_2"
CHIPS = ("gx_0", "gx_1", "gy_0", "gy_1")
C = 128
NB = 4
ROWS = NB * 64
TAPS = 27
EXT = 13
EPSILON = 1e-05
F32 = jnp.float32
BF16 = jnp.bfloat16
COUNT, FACE, CORNER, VALID, CORE_AT = 108, 109, 113, 117, 125
NEIGHBOURS = ((-1, 0), (1, 0), (0, -1), (0, 1), (-1, -1), (-1, 1), (1, -1), (1, 1))
CHUNK = 56
HALF = TAPS * C // 2
VMEM_BYTES = 16 << 20


def row_of(k):
    return slice(k, k + 1)


VOXELS = row_of(0)
RECIP = (row_of(1), row_of(2))
NORM_ROWS = slice(4, 8)
GAIN = (row_of(4), row_of(5))
SHIFT = (row_of(6), row_of(7))
CROSS = (row_of(8), row_of(9))
TOTAL = (row_of(10), row_of(11))


def shift_matrix(flipped):
    def places(axis):
        at = lax.broadcasted_iota(jnp.int32, (144, 144), axis)
        major = (at >= 48).astype(jnp.int32) + (at >= 96).astype(jnp.int32)
        minor = (at >> 4) - 3 * major
        return major, minor, (at >> 2) & 3, at & 3

    b, c, q, r = places(1 if flipped else 0)
    ob, oc, qs, rs = places(0 if flipped else 1)
    hit = (4 * ob + qs == q + b + 3) & (4 * oc + rs == r + c + 3)
    return hit.astype(F32).astype(BF16)


def sources():
    return [(0, 0, 3), (1, 1, 0), (2, 1, 1), (3, 1, 2), (4, 1, 3), (5, 2, 0)]


def sigmoid(v):
    return 1.0 / (1.0 + jnp.exp(-v))


def slope(v):
    s = sigmoid(v)
    return s * (1.0 + v * (1.0 - s))


def occupied_rows(meta):
    brick = lax.broadcasted_iota(jnp.int32, (ROWS, C), 0) // 64
    return (brick < meta[COUNT]).astype(F32)


def shifted_planes(meta, ext, gathered, planes):
    shift = shift_matrix(False)
    for b in range(NB):
        for plane, oa, source in sources():
            for d in range(9):
                entry = meta[27 * b + 9 * oa + d]
                gathered[16 * d : 16 * d + 16, (6 * b + plane) * C : (6 * b + plane + 1) * C] = ext[
                    entry, 16 * source : 16 * source + 16, :
                ]
    for b in range(NB):
        at = slice(6 * b * C, 6 * (b + 1) * C)
        planes[:, at] = jnp.dot(shift, gathered[:, at], preferred_element_type=F32).astype(BF16)


def patches(planes, k):
    a, d = divmod(k, 9)
    tiles = [
        planes[16 * d : 16 * d + 16, (6 * b + p + a) * C : (6 * b + p + a + 1) * C]
        for b in range(NB)
        for p in range(4)
    ]
    return jnp.concatenate(tiles, axis=0)


def convolve(planes, weight):
    total = jnp.zeros((ROWS, C), F32)
    for k in range(0, TAPS, 2):
        taps = range(k, min(k + 2, TAPS))
        columns = jnp.concatenate([patches(planes, tap) for tap in taps], axis=1)
        total += jnp.dot(
            columns, weight[k * C : (k + len(taps)) * C, :], preferred_element_type=F32
        )
    return total


def convolve_back(meta, dz, weight, spread, moved, acc, fetches=()):
    shift_back = shift_matrix(True)
    for a in range(3):
        if fetches:
            fetches[a].wait()
        spread[a] = lax.dot_general(
            dz,
            weight[9 * a * C : 9 * (a + 1) * C, :],
            (((1,), (1,)), ((), ())),
            preferred_element_type=F32,
        )
    acc[...] = jnp.zeros_like(acc)
    for b in range(NB):
        for plane in range(6):
            taps = [a for a in range(3) if 0 <= plane - a < 4]
            for d in range(9):
                total = None
                for a in taps:
                    row = 64 * b + 16 * (plane - a)
                    piece = spread[a, row : row + 16, d * C : (d + 1) * C]
                    total = piece if total is None else total + piece
                moved[16 * d : 16 * d + 16, (6 * b + plane) * C : (6 * b + plane + 1) * C] = (
                    total.astype(BF16)
                )
    for b in range(NB):
        home = jnp.dot(
            shift_back, moved[:, 6 * b * C : 6 * (b + 1) * C], preferred_element_type=F32
        )
        for plane, oa, source in sources():
            for d in range(9):
                entry = meta[27 * b + 9 * oa + d]
                acc[entry, 16 * source : 16 * source + 16, :] += home[
                    16 * d : 16 * d + 16, plane * C : (plane + 1) * C
                ]


def write_sums(out, first, second):
    odd = lax.broadcasted_iota(jnp.int32, (8, C), 0) % 2
    both = jnp.where(odd == 0, jnp.broadcast_to(first, (8, C)), jnp.broadcast_to(second, (8, C)))
    out[...] = jnp.broadcast_to(both[None], (out.shape[0] // 8, 8, C)).reshape(out.shape)


def read_sums(got):
    total = jnp.sum(got[...].reshape(got.shape[0] // 8, 8, C), axis=0)
    odd = lax.broadcasted_iota(jnp.int32, (8, C), 0) % 2
    first = jnp.sum(jnp.where(odd == 0, total, 0.0), axis=0, keepdims=True)
    second = jnp.sum(jnp.where(odd == 1, total, 0.0), axis=0, keepdims=True)
    return first, second


def rows_sum(v):
    return jnp.sum(v, axis=0, keepdims=True)


def statistics(total, squares, voxels):
    center = total / voxels
    spread_sq = squares / voxels - center * center
    return center, lax.rsqrt(spread_sq + EPSILON)


def parity(axis):
    return 1 - lax.rem(lax.axis_index(axis), 2)


def from_next(near, far, even, k):
    return jnp.where(even == 1, near[k], far[k])


def from_previous(near, far, even, k):
    return jnp.where(even == 1, far[k], near[k])


def received_bricks(x_near, x_far, y_near, y_far):
    ex, ey = parity(X_LINE), parity(Y_LINE)
    return (
        from_previous(x_near, x_far, ex, 0), from_next(x_near, x_far, ex, 0),
        from_previous(y_near, y_far, ey, 0), from_next(y_near, y_far, ey, 0),
        from_previous(x_near, x_far, ex, 1), from_previous(x_near, x_far, ex, 2),
        from_next(x_near, x_far, ex, 1), from_next(x_near, x_far, ex, 2),
    )


def sends_of(face, corner, y_near, y_far, x_faces):
    even = parity(Y_LINE)

    def either(number, up, low):
        return jnp.where(even == number, up, low)

    up = (face(2), corner(0), corner(2))
    low = (face(3), corner(1), corner(3))
    pairs = [(face(0), x_faces.at[0]), (face(1), x_faces.at[1])]
    for k in range(3):
        pairs.append((either(1, up[k], low[k]), y_near.at[k]))
        pairs.append((either(0, up[k], low[k]), y_far.at[k]))
    return pairs


def select_sends(meta, field, y_near, y_far, x_faces):
    for entry, out in sends_of(
        lambda k: meta[FACE + k], lambda k: meta[CORNER + k], y_near, y_far, x_faces
    ):
        out[...] = field[entry]


def send_kernel(face_far, corner_far, field, y_near, y_far, x_faces, kept, face, corner, sems):
    copies = [
        pltpu.make_async_copy(field, kept, sems.at[0]),
        pltpu.make_async_copy(face_far, face, sems.at[1]),
        pltpu.make_async_copy(corner_far, corner, sems.at[2]),
    ]
    for copy in copies:
        copy.start()
    for copy in copies:
        copy.wait()
    for entry, out in sends_of(lambda k: face[k], lambda k: corner[k], y_near, y_far, x_faces):
        out[...] = kept[entry]


def fetch_one_kernel(far, out, sem):
    copy = pltpu.make_async_copy(far, out, sem)
    copy.start()
    copy.wait()


def fetch_two_kernel(far, out, sem):
    copy = pltpu.make_async_copy(far, out, sem)
    copy.start()
    copy.wait()


def join_kernel(faces, y_near, y_far, x_near, x_far, *, home):
    ex, ey = parity(X_LINE), parity(Y_LINE)
    before = [from_previous(y_near, y_far, ey, k) for k in (1, 2)]
    after = [from_next(y_near, y_far, ey, k) for k in (1, 2)]
    if home:
        low, up = ((faces[k], after[k], before[k]) for k in range(2))
    else:
        up, low = ((faces[k], before[k], after[k]) for k in range(2))
    for k in range(3):
        x_near[k] = jnp.where(ex == 1, up[k], low[k])
        x_far[k] = jnp.where(ex == 1, low[k], up[k])


def first_kernel(
    meta, voxel_feats, x_near, x_far, y_near, y_far, weight,
    z_out, ext, sums, y_near_out, y_far_out, x_faces, gathered, planes,
):
    ext[NB + 8] = jnp.zeros((64, C), BF16)
    for b in range(NB):
        keep = (meta[COUNT] > b).astype(F32)
        ext[b] = (voxel_feats[b].astype(F32) * keep).astype(BF16)
    for e, brick in enumerate(received_bricks(x_near, x_far, y_near, y_far)):
        keep = meta[VALID + e].astype(F32)
        ext[NB + e] = (brick.astype(F32) * keep).astype(BF16)
    shifted_planes(meta, ext, gathered, planes)
    z = convolve(planes, weight)
    z_out[...] = z.reshape(NB, 64, C)
    select_sends(meta, z_out, y_near_out, y_far_out, x_faces)
    masked = z * occupied_rows(meta)
    row = lax.broadcasted_iota(jnp.int32, (8, C), 0) % 4
    count = (64 * meta[COUNT]).astype(F32)
    part = jnp.where(
        row == 0, rows_sum(masked), jnp.where(row == 1, rows_sum(z * masked), count)
    )
    sums[...] = jnp.broadcast_to(part[None], (64, 8, C)).reshape(512, C)


def second_kernel(
    meta, got, z_one, x_near, x_far, y_near, y_far, norm, weight,
    z_out, ext, sums, xh_out, consts, gathered, planes,
):
    row = lax.broadcasted_iota(jnp.int32, (8, C), 0) % 4
    both = jnp.sum(got[...].reshape(64, 8, C), axis=0)
    total = rows_sum(jnp.where(row == 0, both, 0.0))
    squares = rows_sum(jnp.where(row == 1, both, 0.0))
    voxels = rows_sum(jnp.where(row == 2, both, 0.0))
    center, recip = statistics(total, squares, voxels)
    consts[...] = jnp.zeros_like(consts)
    consts[VOXELS] = voxels
    consts[RECIP[0]] = recip
    consts[NORM_ROWS] = norm[...]
    received = received_bricks(x_near, x_far, y_near, y_far)
    for e in range(EXT - 1):
        keep = meta[COUNT] > e if e < NB else meta[VALID + e - NB] > 0
        field = z_one[e] if e < NB else received[e - NB]
        xh = (field - center) * recip
        xh_out[e] = xh
        u = norm[0:1] * xh + norm[2:3]
        ext[e] = (u * sigmoid(u) * keep.astype(F32)).astype(BF16)
    ext[EXT - 1] = jnp.zeros((64, C), BF16)
    shifted_planes(meta, ext, gathered, planes)
    z = convolve(planes, weight)
    z_out[...] = z
    masked = z * occupied_rows(meta)
    write_sums(sums, rows_sum(masked), rows_sum(z * masked))


def third_kernel(
    meta, got, constants, z_two, voxel_feats, grad_out, out_feats, dv_out, xh_out, consts, sums
):
    total, squares = read_sums(got)
    center, recip = statistics(total, squares, constants[VOXELS])
    consts[...] = constants[...]
    consts[RECIP[1]] = recip
    occupied = occupied_rows(meta)
    xh = (z_two[...] - center) * recip
    xh_out[...] = xh
    feats = voxel_feats[...].astype(F32) * occupied
    pre = constants[GAIN[1]] * xh + constants[SHIFT[1]] + feats
    s = sigmoid(pre)
    out_feats[...] = (pre * s * occupied).astype(BF16)
    dv = grad_out[...].astype(F32) * occupied * (s * (1.0 + pre * (1.0 - s)))
    dv_out[...] = dv
    write_sums(sums, rows_sum(dv), rows_sum(dv * xh))


def norm_back(dv, xh, consts, number, total, cross, occupied):
    voxels = consts[VOXELS]
    scale = occupied * consts[GAIN[number]] * consts[RECIP[number]]
    return (scale * (dv - total / voxels - xh * cross / voxels)).astype(BF16)


def send_gradients(acc, own, y_near, y_far, x_faces):
    even = parity(Y_LINE)
    own[...] = acc[0:NB].reshape(ROWS, C)
    for k in range(3):
        y_near[k] = acc[NB + 2 + 2 * k + even].astype(BF16)
        y_far[k] = acc[NB + 3 + 2 * k - even].astype(BF16)
    x_faces[0] = acc[NB].astype(BF16)
    x_faces[1] = acc[NB + 1].astype(BF16)


def fourth_kernel(
    meta, got, dv, xh_two, constants, xh_one, weight,
    dz_out, own, y_near_out, y_far_out, x_faces, sums, consts, spread, moved, acc,
):
    total, cross = read_sums(got)
    consts[...] = constants[...]
    consts[CROSS[1]] = cross
    consts[TOTAL[1]] = total
    dz = norm_back(dv[...], xh_two[...], constants, 1, total, cross, occupied_rows(meta))
    dz_out[...] = dz
    convolve_back(meta, dz, weight, spread, moved, acc)
    send_gradients(acc, own, y_near_out, y_far_out, x_faces)
    first = jnp.zeros((64, C), F32)
    second = jnp.zeros((64, C), F32)
    for e in range(EXT - 1):
        keep = meta[COUNT] > e if e < NB else meta[VALID + e - NB] > 0
        xh = xh_one[e]
        du = acc[e] * slope(constants[GAIN[0]] * xh + constants[SHIFT[0]]) * keep.astype(F32)
        first += du
        second += du * xh
    write_sums(sums, rows_sum(first), rows_sum(second))


def add_returned(meta, field, x_near, x_far, y_near, y_far):
    back = received_bricks(x_near, x_far, y_near, y_far)
    for at, brick, neighbour in (
        (FACE, 1, 1), (FACE + 1, 0, 0), (FACE + 2, 3, 3), (FACE + 3, 2, 2),
        (CORNER, 6, 7), (CORNER + 1, 7, 6), (CORNER + 2, 4, 5), (CORNER + 3, 5, 4),
    ):
        field[meta[at]] += back[brick].astype(F32) * meta[VALID + neighbour].astype(F32)


def fifth_kernel(
    meta, got, own_in, x_near, x_far, y_near, y_far, xh_one, constants, weight_far,
    dz_out, own, y_near_out, y_far_out, x_faces, consts, weight, sem, field, spread, moved, acc,
):
    fetches = []
    for a in range(3):
        part = pl.ds(9 * a * C, 9 * C)
        fetches.append(pltpu.make_async_copy(weight_far.at[part], weight.at[part], sem.at[a]))
        fetches[-1].start()
    total, cross = read_sums(got)
    consts[...] = constants[...]
    consts[CROSS[0]] = cross
    consts[TOTAL[0]] = total
    field[...] = own_in[...].reshape(NB, 64, C)
    add_returned(meta, field, x_near, x_far, y_near, y_far)
    occupied = occupied_rows(meta)
    xh = xh_one[0:NB].reshape(ROWS, C)
    du = field[...].reshape(ROWS, C) * occupied * slope(
        constants[GAIN[0]] * xh + constants[SHIFT[0]]
    )
    dz = norm_back(du, xh, constants, 0, total, cross, occupied)
    dz_out[...] = dz
    convolve_back(meta, dz, weight, spread, moved, acc, fetches)
    send_gradients(acc, own, y_near_out, y_far_out, x_faces)


def taps_kernel(meta, ext, dz, mine, other, gathered, planes, taps):
    shifted_planes(meta, ext, gathered, planes)
    for k in range(TAPS):
        taps[k * C : (k + 1) * C, :] = lax.dot_general(
            patches(planes, k),
            dz[...],
            (((0,), (0,)), ((), ())),
            preferred_element_type=F32,
        )
    here = meta[CORE_AT] == 0
    mine[30:32] = jnp.zeros((2, CHUNK, C), F32)
    other[30:32] = jnp.zeros((2, CHUNK, C), BF16)
    for c in range(31):
        full = min(CHUNK, HALF - CHUNK * c)
        at = CHUNK * c
        low = taps[at : at + full, :]
        high = taps[HALF + at : HALF + at + full, :]
        mine[c, 0:full, :] = jnp.where(here, low, high)
        other[c, 0:full, :] = jnp.where(here, high, low).astype(BF16)


def second_sum_kernel(mine, received, out):
    out[...] = (mine[...] + received[...].astype(F32)).astype(BF16)


def first_sum_kernel(mine, received, second, out):
    out[0:32] = (mine[...] + received[...].astype(F32)).astype(BF16)
    out[32:64] = second[...]


def total_kernel(consts, pieces, out):
    total = jnp.sum(pieces[...].astype(F32), axis=0) / jnp.sqrt(consts[VOXELS])
    out[...] = jnp.broadcast_to(total.astype(BF16)[None], (64, CHUNK, C))


def last_kernel(
    meta, own, x_near, x_far, y_near, y_far, dv, consts, grad_in, norm_grads, field
):
    field[...] = own[...].reshape(NB, 64, C)
    add_returned(meta, field, x_near, x_far, y_near, y_far)
    total = (dv[...] + field[...].reshape(ROWS, C)) * occupied_rows(meta)
    grad_in[...] = total.astype(BF16)
    root = jnp.sqrt(consts[VOXELS])
    for row, at in enumerate((CROSS[0], TOTAL[0], CROSS[1], TOTAL[1])):
        norm_grads[row : row + 1] = consts[at] / root


def widen_kernel(core, half, *refs, partner):
    out, wide, sems = refs[-3:]
    at = 1 - core[0] if partner else core[0]
    copies = []
    for conv in range(2):
        for piece in range(4):
            for c in range(8 * piece, min(8 * piece + 8, 31)):
                full = min(CHUNK, HALF - CHUNK * c)
                wide[conv, CHUNK * c : CHUNK * c + full, :] = half[32 * conv + c].astype(F32)[
                    0:full
                ]
            first = 8 * CHUNK * piece
            rows = pl.ds(first, min(8 * CHUNK, HALF - first))
            copies.append(
                pltpu.make_async_copy(
                    wide.at[conv, rows], out.at[conv, at, rows], sems.at[4 * conv + piece]
                )
            )
            copies[-1].start()
    for copy in copies:
        copy.wait()


def local(kernel, outs, ins, scratch=(), far=()):
    vmem = pl.BlockSpec(memory_space=pltpu.VMEM)
    smem = pl.BlockSpec(memory_space=pltpu.SMEM)
    hbm = pl.BlockSpec(memory_space=pltpu.HBM)
    specs = [hbm if n in far else smem if a.ndim == 1 else vmem for n, a in enumerate(ins)]
    ins = [
        pltpu.with_memory_space_constraint(a, pltpu.HBM) if n in far else a
        for n, a in enumerate(ins)
    ]
    return pl.pallas_call(
        kernel,
        out_shape=[jax.ShapeDtypeStruct(s, d) for s, d in outs],
        in_specs=specs,
        out_specs=[vmem] * len(outs),
        scratch_shapes=[pltpu.VMEM(*s) if isinstance(s, tuple) else s for s in scratch],
        compiler_params=pltpu.CompilerParams(vmem_limit_bytes=VMEM_BYTES),
    )(*ins)


def widen(core, half, partner, before):
    held = [] if before is None else [before]
    far = pl.BlockSpec(memory_space=pltpu.HBM)
    return pl.pallas_call(
        functools.partial(widen_kernel, partner=partner),
        out_shape=jax.ShapeDtypeStruct((2, 2, HALF, C), F32),
        in_specs=[pl.BlockSpec(memory_space=pltpu.SMEM), pl.BlockSpec(memory_space=pltpu.VMEM)]
        + [far] * len(held),
        out_specs=far,
        scratch_shapes=[pltpu.VMEM((2, HALF, C), F32), pltpu.SemaphoreType.DMA((8,))],
        input_output_aliases={2: 0} if held else {},
        compiler_params=pltpu.CompilerParams(vmem_limit_bytes=VMEM_BYTES),
        name="widen_kernel",
    )(core, half, *held)


def exchange(value, axes):
    return lax.all_to_all(value, axes, 0, 0, tiled=True)


def swap(value):
    return lax.ppermute(value, CORE, [(0, 1), (1, 0)])


def swaps(near, far, axes):
    length = lax.axis_size(axes)
    odd = [(k, (k + 1) % length) for k in range(1, length, 2)]
    far = lax.ppermute(far, axes, odd + [(b, a) for a, b in odd])
    near = lax.ppermute(near, axes, [(k, k ^ 1) for k in range(length)])
    return near, far


def two_hops(y_near, y_far, x_faces, home):
    y_near, y_far = swaps(y_near, y_far, GY)
    outs = [(y_near.shape, y_near.dtype)] * 2
    x_near, x_far = local(functools.partial(join_kernel, home=home), outs, [x_faces, y_near, y_far])
    x_near, x_far = swaps(x_near, x_far, GX)
    return x_near, x_far, y_near, y_far


def program(
    voxel_feats,
    w_first,
    w_second,
    norm_gain,
    norm_shift,
    grad_out,
    brick_count,
    kernel_map,
    face_send,
    corner_send,
):
    face = face_send.reshape(4)
    corner = corner_send.reshape(4)
    i = lax.axis_index(GX)
    j = lax.axis_index(GY)
    dx = np.array([d[0] for d in NEIGHBOURS], np.int32)
    dy = np.array([d[1] for d in NEIGHBOURS], np.int32)
    inside = (i + dx >= 0) & (i + dx < 8) & (j + dy >= 0) & (j + dy < 16)
    meta = jnp.concatenate(
        [
            kernel_map.reshape(-1),
            brick_count,
            face,
            corner,
            inside.astype(jnp.int32),
            lax.axis_index(CORE).reshape(1),
        ]
    )
    norm = jnp.concatenate([norm_gain, norm_shift], axis=0)
    flat_one = w_first.reshape(TAPS * C, C)
    flat_two = w_second.reshape(TAPS * C, C)
    brick = (64, C)
    three, two = (3,) + brick, (2,) + brick
    rows = (ROWS, C)
    sums = ((2 * 128, C), F32)
    ext = ((EXT,) + brick, BF16)
    list_xh = ((EXT - 1,) + brick, F32)
    table = ((16, C), F32)
    sem = pltpu.SemaphoreType.DMA
    weight = ((TAPS * C, C), BF16)
    gathered = ((144, 6 * NB * C), BF16)
    forward = [gathered, gathered]

    *sends, kept = local(
        send_kernel,
        [(three, BF16), (three, BF16), (two, BF16), ((NB,) + brick, BF16)],
        [face, corner, voxel_feats],
        [pltpu.SMEM((4,), jnp.int32), pltpu.SMEM((4,), jnp.int32), sem((3,))],
        far=(0, 1, 2),
    )
    (near_one,) = local(fetch_one_kernel, [weight], [flat_one], [sem(())], far=(0,))
    (near_two,) = local(fetch_two_kernel, [weight], [flat_two], [sem(())], far=(0,))
    received = two_hops(*sends, False)
    z_one, ext_one, part, *sends = local(
        first_kernel,
        [((NB,) + brick, F32), ext, ((512, C), F32), (three, F32), (three, F32), (two, F32)],
        [meta, kept, *received, near_one],
        forward,
    )
    received = two_hops(*sends, False)
    part = exchange(part, GX_GY)
    z_two, ext_two, part, xh_one, consts = local(
        second_kernel,
        [(rows, F32), ext, sums, list_xh, table],
        [meta, part, z_one, *received, norm, near_two],
        forward,
    )
    part = exchange(part, GX_GY)
    out_feats, dv, xh_two, consts, part = local(
        third_kernel,
        [(rows, BF16), (rows, F32), (rows, F32), table, sums],
        [meta, part, consts, z_two, voxel_feats.reshape(rows), grad_out.reshape(rows)],
    )
    part = exchange(part, GX_GY)
    back = [((3, ROWS, 9 * C), F32), gathered, ((EXT,) + brick, F32)]
    dz_two, own, y_near, y_far, x_faces, part, consts = local(
        fourth_kernel,
        [(rows, BF16), (rows, F32), (three, BF16), (three, BF16), (two, BF16), sums, table],
        [meta, part, dv, xh_two, consts, xh_one, near_two],
        back,
    )
    returned = two_hops(y_near, y_far, x_faces, True)
    chunks = (32, CHUNK, C)
    halves = [(chunks, F32), (chunks, BF16)]
    products = [gathered, gathered, ((TAPS * C, C), F32)]
    mine, other = local(taps_kernel, halves, [meta, ext_two, dz_two], products)
    (second,) = local(second_sum_kernel, [(chunks, BF16)], [mine, swap(other)])
    part = exchange(part, GX_GY)
    dz_one, own, y_near, y_far, x_faces, consts = local(
        fifth_kernel,
        [(rows, BF16), (rows, F32), (three, BF16), (three, BF16), (two, BF16), table],
        [meta, part, own, *returned, xh_one, consts, flat_one],
        [weight, sem((3,)), ((NB,) + brick, F32)] + back,
        far=(9,),
    )
    returned = two_hops(y_near, y_far, x_faces, True)
    mine, other = local(taps_kernel, halves, [meta, ext_one, dz_one], products)
    grad_in, norm_grads = local(
        last_kernel,
        [(rows, BF16), ((4, C), F32)],
        [meta, own, *returned, dv, consts],
        [((NB,) + brick, F32)],
    )
    both = ((64, CHUNK, C), BF16)
    (part,) = local(first_sum_kernel, [both], [mine, swap(other), second])
    (whole,) = local(total_kernel, [both], [consts, exchange(part, CHIPS)])
    whole = exchange(whole, CHIPS)
    partner = swap(whole)
    core = lax.axis_index(CORE).reshape(1)
    weight_grads = widen(core, whole, False, None)
    weight_grads = widen(core, partner, True, weight_grads).reshape(2, TAPS, C, C)
    return (
        out_feats.reshape(NB, 64, C),
        grad_in.reshape(NB, 64, C),
        weight_grads,
        norm_grads,
    )


def solution(mesh):
    split = Mesh(mesh.devices.reshape(2, 4, 4, 2, 2), GX_GY)
    in_specs = (
        P(GX_GY, None, None),
        P(),
        P(),
        P(),
        P(),
        P(GX_GY, None, None),
        P(GX_GY),
        P(GX_GY, None),
        P(GX_GY, None, None),
        P(GX_GY, None, None),
    )
    out_specs = (P(GX_GY, None, None), P(GX_GY, None, None), P(), P())
    return jax.shard_map(program, mesh=split, in_specs=in_specs, out_specs=out_specs, check_vma=False)
```

```python
import functools

import jax
import jax.numpy as jnp
import numpy as np
from jax import lax
from jax.experimental import pallas as pl
from jax.experimental.pallas import tpu as pltpu
from jax.sharding import Mesh
from jax.sharding import PartitionSpec as P

GX = ("gx_0", "gx_1")
GY = ("gy_0", "gy_1", "gy_2")
GX_GY = ("gx_0", "gx_1", "gy_0", "gy_1", "gy_2")
CORE = ("gy_2",)
X_LINE = "gx_1"
Y_LINE = "gy_2"
CHIPS = ("gx_0", "gx_1", "gy_0", "gy_1")
C = 128
NB = 4
ROWS = NB * 64
TAPS = 27
EXT = 13
EPSILON = 1e-05
F32 = jnp.float32
BF16 = jnp.bfloat16
COUNT, FACE, CORNER, VALID, CORE_AT = 108, 109, 113, 117, 125
NEIGHBOURS = ((-1, 0), (1, 0), (0, -1), (0, 1), (-1, -1), (-1, 1), (1, -1), (1, 1))
CHUNK = 56
HALF = TAPS * C // 2
VMEM_BYTES = 16 << 20


def row_of(k):
    return slice(k, k + 1)


VOXELS = row_of(0)
RECIP = (row_of(1), row_of(2))
NORM_ROWS = slice(4, 8)
GAIN = (row_of(4), row_of(5))
SHIFT = (row_of(6), row_of(7))
CROSS = (row_of(8), row_of(9))
TOTAL = (row_of(10), row_of(11))


def shift_matrix(flipped):
    def places(axis):
        at = lax.broadcasted_iota(jnp.int32, (144, 144), axis)
        major = (at >= 48).astype(jnp.int32) + (at >= 96).astype(jnp.int32)
        minor = (at >> 4) - 3 * major
        return major, minor, (at >> 2) & 3, at & 3

    b, c, q, r = places(1 if flipped else 0)
    ob, oc, qs, rs = places(0 if flipped else 1)
    hit = (4 * ob + qs == q + b + 3) & (4 * oc + rs == r + c + 3)
    return hit.astype(F32).astype(BF16)


def sources():
    return [(0, 0, 3), (1, 1, 0), (2, 1, 1), (3, 1, 2), (4, 1, 3), (5, 2, 0)]


def sigmoid(v):
    return 1.0 / (1.0 + jnp.exp(-v))


def slope(v):
    s = sigmoid(v)
    return s * (1.0 + v * (1.0 - s))


def occupied_rows(meta):
    brick = lax.broadcasted_iota(jnp.int32, (ROWS, C), 0) // 64
    return (brick < meta[COUNT]).astype(F32)


def shifted_planes(meta, ext, gathered, planes):
    shift = shift_matrix(False)
    for b in range(NB):
        for plane, oa, source in sources():
            for d in range(9):
                entry = meta[27 * b + 9 * oa + d]
                gathered[16 * d : 16 * d + 16, (6 * b + plane) * C : (6 * b + plane + 1) * C] = ext[
                    entry, 16 * source : 16 * source + 16, :
                ]
    for b in range(NB):
        at = slice(6 * b * C, 6 * (b + 1) * C)
        planes[:, at] = jnp.dot(shift, gathered[:, at], preferred_element_type=F32).astype(BF16)


def patches(planes, k):
    a, d = divmod(k, 9)
    tiles = [
        planes[16 * d : 16 * d + 16, (6 * b + p + a) * C : (6 * b + p + a + 1) * C]
        for b in range(NB)
        for p in range(4)
    ]
    return jnp.concatenate(tiles, axis=0)


def convolve(planes, weight):
    total = jnp.zeros((ROWS, C), F32)
    for k in range(0, TAPS, 2):
        taps = range(k, min(k + 2, TAPS))
        columns = jnp.concatenate([patches(planes, tap) for tap in taps], axis=1)
        total += jnp.dot(
            columns, weight[k * C : (k + len(taps)) * C, :], preferred_element_type=F32
        )
    return total


def convolve_back(meta, dz, weight, spread, moved, acc):
    shift_back = shift_matrix(True)
    for a in range(3):
        spread[a] = lax.dot_general(
            dz,
            weight[9 * a * C : 9 * (a + 1) * C, :],
            (((1,), (1,)), ((), ())),
            preferred_element_type=F32,
        )
    acc[...] = jnp.zeros_like(acc)
    for b in range(NB):
        for plane in range(6):
            taps = [a for a in range(3) if 0 <= plane - a < 4]
            for d in range(9):
                total = None
                for a in taps:
                    row = 64 * b + 16 * (plane - a)
                    piece = spread[a, row : row + 16, d * C : (d + 1) * C]
                    total = piece if total is None else total + piece
                moved[16 * d : 16 * d + 16, (6 * b + plane) * C : (6 * b + plane + 1) * C] = (
                    total.astype(BF16)
                )
    for b in range(NB):
        home = jnp.dot(
            shift_back, moved[:, 6 * b * C : 6 * (b + 1) * C], preferred_element_type=F32
        )
        for plane, oa, source in sources():
            for d in range(9):
                entry = meta[27 * b + 9 * oa + d]
                acc[entry, 16 * source : 16 * source + 16, :] += home[
                    16 * d : 16 * d + 16, plane * C : (plane + 1) * C
                ]


def write_sums(out, first, second):
    odd = lax.broadcasted_iota(jnp.int32, (8, C), 0) % 2
    both = jnp.where(odd == 0, jnp.broadcast_to(first, (8, C)), jnp.broadcast_to(second, (8, C)))
    out[...] = jnp.broadcast_to(both[None], (out.shape[0] // 8, 8, C)).reshape(out.shape)


def read_sums(got):
    total = jnp.sum(got[...].reshape(got.shape[0] // 8, 8, C), axis=0)
    odd = lax.broadcasted_iota(jnp.int32, (8, C), 0) % 2
    first = jnp.sum(jnp.where(odd == 0, total, 0.0), axis=0, keepdims=True)
    second = jnp.sum(jnp.where(odd == 1, total, 0.0), axis=0, keepdims=True)
    return first, second


def rows_sum(v):
    return jnp.sum(v, axis=0, keepdims=True)


def statistics(total, squares, voxels):
    center = total / voxels
    spread_sq = squares / voxels - center * center
    return center, lax.rsqrt(spread_sq + EPSILON)


def parity(axis):
    return 1 - lax.rem(lax.axis_index(axis), 2)


def from_next(near, far, even, k):
    return jnp.where(even == 1, near[k], far[k])


def from_previous(near, far, even, k):
    return jnp.where(even == 1, far[k], near[k])


def received_bricks(x_near, x_far, y_near, y_far):
    ex, ey = parity(X_LINE), parity(Y_LINE)
    return (
        from_previous(x_near, x_far, ex, 0), from_next(x_near, x_far, ex, 0),
        from_previous(y_near, y_far, ey, 0), from_next(y_near, y_far, ey, 0),
        from_previous(x_near, x_far, ex, 1), from_previous(x_near, x_far, ex, 2),
        from_next(x_near, x_far, ex, 1), from_next(x_near, x_far, ex, 2),
    )


def sends_of(face, corner, y_near, y_far, x_faces):
    even = parity(Y_LINE)

    def either(number, up, low):
        return jnp.where(even == number, up, low)

    up = (face(2), corner(0), corner(2))
    low = (face(3), corner(1), corner(3))
    pairs = [(face(0), x_faces.at[0]), (face(1), x_faces.at[1])]
    for k in range(3):
        pairs.append((either(1, up[k], low[k]), y_near.at[k]))
        pairs.append((either(0, up[k], low[k]), y_far.at[k]))
    return pairs


def select_sends(meta, field, y_near, y_far, x_faces):
    for entry, out in sends_of(
        lambda k: meta[FACE + k], lambda k: meta[CORNER + k], y_near, y_far, x_faces
    ):
        out[...] = field[entry]


def send_kernel(face_far, corner_far, field, y_near, y_far, x_faces, kept, face, corner, sems):
    copies = [
        pltpu.make_async_copy(field, kept, sems.at[0]),
        pltpu.make_async_copy(face_far, face, sems.at[1]),
        pltpu.make_async_copy(corner_far, corner, sems.at[2]),
    ]
    for copy in copies:
        copy.start()
    for copy in copies:
        copy.wait()
    for entry, out in sends_of(lambda k: face[k], lambda k: corner[k], y_near, y_far, x_faces):
        out[...] = kept[entry]


def fetch_one_kernel(far, out, sem):
    copy = pltpu.make_async_copy(far, out, sem)
    copy.start()
    copy.wait()


def fetch_two_kernel(far, out, sem):
    copy = pltpu.make_async_copy(far, out, sem)
    copy.start()
    copy.wait()


def join_kernel(faces, y_near, y_far, x_near, x_far, *, home):
    ex, ey = parity(X_LINE), parity(Y_LINE)
    before = [from_previous(y_near, y_far, ey, k) for k in (1, 2)]
    after = [from_next(y_near, y_far, ey, k) for k in (1, 2)]
    if home:
        low, up = ((faces[k], after[k], before[k]) for k in range(2))
    else:
        up, low = ((faces[k], before[k], after[k]) for k in range(2))
    for k in range(3):
        x_near[k] = jnp.where(ex == 1, up[k], low[k])
        x_far[k] = jnp.where(ex == 1, low[k], up[k])


def first_kernel(
    meta, voxel_feats, x_near, x_far, y_near, y_far, weight,
    z_out, ext, sums, y_near_out, y_far_out, x_faces, gathered, planes,
):
    ext[NB + 8] = jnp.zeros((64, C), BF16)
    for b in range(NB):
        keep = (meta[COUNT] > b).astype(F32)
        ext[b] = (voxel_feats[b].astype(F32) * keep).astype(BF16)
    for e, brick in enumerate(received_bricks(x_near, x_far, y_near, y_far)):
        keep = meta[VALID + e].astype(F32)
        ext[NB + e] = (brick.astype(F32) * keep).astype(BF16)
    shifted_planes(meta, ext, gathered, planes)
    z = convolve(planes, weight)
    z_out[...] = z.reshape(NB, 64, C)
    select_sends(meta, z_out, y_near_out, y_far_out, x_faces)
    masked = z * occupied_rows(meta)
    row = lax.broadcasted_iota(jnp.int32, (8, C), 0) % 4
    count = (64 * meta[COUNT]).astype(F32)
    part = jnp.where(
        row == 0, rows_sum(masked), jnp.where(row == 1, rows_sum(z * masked), count)
    )
    sums[...] = jnp.broadcast_to(part[None], (64, 8, C)).reshape(512, C)


def second_kernel(
    meta, got, z_one, x_near, x_far, y_near, y_far, norm, weight,
    z_out, ext, sums, xh_out, consts, gathered, planes,
):
    row = lax.broadcasted_iota(jnp.int32, (8, C), 0) % 4
    both = jnp.sum(got[...].reshape(64, 8, C), axis=0)
    total = rows_sum(jnp.where(row == 0, both, 0.0))
    squares = rows_sum(jnp.where(row == 1, both, 0.0))
    voxels = rows_sum(jnp.where(row == 2, both, 0.0))
    center, recip = statistics(total, squares, voxels)
    consts[...] = jnp.zeros_like(consts)
    consts[VOXELS] = voxels
    consts[RECIP[0]] = recip
    consts[NORM_ROWS] = norm[...]
    received = received_bricks(x_near, x_far, y_near, y_far)
    for e in range(EXT - 1):
        keep = meta[COUNT] > e if e < NB else meta[VALID + e - NB] > 0
        field = z_one[e] if e < NB else received[e - NB]
        xh = (field - center) * recip
        xh_out[e] = xh
        u = norm[0:1] * xh + norm[2:3]
        ext[e] = (u * sigmoid(u) * keep.astype(F32)).astype(BF16)
    ext[EXT - 1] = jnp.zeros((64, C), BF16)
    shifted_planes(meta, ext, gathered, planes)
    z = convolve(planes, weight)
    z_out[...] = z
    masked = z * occupied_rows(meta)
    write_sums(sums, rows_sum(masked), rows_sum(z * masked))


def third_kernel(
    meta, got, constants, z_two, voxel_feats, grad_out, out_feats, dv_out, xh_out, consts, sums
):
    total, squares = read_sums(got)
    center, recip = statistics(total, squares, constants[VOXELS])
    consts[...] = constants[...]
    consts[RECIP[1]] = recip
    occupied = occupied_rows(meta)
    xh = (z_two[...] - center) * recip
    xh_out[...] = xh
    feats = voxel_feats[...].astype(F32) * occupied
    pre = constants[GAIN[1]] * xh + constants[SHIFT[1]] + feats
    s = sigmoid(pre)
    out_feats[...] = (pre * s * occupied).astype(BF16)
    dv = grad_out[...].astype(F32) * occupied * (s * (1.0 + pre * (1.0 - s)))
    dv_out[...] = dv
    write_sums(sums, rows_sum(dv), rows_sum(dv * xh))


def norm_back(dv, xh, consts, number, total, cross, occupied):
    voxels = consts[VOXELS]
    scale = occupied * consts[GAIN[number]] * consts[RECIP[number]]
    return (scale * (dv - total / voxels - xh * cross / voxels)).astype(BF16)


def send_gradients(acc, own, y_near, y_far, x_faces):
    even = parity(Y_LINE)
    own[...] = acc[0:NB].reshape(ROWS, C)
    for k in range(3):
        y_near[k] = acc[NB + 2 + 2 * k + even].astype(BF16)
        y_far[k] = acc[NB + 3 + 2 * k - even].astype(BF16)
    x_faces[0] = acc[NB].astype(BF16)
    x_faces[1] = acc[NB + 1].astype(BF16)


def fourth_kernel(
    meta, got, dv, xh_two, constants, xh_one, weight,
    dz_out, own, y_near_out, y_far_out, x_faces, sums, consts, spread, moved, acc,
):
    total, cross = read_sums(got)
    consts[...] = constants[...]
    consts[CROSS[1]] = cross
    consts[TOTAL[1]] = total
    dz = norm_back(dv[...], xh_two[...], constants, 1, total, cross, occupied_rows(meta))
    dz_out[...] = dz
    convolve_back(meta, dz, weight, spread, moved, acc)
    send_gradients(acc, own, y_near_out, y_far_out, x_faces)
    first = jnp.zeros((64, C), F32)
    second = jnp.zeros((64, C), F32)
    for e in range(EXT - 1):
        keep = meta[COUNT] > e if e < NB else meta[VALID + e - NB] > 0
        xh = xh_one[e]
        du = acc[e] * slope(constants[GAIN[0]] * xh + constants[SHIFT[0]]) * keep.astype(F32)
        first += du
        second += du * xh
    write_sums(sums, rows_sum(first), rows_sum(second))


def add_returned(meta, field, x_near, x_far, y_near, y_far):
    back = received_bricks(x_near, x_far, y_near, y_far)
    for at, brick, neighbour in (
        (FACE, 1, 1), (FACE + 1, 0, 0), (FACE + 2, 3, 3), (FACE + 3, 2, 2),
        (CORNER, 6, 7), (CORNER + 1, 7, 6), (CORNER + 2, 4, 5), (CORNER + 3, 5, 4),
    ):
        field[meta[at]] += back[brick].astype(F32) * meta[VALID + neighbour].astype(F32)


def fifth_kernel(
    meta, got, own_in, x_near, x_far, y_near, y_far, xh_one, constants, dz_out, consts, field
):
    total, cross = read_sums(got)
    consts[...] = constants[...]
    consts[CROSS[0]] = cross
    consts[TOTAL[0]] = total
    field[...] = own_in[...].reshape(NB, 64, C)
    add_returned(meta, field, x_near, x_far, y_near, y_far)
    occupied = occupied_rows(meta)
    xh = xh_one[0:NB].reshape(ROWS, C)
    du = field[...].reshape(ROWS, C) * occupied * slope(
        constants[GAIN[0]] * xh + constants[SHIFT[0]]
    )
    dz_out[...] = norm_back(du, xh, constants, 0, total, cross, occupied)


def back_kernel(
    meta, dz, weight_far, own, y_near_out, y_far_out, x_faces, weight, sem, spread, moved, acc
):
    fetch = pltpu.make_async_copy(weight_far, weight, sem)
    fetch.start()
    fetch.wait()
    convolve_back(meta, dz[...], weight, spread, moved, acc)
    send_gradients(acc, own, y_near_out, y_far_out, x_faces)


def taps_kernel(meta, ext, dz, mine, other, gathered, planes, taps):
    shifted_planes(meta, ext, gathered, planes)
    for k in range(TAPS):
        taps[k * C : (k + 1) * C, :] = lax.dot_general(
            patches(planes, k),
            dz[...],
            (((0,), (0,)), ((), ())),
            preferred_element_type=F32,
        )
    here = meta[CORE_AT] == 0
    mine[30:32] = jnp.zeros((2, CHUNK, C), F32)
    other[30:32] = jnp.zeros((2, CHUNK, C), BF16)
    for c in range(31):
        full = min(CHUNK, HALF - CHUNK * c)
        at = CHUNK * c
        low = taps[at : at + full, :]
        high = taps[HALF + at : HALF + at + full, :]
        mine[c, 0:full, :] = jnp.where(here, low, high)
        other[c, 0:full, :] = jnp.where(here, high, low).astype(BF16)


def second_sum_kernel(mine, received, out):
    out[...] = (mine[...] + received[...].astype(F32)).astype(BF16)


def first_sum_kernel(mine, received, second, out):
    out[0:32] = (mine[...] + received[...].astype(F32)).astype(BF16)
    out[32:64] = second[...]


def total_kernel(consts, pieces, out):
    total = jnp.sum(pieces[...].astype(F32), axis=0) / jnp.sqrt(consts[VOXELS])
    out[...] = jnp.broadcast_to(total.astype(BF16)[None], (64, CHUNK, C))


def last_kernel(
    meta, own, x_near, x_far, y_near, y_far, dv, consts, grad_in, norm_grads, field
):
    field[...] = own[...].reshape(NB, 64, C)
    add_returned(meta, field, x_near, x_far, y_near, y_far)
    total = (dv[...] + field[...].reshape(ROWS, C)) * occupied_rows(meta)
    grad_in[...] = total.astype(BF16)
    root = jnp.sqrt(consts[VOXELS])
    for row, at in enumerate((CROSS[0], TOTAL[0], CROSS[1], TOTAL[1])):
        norm_grads[row : row + 1] = consts[at] / root


def widen_kernel(core, half, *refs, partner):
    out, wide, sems = refs[-3:]
    at = 1 - core[0] if partner else core[0]
    copies = []
    for conv in range(2):
        for piece in range(4):
            for c in range(8 * piece, min(8 * piece + 8, 31)):
                full = min(CHUNK, HALF - CHUNK * c)
                wide[conv, CHUNK * c : CHUNK * c + full, :] = half[32 * conv + c].astype(F32)[
                    0:full
                ]
            first = 8 * CHUNK * piece
            rows = pl.ds(first, min(8 * CHUNK, HALF - first))
            copies.append(
                pltpu.make_async_copy(
                    wide.at[conv, rows], out.at[conv, at, rows], sems.at[4 * conv + piece]
                )
            )
            copies[-1].start()
    for copy in copies:
        copy.wait()


def local(kernel, outs, ins, scratch=(), far=()):
    vmem = pl.BlockSpec(memory_space=pltpu.VMEM)
    smem = pl.BlockSpec(memory_space=pltpu.SMEM)
    hbm = pl.BlockSpec(memory_space=pltpu.HBM)
    specs = [hbm if n in far else smem if a.ndim == 1 else vmem for n, a in enumerate(ins)]
    ins = [
        pltpu.with_memory_space_constraint(a, pltpu.HBM) if n in far else a
        for n, a in enumerate(ins)
    ]
    return pl.pallas_call(
        kernel,
        out_shape=[jax.ShapeDtypeStruct(s, d) for s, d in outs],
        in_specs=specs,
        out_specs=[vmem] * len(outs),
        scratch_shapes=[pltpu.VMEM(*s) if isinstance(s, tuple) else s for s in scratch],
        compiler_params=pltpu.CompilerParams(vmem_limit_bytes=VMEM_BYTES),
    )(*ins)


def widen(core, half, partner, before):
    held = [] if before is None else [before]
    far = pl.BlockSpec(memory_space=pltpu.HBM)
    return pl.pallas_call(
        functools.partial(widen_kernel, partner=partner),
        out_shape=jax.ShapeDtypeStruct((2, 2, HALF, C), F32),
        in_specs=[pl.BlockSpec(memory_space=pltpu.SMEM), pl.BlockSpec(memory_space=pltpu.VMEM)]
        + [far] * len(held),
        out_specs=far,
        scratch_shapes=[pltpu.VMEM((2, HALF, C), F32), pltpu.SemaphoreType.DMA((8,))],
        input_output_aliases={2: 0} if held else {},
        compiler_params=pltpu.CompilerParams(vmem_limit_bytes=VMEM_BYTES),
        name="widen_kernel",
    )(core, half, *held)


def exchange(value, axes):
    return lax.all_to_all(value, axes, 0, 0, tiled=True)


def swap(value):
    return lax.ppermute(value, CORE, [(0, 1), (1, 0)])


def swaps(near, far, axes):
    length = lax.axis_size(axes)
    odd = [(k, (k + 1) % length) for k in range(1, length, 2)]
    far = lax.ppermute(far, axes, odd + [(b, a) for a, b in odd])
    near = lax.ppermute(near, axes, [(k, k ^ 1) for k in range(length)])
    return near, far


def two_hops(y_near, y_far, x_faces, home):
    y_near, y_far = swaps(y_near, y_far, GY)
    outs = [(y_near.shape, y_near.dtype)] * 2
    x_near, x_far = local(functools.partial(join_kernel, home=home), outs, [x_faces, y_near, y_far])
    x_near, x_far = swaps(x_near, x_far, GX)
    return x_near, x_far, y_near, y_far


def program(
    voxel_feats,
    w_first,
    w_second,
    norm_gain,
    norm_shift,
    grad_out,
    brick_count,
    kernel_map,
    face_send,
    corner_send,
):
    face = face_send.reshape(4)
    corner = corner_send.reshape(4)
    i = lax.axis_index(GX)
    j = lax.axis_index(GY)
    dx = np.array([d[0] for d in NEIGHBOURS], np.int32)
    dy = np.array([d[1] for d in NEIGHBOURS], np.int32)
    inside = (i + dx >= 0) & (i + dx < 8) & (j + dy >= 0) & (j + dy < 16)
    meta = jnp.concatenate(
        [
            kernel_map.reshape(-1),
            brick_count,
            face,
            corner,
            inside.astype(jnp.int32),
            lax.axis_index(CORE).reshape(1),
        ]
    )
    norm = jnp.concatenate([norm_gain, norm_shift], axis=0)
    flat_one = w_first.reshape(TAPS * C, C)
    flat_two = w_second.reshape(TAPS * C, C)
    brick = (64, C)
    three, two = (3,) + brick, (2,) + brick
    rows = (ROWS, C)
    sums = ((2 * 128, C), F32)
    ext = ((EXT,) + brick, BF16)
    list_xh = ((EXT - 1,) + brick, F32)
    table = ((16, C), F32)
    sem = pltpu.SemaphoreType.DMA
    weight = ((TAPS * C, C), BF16)
    gathered = ((144, 6 * NB * C), BF16)
    forward = [gathered, gathered]

    *sends, kept = local(
        send_kernel,
        [(three, BF16), (three, BF16), (two, BF16), ((NB,) + brick, BF16)],
        [face, corner, voxel_feats],
        [pltpu.SMEM((4,), jnp.int32), pltpu.SMEM((4,), jnp.int32), sem((3,))],
        far=(0, 1, 2),
    )
    (near_one,) = local(fetch_one_kernel, [weight], [flat_one], [sem(())], far=(0,))
    (near_two,) = local(fetch_two_kernel, [weight], [flat_two], [sem(())], far=(0,))
    received = two_hops(*sends, False)
    z_one, ext_one, part, *sends = local(
        first_kernel,
        [((NB,) + brick, F32), ext, ((512, C), F32), (three, F32), (three, F32), (two, F32)],
        [meta, kept, *received, near_one],
        forward,
    )
    received = two_hops(*sends, False)
    part = exchange(part, GX_GY)
    z_two, ext_two, part, xh_one, consts = local(
        second_kernel,
        [(rows, F32), ext, sums, list_xh, table],
        [meta, part, z_one, *received, norm, near_two],
        forward,
    )
    part = exchange(part, GX_GY)
    out_feats, dv, xh_two, consts, part = local(
        third_kernel,
        [(rows, BF16), (rows, F32), (rows, F32), table, sums],
        [meta, part, consts, z_two, voxel_feats.reshape(rows), grad_out.reshape(rows)],
    )
    part = exchange(part, GX_GY)
    back = [((3, ROWS, 9 * C), F32), gathered, ((EXT,) + brick, F32)]
    dz_two, own, y_near, y_far, x_faces, part, consts = local(
        fourth_kernel,
        [(rows, BF16), (rows, F32), (three, BF16), (three, BF16), (two, BF16), sums, table],
        [meta, part, dv, xh_two, consts, xh_one, near_two],
        back,
    )
    returned = two_hops(y_near, y_far, x_faces, True)
    chunks = (32, CHUNK, C)
    halves = [(chunks, F32), (chunks, BF16)]
    products = [gathered, gathered, ((TAPS * C, C), F32)]
    mine, other = local(taps_kernel, halves, [meta, ext_two, dz_two], products)
    (second,) = local(second_sum_kernel, [(chunks, BF16)], [mine, swap(other)])
    part = exchange(part, GX_GY)
    dz_one, consts = local(
        fifth_kernel,
        [(rows, BF16), table],
        [meta, part, own, *returned, xh_one, consts],
        [((NB,) + brick, F32)],
    )
    own, y_near, y_far, x_faces = local(
        back_kernel,
        [(rows, F32), (three, BF16), (three, BF16), (two, BF16)],
        [meta, dz_one, flat_one],
        [weight, sem(())] + back,
        far=(2,),
    )
    returned = two_hops(y_near, y_far, x_faces, True)
    mine, other = local(taps_kernel, halves, [meta, ext_one, dz_one], products)
    grad_in, norm_grads = local(
        last_kernel,
        [(rows, BF16), ((4, C), F32)],
        [meta, own, *returned, dv, consts],
        [((NB,) + brick, F32)],
    )
    both = ((64, CHUNK, C), BF16)
    (part,) = local(first_sum_kernel, [both], [mine, swap(other), second])
    part = exchange(part, CHIPS)
    (whole,) = local(total_kernel, [both], [consts, part])
    whole = exchange(whole, CHIPS)
    partner = swap(whole)
    core = lax.axis_index(CORE).reshape(1)
    weight_grads = widen(core, whole, False, None)
    weight_grads = widen(core, partner, True, weight_grads).reshape(2, TAPS, C, C)
    return (
        out_feats.reshape(NB, 64, C),
        grad_in.reshape(NB, 64, C),
        weight_grads,
        norm_grads,
    )


def solution(mesh):
    split = Mesh(mesh.devices.reshape(2, 4, 4, 2, 2), GX_GY)
    in_specs = (
        P(GX_GY, None, None),
        P(),
        P(),
        P(),
        P(),
        P(GX_GY, None, None),
        P(GX_GY),
        P(GX_GY, None),
        P(GX_GY, None, None),
        P(GX_GY, None, None),
    )
    out_specs = (P(GX_GY, None, None), P(GX_GY, None, None), P(), P())
    return jax.shard_map(program, mesh=split, in_specs=in_specs, out_specs=out_specs, check_vma=False)
```

```python
import functools

import jax
import jax.numpy as jnp
import numpy as np
from jax import lax
from jax.experimental import pallas as pl
from jax.experimental.pallas import tpu as pltpu
from jax.sharding import Mesh
from jax.sharding import PartitionSpec as P

GX = ("gx_0", "gx_1")
GY = ("gy_0", "gy_1", "gy_2")
GX_GY = ("gx_0", "gx_1", "gy_0", "gy_1", "gy_2")
CORE = ("gy_2",)
X_LINE = "gx_1"
Y_LINE = "gy_2"
CHIPS = ("gx_0", "gx_1", "gy_0", "gy_1")
C = 128
NB = 4
ROWS = NB * 64
TAPS = 27
EXT = 13
EPSILON = 1e-05
F32 = jnp.float32
BF16 = jnp.bfloat16
COUNT, FACE, CORNER, VALID, CORE_AT = 108, 109, 113, 117, 125
NEIGHBOURS = ((-1, 0), (1, 0), (0, -1), (0, 1), (-1, -1), (-1, 1), (1, -1), (1, 1))
CHUNK = 56
HALF = TAPS * C // 2
VMEM_BYTES = 16 << 20


def row_of(k):
    return slice(k, k + 1)


VOXELS = row_of(0)
RECIP = (row_of(1), row_of(2))
NORM_ROWS = slice(4, 8)
GAIN = (row_of(4), row_of(5))
SHIFT = (row_of(6), row_of(7))
CROSS = (row_of(8), row_of(9))
TOTAL = (row_of(10), row_of(11))


def shift_matrix(flipped):
    def places(axis):
        at = lax.broadcasted_iota(jnp.int32, (144, 144), axis)
        major = (at >= 48).astype(jnp.int32) + (at >= 96).astype(jnp.int32)
        minor = (at >> 4) - 3 * major
        return major, minor, (at >> 2) & 3, at & 3

    b, c, q, r = places(1 if flipped else 0)
    ob, oc, qs, rs = places(0 if flipped else 1)
    hit = (4 * ob + qs == q + b + 3) & (4 * oc + rs == r + c + 3)
    return hit.astype(F32).astype(BF16)


def sources():
    return [(0, 0, 3), (1, 1, 0), (2, 1, 1), (3, 1, 2), (4, 1, 3), (5, 2, 0)]


def sigmoid(v):
    return 1.0 / (1.0 + jnp.exp(-v))


def slope(v):
    s = sigmoid(v)
    return s * (1.0 + v * (1.0 - s))


def occupied_rows(meta):
    brick = lax.broadcasted_iota(jnp.int32, (ROWS, C), 0) // 64
    return (brick < meta[COUNT]).astype(F32)


def shifted_planes(meta, ext, gathered, planes):
    shift = shift_matrix(False)
    for b in range(NB):
        for plane, oa, source in sources():
            for d in range(9):
                entry = meta[27 * b + 9 * oa + d]
                gathered[16 * d : 16 * d + 16, (6 * b + plane) * C : (6 * b + plane + 1) * C] = ext[
                    entry, 16 * source : 16 * source + 16, :
                ]
    for b in range(NB):
        at = slice(6 * b * C, 6 * (b + 1) * C)
        planes[:, at] = jnp.dot(shift, gathered[:, at], preferred_element_type=F32).astype(BF16)


def patches(planes, k):
    a, d = divmod(k, 9)
    tiles = [
        planes[16 * d : 16 * d + 16, (6 * b + p + a) * C : (6 * b + p + a + 1) * C]
        for b in range(NB)
        for p in range(4)
    ]
    return jnp.concatenate(tiles, axis=0)


def convolve(planes, weight):
    total = jnp.zeros((ROWS, C), F32)
    for k in range(0, TAPS, 2):
        taps = range(k, min(k + 2, TAPS))
        columns = jnp.concatenate([patches(planes, tap) for tap in taps], axis=1)
        total += jnp.dot(
            columns, weight[k * C : (k + len(taps)) * C, :], preferred_element_type=F32
        )
    return total


def convolve_back(meta, dz, weight, spread, moved, acc):
    shift_back = shift_matrix(True)
    for a in range(3):
        spread[a] = lax.dot_general(
            dz,
            weight[9 * a * C : 9 * (a + 1) * C, :],
            (((1,), (1,)), ((), ())),
            preferred_element_type=F32,
        )
    acc[...] = jnp.zeros_like(acc)
    for b in range(NB):
        for plane in range(6):
            taps = [a for a in range(3) if 0 <= plane - a < 4]
            for d in range(9):
                total = None
                for a in taps:
                    row = 64 * b + 16 * (plane - a)
                    piece = spread[a, row : row + 16, d * C : (d + 1) * C]
                    total = piece if total is None else total + piece
                moved[16 * d : 16 * d + 16, (6 * b + plane) * C : (6 * b + plane + 1) * C] = (
                    total.astype(BF16)
                )
    for b in range(NB):
        home = jnp.dot(
            shift_back, moved[:, 6 * b * C : 6 * (b + 1) * C], preferred_element_type=F32
        )
        for plane, oa, source in sources():
            for d in range(9):
                entry = meta[27 * b + 9 * oa + d]
                acc[entry, 16 * source : 16 * source + 16, :] += home[
                    16 * d : 16 * d + 16, plane * C : (plane + 1) * C
                ]


def write_sums(out, first, second):
    odd = lax.broadcasted_iota(jnp.int32, (8, C), 0) % 2
    both = jnp.where(odd == 0, jnp.broadcast_to(first, (8, C)), jnp.broadcast_to(second, (8, C)))
    out[...] = jnp.broadcast_to(both[None], (out.shape[0] // 8, 8, C)).reshape(out.shape)


def read_sums(got):
    total = jnp.sum(got[...].reshape(got.shape[0] // 8, 8, C), axis=0)
    odd = lax.broadcasted_iota(jnp.int32, (8, C), 0) % 2
    first = jnp.sum(jnp.where(odd == 0, total, 0.0), axis=0, keepdims=True)
    second = jnp.sum(jnp.where(odd == 1, total, 0.0), axis=0, keepdims=True)
    return first, second


def rows_sum(v):
    return jnp.sum(v, axis=0, keepdims=True)


def statistics(total, squares, voxels):
    center = total / voxels
    spread_sq = squares / voxels - center * center
    return center, lax.rsqrt(spread_sq + EPSILON)


def parity(axis):
    return 1 - lax.rem(lax.axis_index(axis), 2)


def from_next(near, far, even, k):
    return jnp.where(even == 1, near[k], far[k])


def from_previous(near, far, even, k):
    return jnp.where(even == 1, far[k], near[k])


def received_bricks(x_near, x_far, y_near, y_far):
    ex, ey = parity(X_LINE), parity(Y_LINE)
    return (
        from_previous(x_near, x_far, ex, 0), from_next(x_near, x_far, ex, 0),
        from_previous(y_near, y_far, ey, 0), from_next(y_near, y_far, ey, 0),
        from_previous(x_near, x_far, ex, 1), from_previous(x_near, x_far, ex, 2),
        from_next(x_near, x_far, ex, 1), from_next(x_near, x_far, ex, 2),
    )


def sends_of(face, corner, y_near, y_far, x_faces):
    even = parity(Y_LINE)

    def either(number, up, low):
        return jnp.where(even == number, up, low)

    up = (face(2), corner(0), corner(2))
    low = (face(3), corner(1), corner(3))
    pairs = [(face(0), x_faces.at[0]), (face(1), x_faces.at[1])]
    for k in range(3):
        pairs.append((either(1, up[k], low[k]), y_near.at[k]))
        pairs.append((either(0, up[k], low[k]), y_far.at[k]))
    return pairs


def select_sends(meta, field, y_near, y_far, x_faces):
    for entry, out in sends_of(
        lambda k: meta[FACE + k], lambda k: meta[CORNER + k], y_near, y_far, x_faces
    ):
        out[...] = field[entry]


def send_kernel(face_far, corner_far, field, y_near, y_far, x_faces, kept, face, corner, sems):
    copies = [
        pltpu.make_async_copy(field, kept, sems.at[0]),
        pltpu.make_async_copy(face_far, face, sems.at[1]),
        pltpu.make_async_copy(corner_far, corner, sems.at[2]),
    ]
    for copy in copies:
        copy.start()
    for copy in copies:
        copy.wait()
    for entry, out in sends_of(lambda k: face[k], lambda k: corner[k], y_near, y_far, x_faces):
        out[...] = kept[entry]


def fetch_one_kernel(far, out, sem):
    copy = pltpu.make_async_copy(far, out, sem)
    copy.start()
    copy.wait()


def fetch_two_kernel(far, out, sem):
    copy = pltpu.make_async_copy(far, out, sem)
    copy.start()
    copy.wait()


def join_kernel(faces, y_near, y_far, x_near, x_far, *, home):
    ex, ey = parity(X_LINE), parity(Y_LINE)
    before = [from_previous(y_near, y_far, ey, k) for k in (1, 2)]
    after = [from_next(y_near, y_far, ey, k) for k in (1, 2)]
    if home:
        low, up = ((faces[k], after[k], before[k]) for k in range(2))
    else:
        up, low = ((faces[k], before[k], after[k]) for k in range(2))
    for k in range(3):
        x_near[k] = jnp.where(ex == 1, up[k], low[k])
        x_far[k] = jnp.where(ex == 1, low[k], up[k])


def first_kernel(
    meta, voxel_feats, x_near, x_far, y_near, y_far, weight,
    z_out, ext, sums, y_near_out, y_far_out, x_faces, gathered, planes,
):
    ext[NB + 8] = jnp.zeros((64, C), BF16)
    for b in range(NB):
        keep = (meta[COUNT] > b).astype(F32)
        ext[b] = (voxel_feats[b].astype(F32) * keep).astype(BF16)
    for e, brick in enumerate(received_bricks(x_near, x_far, y_near, y_far)):
        keep = meta[VALID + e].astype(F32)
        ext[NB + e] = (brick.astype(F32) * keep).astype(BF16)
    shifted_planes(meta, ext, gathered, planes)
    z = convolve(planes, weight)
    z_out[...] = z.reshape(NB, 64, C)
    select_sends(meta, z_out, y_near_out, y_far_out, x_faces)
    masked = z * occupied_rows(meta)
    row = lax.broadcasted_iota(jnp.int32, (8, C), 0) % 4
    count = (64 * meta[COUNT]).astype(F32)
    part = jnp.where(
        row == 0, rows_sum(masked), jnp.where(row == 1, rows_sum(z * masked), count)
    )
    sums[...] = jnp.broadcast_to(part[None], (64, 8, C)).reshape(512, C)


def second_kernel(
    meta, got, z_one, x_near, x_far, y_near, y_far, norm, weight,
    z_out, ext, sums, xh_out, consts, gathered, planes,
):
    row = lax.broadcasted_iota(jnp.int32, (8, C), 0) % 4
    both = jnp.sum(got[...].reshape(64, 8, C), axis=0)
    total = rows_sum(jnp.where(row == 0, both, 0.0))
    squares = rows_sum(jnp.where(row == 1, both, 0.0))
    voxels = rows_sum(jnp.where(row == 2, both, 0.0))
    center, recip = statistics(total, squares, voxels)
    consts[...] = jnp.zeros_like(consts)
    consts[VOXELS] = voxels
    consts[RECIP[0]] = recip
    consts[NORM_ROWS] = norm[...]
    received = received_bricks(x_near, x_far, y_near, y_far)
    for e in range(EXT - 1):
        keep = meta[COUNT] > e if e < NB else meta[VALID + e - NB] > 0
        field = z_one[e] if e < NB else received[e - NB]
        xh = (field - center) * recip
        xh_out[e] = xh
        u = norm[0:1] * xh + norm[2:3]
        ext[e] = (u * sigmoid(u) * keep.astype(F32)).astype(BF16)
    ext[EXT - 1] = jnp.zeros((64, C), BF16)
    shifted_planes(meta, ext, gathered, planes)
    z = convolve(planes, weight)
    z_out[...] = z
    masked = z * occupied_rows(meta)
    write_sums(sums, rows_sum(masked), rows_sum(z * masked))


def third_kernel(
    meta, got, constants, z_two, voxel_feats, grad_out, out_feats, dv_out, xh_out, consts, sums
):
    total, squares = read_sums(got)
    center, recip = statistics(total, squares, constants[VOXELS])
    consts[...] = constants[...]
    consts[RECIP[1]] = recip
    occupied = occupied_rows(meta)
    xh = (z_two[...] - center) * recip
    xh_out[...] = xh
    feats = voxel_feats[...].astype(F32) * occupied
    pre = constants[GAIN[1]] * xh + constants[SHIFT[1]] + feats
    s = sigmoid(pre)
    out_feats[...] = (pre * s * occupied).astype(BF16)
    dv = grad_out[...].astype(F32) * occupied * (s * (1.0 + pre * (1.0 - s)))
    dv_out[...] = dv
    write_sums(sums, rows_sum(dv), rows_sum(dv * xh))


def norm_back(dv, xh, consts, number, total, cross, occupied):
    voxels = consts[VOXELS]
    scale = occupied * consts[GAIN[number]] * consts[RECIP[number]]
    return (scale * (dv - total / voxels - xh * cross / voxels)).astype(BF16)


def send_gradients(acc, own, y_near, y_far, x_faces):
    even = parity(Y_LINE)
    own[...] = acc[0:NB].reshape(ROWS, C)
    for k in range(3):
        y_near[k] = acc[NB + 2 + 2 * k + even].astype(BF16)
        y_far[k] = acc[NB + 3 + 2 * k - even].astype(BF16)
    x_faces[0] = acc[NB].astype(BF16)
    x_faces[1] = acc[NB + 1].astype(BF16)


def fourth_kernel(
    meta, got, dv, xh_two, constants, xh_one, weight,
    dz_out, own, y_near_out, y_far_out, x_faces, sums, consts, spread, moved, acc,
):
    total, cross = read_sums(got)
    consts[...] = constants[...]
    consts[CROSS[1]] = cross
    consts[TOTAL[1]] = total
    dz = norm_back(dv[...], xh_two[...], constants, 1, total, cross, occupied_rows(meta))
    dz_out[...] = dz
    convolve_back(meta, dz, weight, spread, moved, acc)
    send_gradients(acc, own, y_near_out, y_far_out, x_faces)
    first = jnp.zeros((64, C), F32)
    second = jnp.zeros((64, C), F32)
    for e in range(EXT - 1):
        keep = meta[COUNT] > e if e < NB else meta[VALID + e - NB] > 0
        xh = xh_one[e]
        du = acc[e] * slope(constants[GAIN[0]] * xh + constants[SHIFT[0]]) * keep.astype(F32)
        first += du
        second += du * xh
    write_sums(sums, rows_sum(first), rows_sum(second))


def add_returned(meta, field, x_near, x_far, y_near, y_far):
    back = received_bricks(x_near, x_far, y_near, y_far)
    for at, brick, neighbour in (
        (FACE, 1, 1), (FACE + 1, 0, 0), (FACE + 2, 3, 3), (FACE + 3, 2, 2),
        (CORNER, 6, 7), (CORNER + 1, 7, 6), (CORNER + 2, 4, 5), (CORNER + 3, 5, 4),
    ):
        field[meta[at]] += back[brick].astype(F32) * meta[VALID + neighbour].astype(F32)


def fifth_kernel(
    meta, got, own_in, x_near, x_far, y_near, y_far, xh_one, constants, dz_out, consts, field
):
    total, cross = read_sums(got)
    consts[...] = constants[...]
    consts[CROSS[0]] = cross
    consts[TOTAL[0]] = total
    field[...] = own_in[...].reshape(NB, 64, C)
    add_returned(meta, field, x_near, x_far, y_near, y_far)
    occupied = occupied_rows(meta)
    xh = xh_one[0:NB].reshape(ROWS, C)
    du = field[...].reshape(ROWS, C) * occupied * slope(
        constants[GAIN[0]] * xh + constants[SHIFT[0]]
    )
    dz_out[...] = norm_back(du, xh, constants, 0, total, cross, occupied)


def back_kernel(
    meta, dz, weight_far, own, y_near_out, y_far_out, x_faces, weight, sem, spread, moved, acc
):
    fetch = pltpu.make_async_copy(weight_far, weight, sem)
    fetch.start()
    fetch.wait()
    convolve_back(meta, dz[...], weight, spread, moved, acc)
    send_gradients(acc, own, y_near_out, y_far_out, x_faces)


def planes_kernel(meta, ext, planes, gathered):
    shifted_planes(meta, ext, gathered, planes)


def taps_kernel(meta, ext, dz, mine, other, gathered, planes, taps):
    shifted_planes(meta, ext, gathered, planes)
    tap_halves(meta, planes, dz, mine, other, taps)


def planes_taps_kernel(meta, planes, dz, mine, other, taps):
    tap_halves(meta, planes, dz, mine, other, taps)


def tap_halves(meta, planes, dz, mine, other, taps):
    for k in range(TAPS):
        taps[k * C : (k + 1) * C, :] = lax.dot_general(
            patches(planes, k),
            dz[...],
            (((0,), (0,)), ((), ())),
            preferred_element_type=F32,
        )
    here = meta[CORE_AT] == 0
    mine[30:32] = jnp.zeros((2, CHUNK, C), F32)
    other[30:32] = jnp.zeros((2, CHUNK, C), BF16)
    for c in range(31):
        full = min(CHUNK, HALF - CHUNK * c)
        at = CHUNK * c
        low = taps[at : at + full, :]
        high = taps[HALF + at : HALF + at + full, :]
        mine[c, 0:full, :] = jnp.where(here, low, high)
        other[c, 0:full, :] = jnp.where(here, high, low).astype(BF16)


def second_sum_kernel(mine, received, out):
    out[...] = (mine[...] + received[...].astype(F32)).astype(BF16)


def first_sum_kernel(mine, received, second, out):
    out[0:32] = (mine[...] + received[...].astype(F32)).astype(BF16)
    out[32:64] = second[...]


def total_kernel(consts, pieces, out):
    total = jnp.sum(pieces[...].astype(F32), axis=0) / jnp.sqrt(consts[VOXELS])
    out[...] = jnp.broadcast_to(total.astype(BF16)[None], (64, CHUNK, C))


def last_kernel(
    meta, own, x_near, x_far, y_near, y_far, dv, consts, grad_in, norm_grads, field
):
    field[...] = own[...].reshape(NB, 64, C)
    add_returned(meta, field, x_near, x_far, y_near, y_far)
    total = (dv[...] + field[...].reshape(ROWS, C)) * occupied_rows(meta)
    grad_in[...] = total.astype(BF16)
    root = jnp.sqrt(consts[VOXELS])
    for row, at in enumerate((CROSS[0], TOTAL[0], CROSS[1], TOTAL[1])):
        norm_grads[row : row + 1] = consts[at] / root


def widen_kernel(core, half, *refs, partner):
    out, wide, sems = refs[-3:]
    at = 1 - core[0] if partner else core[0]
    copies = []
    for conv in range(2):
        for piece in range(4):
            for c in range(8 * piece, min(8 * piece + 8, 31)):
                full = min(CHUNK, HALF - CHUNK * c)
                wide[conv, CHUNK * c : CHUNK * c + full, :] = half[32 * conv + c].astype(F32)[
                    0:full
                ]
            first = 8 * CHUNK * piece
            rows = pl.ds(first, min(8 * CHUNK, HALF - first))
            copies.append(
                pltpu.make_async_copy(
                    wide.at[conv, rows], out.at[conv, at, rows], sems.at[4 * conv + piece]
                )
            )
            copies[-1].start()
    for copy in copies:
        copy.wait()


def local(kernel, outs, ins, scratch=(), far=()):
    vmem = pl.BlockSpec(memory_space=pltpu.VMEM)
    smem = pl.BlockSpec(memory_space=pltpu.SMEM)
    hbm = pl.BlockSpec(memory_space=pltpu.HBM)
    specs = [hbm if n in far else smem if a.ndim == 1 else vmem for n, a in enumerate(ins)]
    ins = [
        pltpu.with_memory_space_constraint(a, pltpu.HBM) if n in far else a
        for n, a in enumerate(ins)
    ]
    return pl.pallas_call(
        kernel,
        out_shape=[jax.ShapeDtypeStruct(s, d) for s, d in outs],
        in_specs=specs,
        out_specs=[vmem] * len(outs),
        scratch_shapes=[pltpu.VMEM(*s) if isinstance(s, tuple) else s for s in scratch],
        compiler_params=pltpu.CompilerParams(vmem_limit_bytes=VMEM_BYTES),
    )(*ins)


def widen(core, half, partner, before):
    held = [] if before is None else [before]
    far = pl.BlockSpec(memory_space=pltpu.HBM)
    return pl.pallas_call(
        functools.partial(widen_kernel, partner=partner),
        out_shape=jax.ShapeDtypeStruct((2, 2, HALF, C), F32),
        in_specs=[pl.BlockSpec(memory_space=pltpu.SMEM), pl.BlockSpec(memory_space=pltpu.VMEM)]
        + [far] * len(held),
        out_specs=far,
        scratch_shapes=[pltpu.VMEM((2, HALF, C), F32), pltpu.SemaphoreType.DMA((8,))],
        input_output_aliases={2: 0} if held else {},
        compiler_params=pltpu.CompilerParams(vmem_limit_bytes=VMEM_BYTES),
        name="widen_kernel",
    )(core, half, *held)


def exchange(value, axes):
    return lax.all_to_all(value, axes, 0, 0, tiled=True)


def swap(value):
    return lax.ppermute(value, CORE, [(0, 1), (1, 0)])


def swaps(near, far, axes):
    length = lax.axis_size(axes)
    odd = [(k, (k + 1) % length) for k in range(1, length, 2)]
    far = lax.ppermute(far, axes, odd + [(b, a) for a, b in odd])
    near = lax.ppermute(near, axes, [(k, k ^ 1) for k in range(length)])
    return near, far


def two_hops(y_near, y_far, x_faces, home):
    y_near, y_far = swaps(y_near, y_far, GY)
    outs = [(y_near.shape, y_near.dtype)] * 2
    x_near, x_far = local(functools.partial(join_kernel, home=home), outs, [x_faces, y_near, y_far])
    x_near, x_far = swaps(x_near, x_far, GX)
    return x_near, x_far, y_near, y_far


def program(
    voxel_feats,
    w_first,
    w_second,
    norm_gain,
    norm_shift,
    grad_out,
    brick_count,
    kernel_map,
    face_send,
    corner_send,
):
    face = face_send.reshape(4)
    corner = corner_send.reshape(4)
    i = lax.axis_index(GX)
    j = lax.axis_index(GY)
    dx = np.array([d[0] for d in NEIGHBOURS], np.int32)
    dy = np.array([d[1] for d in NEIGHBOURS], np.int32)
    inside = (i + dx >= 0) & (i + dx < 8) & (j + dy >= 0) & (j + dy < 16)
    meta = jnp.concatenate(
        [
            kernel_map.reshape(-1),
            brick_count,
            face,
            corner,
            inside.astype(jnp.int32),
            lax.axis_index(CORE).reshape(1),
        ]
    )
    norm = jnp.concatenate([norm_gain, norm_shift], axis=0)
    flat_one = w_first.reshape(TAPS * C, C)
    flat_two = w_second.reshape(TAPS * C, C)
    brick = (64, C)
    three, two = (3,) + brick, (2,) + brick
    rows = (ROWS, C)
    sums = ((2 * 128, C), F32)
    ext = ((EXT,) + brick, BF16)
    list_xh = ((EXT - 1,) + brick, F32)
    table = ((16, C), F32)
    sem = pltpu.SemaphoreType.DMA
    weight = ((TAPS * C, C), BF16)
    gathered = ((144, 6 * NB * C), BF16)
    forward = [gathered, gathered]

    *sends, kept = local(
        send_kernel,
        [(three, BF16), (three, BF16), (two, BF16), ((NB,) + brick, BF16)],
        [face, corner, voxel_feats],
        [pltpu.SMEM((4,), jnp.int32), pltpu.SMEM((4,), jnp.int32), sem((3,))],
        far=(0, 1, 2),
    )
    (near_one,) = local(fetch_one_kernel, [weight], [flat_one], [sem(())], far=(0,))
    (near_two,) = local(fetch_two_kernel, [weight], [flat_two], [sem(())], far=(0,))
    received = two_hops(*sends, False)
    z_one, ext_one, part, *sends = local(
        first_kernel,
        [((NB,) + brick, F32), ext, ((512, C), F32), (three, F32), (three, F32), (two, F32)],
        [meta, kept, *received, near_one],
        forward,
    )
    received = two_hops(*sends, False)
    part = exchange(part, GX_GY)
    z_two, ext_two, part, xh_one, consts = local(
        second_kernel,
        [(rows, F32), ext, sums, list_xh, table],
        [meta, part, z_one, *received, norm, near_two],
        forward,
    )
    part = exchange(part, GX_GY)
    out_feats, dv, xh_two, consts, part = local(
        third_kernel,
        [(rows, BF16), (rows, F32), (rows, F32), table, sums],
        [meta, part, consts, z_two, voxel_feats.reshape(rows), grad_out.reshape(rows)],
    )
    part = exchange(part, GX_GY)
    back = [((3, ROWS, 9 * C), F32), gathered, ((EXT,) + brick, F32)]
    dz_two, own, y_near, y_far, x_faces, part, consts = local(
        fourth_kernel,
        [(rows, BF16), (rows, F32), (three, BF16), (three, BF16), (two, BF16), sums, table],
        [meta, part, dv, xh_two, consts, xh_one, near_two],
        back,
    )
    returned = two_hops(y_near, y_far, x_faces, True)
    chunks = (32, CHUNK, C)
    halves = [(chunks, F32), (chunks, BF16)]
    products = [gathered, gathered, ((TAPS * C, C), F32)]
    (planes_one,) = local(planes_kernel, [gathered], [meta, ext_one], [gathered])
    mine, other = local(taps_kernel, halves, [meta, ext_two, dz_two], products)
    (second,) = local(second_sum_kernel, [(chunks, BF16)], [mine, swap(other)])
    part = exchange(part, GX_GY)
    dz_one, consts = local(
        fifth_kernel,
        [(rows, BF16), table],
        [meta, part, own, *returned, xh_one, consts],
        [((NB,) + brick, F32)],
    )
    own, y_near, y_far, x_faces = local(
        back_kernel,
        [(rows, F32), (three, BF16), (three, BF16), (two, BF16)],
        [meta, dz_one, flat_one],
        [weight, sem(())] + back,
        far=(2,),
    )
    returned = two_hops(y_near, y_far, x_faces, True)
    mine, other = local(
        planes_taps_kernel, halves, [meta, planes_one, dz_one], products[2:]
    )
    grad_in, norm_grads = local(
        last_kernel,
        [(rows, BF16), ((4, C), F32)],
        [meta, own, *returned, dv, consts],
        [((NB,) + brick, F32)],
    )
    both = ((64, CHUNK, C), BF16)
    (part,) = local(first_sum_kernel, [both], [mine, swap(other), second])
    part = exchange(part, CHIPS)
    (whole,) = local(total_kernel, [both], [consts, part])
    whole = exchange(whole, CHIPS)
    partner = swap(whole)
    core = lax.axis_index(CORE).reshape(1)
    weight_grads = widen(core, whole, False, None)
    weight_grads = widen(core, partner, True, weight_grads).reshape(2, TAPS, C, C)
    return (
        out_feats.reshape(NB, 64, C),
        grad_in.reshape(NB, 64, C),
        weight_grads,
        norm_grads,
    )


def solution(mesh):
    split = Mesh(mesh.devices.reshape(2, 4, 4, 2, 2), GX_GY)
    in_specs = (
        P(GX_GY, None, None),
        P(),
        P(),
        P(),
        P(),
        P(GX_GY, None, None),
        P(GX_GY),
        P(GX_GY, None),
        P(GX_GY, None, None),
        P(GX_GY, None, None),
    )
    out_specs = (P(GX_GY, None, None), P(GX_GY, None, None), P(), P())
    return jax.shard_map(program, mesh=split, in_specs=in_specs, out_specs=out_specs, check_vma=False)
```
